512 devices in a mesh: dom: 128 (over y, z, core), rep: 4 (over x).
Axes of the slice: x: 4, y: 8, z: 8, core: 2. Of those that a mesh axis runs over, the one named last changes fastest.
Arguments:
- feats: bfloat16 [65536, 512], P('dom', 'rep'), may hold values from -6 to 6
- hist_one: bfloat16 [65536, 512], P('dom', 'rep'), may hold values from -6 to 6
- local_val: bfloat16 [65536, 128], P('dom'), may hold values from -0.375 to 0.375
- halo_val: bfloat16 [65536, 128], P('dom'), may hold values from -0.375 to 0.375
- halo_send: int32 [128, 128, 4], P('dom'), may hold values from 0 to 511
- halo_tile: int32 [128, 4], P('dom'), may hold values from 0 to 3, as said below
- tile_type: int32 [128, 4], P('dom'), may hold values from 0 to 7
- w_one: bfloat16 [512, 8, 512], P(None, None, 'rep'), may hold values from -0.25 to 0.25
- w_two: bfloat16 [512, 8, 512], P(None, None, 'rep'), may hold values from -0.25 to 0.25
- grad_out: bfloat16 [65536, 512], P('dom', 'rep'), may hold values from -6 to 6
Outputs:
- hidden_two: bfloat16 [65536, 512], P('dom', 'rep')
- history_one: bfloat16 [65536, 512], P('dom', 'rep')
- grad_w_one: float32 [512, 8, 512], P(None, None, 'rep')
- grad_w_two: float32 [512, 8, 512], P(None, None, 'rep')
The draws below stay inside these ranges and needn't reach their ends.
Inputs may be any that keep to these rules, and one draw needn't show every extreme that they name: `halo_tile`: for each partition, every one of the 4 halo blocks is read by exactly 1 of its row blocks.
All inputs are finite; a program needn't handle non-finite values.
Results may differ from the reference program's by a relative error of at most 0.013.
Values may be sent and summed in bfloat16 or wider, within the bound.
No kernel may reach another device: no remote copies, remote signals or barrier semaphores. Data moves between devices by JAX's collectives and lax.ppermute only.
A program may use at most 64 MiB of HBM per device.

```python
import math
import jax
import jax.numpy as jnp
import numpy as np
from jax import lax

D = 512
E = 8
TILE = 128
NODES_DEV = 512
NODES = 65536
CAP = 4
ROWBLK = 4
HALOBLK = 4
N_DOM = 128
N_REP = 4


def draw_halo_tile(key, part):
    keys = jax.random.split(key, N_DOM)

    def one_partition(single):
        return (jax.random.permutation(single, ROWBLK) % HALOBLK).astype(jnp.int32)
    return jax.vmap(one_partition)(keys)


def plant(values, own_key, smallest, high):
    longest = values.shape.index(max(values.shape))
    spots = []
    for shift in (0, 1):
        where = [jax.random.randint(jax.random.fold_in(own_key, axis), (), 0, length) for axis, length in enumerate(values.shape)]
        where[longest] = (where[longest] + shift) % values.shape[longest]
        spots.append(tuple(where))
    return values.at[spots[0]].set(smallest).at[spots[1]].set(high)


def levels(stream_key, shape, cuts, least, high):
    gain, own = 1.0, jax.random.fold_in(stream_key, 6)
    for dim, blocks in cuts:
        steps = jnp.exp(jax.random.uniform(jax.random.fold_in(own, dim), (blocks,), jnp.float32, least / len(cuts), high / len(cuts)))
        gain = gain * jnp.repeat(steps, shape[dim] // blocks).reshape([-1 if axis == dim else 1 for axis in range(len(shape))])
    return gain


def rank_bounds(count, lean):
    weights = [(1 << 20) // math.isqrt(rank ** lean) + 1 for rank in range(1, count + 1)]
    scale = 1 + sum(weights) // (1 << 30)
    return np.cumsum(np.array([max(1, weight // scale) for weight in weights]))


def ranked(stream_key, shape, amount, skew):
    table = rank_bounds(amount, skew)
    ticket = jax.random.randint(jax.random.fold_in(stream_key, 1), shape, 0, int(table[amount - 1]))
    rank = jnp.searchsorted(jnp.asarray(table, jnp.int32), ticket, side="right")
    return jax.random.permutation(jax.random.fold_in(stream_key, 2), amount)[rank].astype(jnp.int32)


def scatter_about(rng, extent, scale, most, shards=(), kind=jnp.bfloat16):
    drawn = scale * jax.random.normal(rng, extent, jnp.float32)
    if shards:
        drawn = drawn * levels(rng, extent, shards, -0.22, 0.18)
    return jnp.clip(drawn, -most, most).astype(kind)


def setup_inputs(seed: int = 0) -> dict:
    arg_keys = jax.random.split(jax.random.key(seed), 11)
    feats = scatter_about(arg_keys[0], (NODES, D), 1.0, 6.0, ((0, 128), (1, 4)))
    hist_one = scatter_about(arg_keys[1], (NODES, D), 1.0, 6.0, ((0, 128), (1, 4)))
    local_val = scatter_about(arg_keys[2], (NODES, TILE), (2 * TILE) ** -0.5, 0.375, ((0, 128),))
    halo_val = scatter_about(arg_keys[3], (NODES, TILE), (2 * TILE) ** -0.5, 0.375, ((0, 128),))
    halo_send = plant(jax.random.randint(arg_keys[4], (N_DOM, N_DOM, CAP), 0, NODES_DEV), jax.random.fold_in(arg_keys[4], 1), 0, NODES_DEV - 1).astype(jnp.int32)
    halo_tile = draw_halo_tile(jax.random.fold_in(arg_keys[10], 71), 0)
    tile_type = plant(ranked(arg_keys[6], (N_DOM, ROWBLK), E, 2), jax.random.fold_in(arg_keys[6], 3), 0, E - 1).astype(jnp.int32)
    w_one = scatter_about(arg_keys[7], (D, E, D), D ** -0.5, 0.25, ((2, 4),))
    w_two = scatter_about(arg_keys[8], (D, E, D), D ** -0.5, 0.25, ((2, 4),))
    grad_out = scatter_about(arg_keys[9], (NODES, D), 1.0, 6.0, ((0, 128), (1, 4)))
    return dict(feats=feats, hist_one=hist_one, local_val=local_val, halo_val=halo_val, halo_send=halo_send, halo_tile=halo_tile, tile_type=tile_type, w_one=w_one, w_two=w_two, grad_out=grad_out)


def slope_silu(value):
    sig = jax.nn.sigmoid(value)
    return sig * (1.0 + value * (1.0 - sig))


def aggregate(source, halo, local_blocks, halo_blocks, halo_pick):
    rows, tile, _ = local_blocks.shape
    width = source.shape[1]
    src = source.reshape(rows, tile, width).astype(jnp.float32)
    halo_tiles = jnp.take(halo.reshape(-1, tile, width), halo_pick, axis=0).astype(jnp.float32)
    total = jnp.einsum("jrk,jkc->jrc", local_blocks.astype(jnp.float32), src)
    total = total + jnp.einsum("jrk,jkc->jrc", halo_blocks.astype(jnp.float32), halo_tiles)
    return total.astype(jnp.bfloat16)


def reference(feats, hist_one, local_val, halo_val, halo_send, halo_tile, tile_type, w_one, w_two, grad_out):
    nodes, width = feats.shape
    tile = local_val.shape[1]
    devs = halo_send.shape[0]
    per_dev = nodes // devs
    rows = per_dev // tile
    experts = w_one.shape[1]
    cols = width // N_REP
    feats_dev = feats.reshape(devs, per_dev, width)
    grad_dev = grad_out.reshape(devs, per_dev, width)
    local_dev = local_val.reshape(devs, rows, tile, tile)
    halo_dev = halo_val.reshape(devs, rows, tile, tile)

    def one_device(carry, device):
        grad_one, grad_two = carry
        own_feats = feats_dev[device]
        local_blocks = local_dev[device]
        halo_blocks = halo_dev[device]
        halo_pick = halo_tile[device]
        types = tile_type[device]
        wanted = jnp.take(halo_send, device, axis=1)
        index = (jnp.arange(devs, dtype=jnp.int32)[:, None] * per_dev + wanted).reshape(-1).astype(jnp.int32)
        halo_first = jnp.take(feats, index, axis=0)
        halo_second = jnp.take(hist_one, index, axis=0)
        chosen_one = jnp.take(w_one, types, axis=1).astype(jnp.float32)
        chosen_two = jnp.take(w_two, types, axis=1).astype(jnp.float32)
        agg_one = aggregate(own_feats, halo_first, local_blocks, halo_blocks, halo_pick)
        z_one = jnp.einsum("jrd,djc->jrc", agg_one.astype(jnp.float32), chosen_one)
        h_one = (own_feats.reshape(rows, tile, width).astype(jnp.float32) + jax.nn.silu(z_one)).astype(jnp.bfloat16)
        agg_two = aggregate(h_one.reshape(per_dev, width), halo_second, local_blocks, halo_blocks, halo_pick)
        z_two = jnp.einsum("jrd,djc->jrc", agg_two.astype(jnp.float32), chosen_two)
        h_two = (h_one.astype(jnp.float32) + jax.nn.silu(z_two)).astype(jnp.bfloat16)
        upstream = grad_dev[device].reshape(rows, tile, width).astype(jnp.float32)
        dz_two = (upstream * slope_silu(z_two)).astype(jnp.bfloat16)
        dz_split = dz_two.astype(jnp.float32).reshape(rows, tile, N_REP, cols)
        w_split = chosen_two.reshape(width, rows, N_REP, cols)
        partial_back = jnp.einsum("jrqc,djqc->qjrd", dz_split, w_split)
        partial_back = lax.optimization_barrier(partial_back.astype(jnp.bfloat16))
        dagg_two = jnp.sum(partial_back.astype(jnp.float32), axis=0).astype(jnp.bfloat16)
        dh_one = upstream + jnp.einsum("jrk,jrc->jkc", local_blocks.astype(jnp.float32), dagg_two.astype(jnp.float32))
        dz_one = (dh_one * slope_silu(z_one)).astype(jnp.bfloat16)
        onehot = (types[:, None] == jnp.arange(experts, dtype=jnp.int32)[None, :]).astype(jnp.float32)
        tile_one = jnp.einsum("jrd,jrc->jdc", agg_one.astype(jnp.float32), dz_one.astype(jnp.float32))
        tile_two = jnp.einsum("jrd,jrc->jdc", agg_two.astype(jnp.float32), dz_two.astype(jnp.float32))
        grad_one = grad_one + jnp.einsum("je,jdc->dec", onehot, tile_one)
        grad_two = grad_two + jnp.einsum("je,jdc->dec", onehot, tile_two)
        return (grad_one, grad_two), (h_two.reshape(per_dev, width), h_one.reshape(per_dev, width))

    start = (jnp.zeros(w_one.shape, jnp.float32), jnp.zeros(w_two.shape, jnp.float32))
    (grad_one, grad_two), (h_two, h_one) = lax.scan(one_device, start, jnp.arange(devs, dtype=jnp.int32))
    return h_two.reshape(nodes, width), h_one.reshape(nodes, width), grad_one, grad_two
```

```python
import jax
import jax.numpy as jnp
import numpy as np
from jax import lax
from jax.sharding import Mesh, PartitionSpec as P

DOM = ("y", "z", "c")
BF = jnp.bfloat16
F32 = jnp.float32


def slope_silu(value):
    sig = jax.nn.sigmoid(value)
    return sig * (1.0 + value * (1.0 - sig))


def dot(spec, a, b):
    return jnp.einsum(spec, a, b, preferred_element_type=F32)


def spread_rep(rows):
    copies = jnp.broadcast_to(rows[None], (4,) + rows.shape)
    return lax.all_to_all(copies, "rep", split_axis=0, concat_axis=0, tiled=True)


def shards(
    feats, hist_one, local_val, halo_val, halo_send, halo_tile, tile_type, w_one, w_two, grad_out
):
    tile = local_val.shape[1]
    rows = feats.shape[0] // tile
    cols = feats.shape[1]
    width, experts, _ = w_one.shape
    reps = width // cols
    parts, cap = halo_send.shape[1], halo_send.shape[2]
    nodes = feats.shape[0]
    local_blocks = local_val.reshape(rows, tile, tile)
    halo_blocks = halo_val.reshape(rows, tile, tile)
    halo_pick = halo_tile[0]
    types = tile_type[0]
    send_rows = halo_send[0]
    code = jnp.broadcast_to(types.astype(F32)[:, None, None], (rows, 4, 128)).reshape(16, 128)
    all_types = lax.all_gather(code, DOM, axis=0, tiled=False)[:, ::4, 0]

    index = jnp.stack([send_rows, send_rows + nodes], axis=1).reshape(-1)
    pick = (index[:, None] == jnp.arange(2 * nodes, dtype=jnp.int32)[None, :]).astype(BF)
    table = jnp.concatenate([feats, hist_one], axis=0)
    picked = dot("ab,bc->ac", pick, table).astype(BF).reshape(parts, 2 * cap, cols)
    landed = lax.all_to_all(picked, DOM, split_axis=0, concat_axis=0, tiled=True)
    landed = landed.reshape(rows, 2 * tile, cols)
    order = np.zeros((2, tile, 2 * tile), np.float32)
    for t in range(2):
        for k in range(tile):
            order[t, k, (k // cap) * 2 * cap + t * cap + k % cap] = 1.0
    wide = dot("jrk,tkm->tjrm", halo_blocks, jnp.asarray(order, BF)).astype(BF)
    halo = jnp.take(landed, halo_pick, axis=0)

    source = feats.reshape(rows, tile, cols)
    agg_own = (dot("jrk,jkc->jrc", local_blocks, source) + dot("jrk,jkc->jrc", wide[0], halo)).astype(BF)
    agg_one = spread_rep(agg_own.reshape(nodes, cols)).reshape(reps, rows, tile, cols)
    pick_one = jnp.take(w_one, types, axis=1).reshape(reps, cols, rows, cols)
    z_one = dot("qjrd,qdjc->jrc", agg_one, pick_one)
    h_one = (source.astype(F32) + jax.nn.silu(z_one)).astype(BF)

    agg_own = (dot("jrk,jkc->jrc", local_blocks, h_one) + dot("jrk,jkc->jrc", wide[1], halo)).astype(BF)
    agg_two = spread_rep(agg_own.reshape(nodes, cols)).reshape(reps, rows, tile, cols)
    pick_two = jnp.take(w_two, types, axis=1).reshape(reps, cols, rows, cols)
    z_two = dot("qjrd,qdjc->jrc", agg_two, pick_two)
    h_two = (h_one.astype(F32) + jax.nn.silu(z_two)).astype(BF)
    upstream = grad_out.reshape(rows, tile, cols).astype(F32)
    dz_two = (upstream * slope_silu(z_two)).astype(BF)
    partial_back = dot("jrc,qdjc->qjrd", dz_two, pick_two).astype(BF).reshape(reps, nodes, cols)
    partial_back = lax.all_to_all(partial_back, "rep", split_axis=0, concat_axis=0, tiled=True)
    dagg = jnp.sum(partial_back.astype(F32), axis=0).astype(BF).reshape(rows, tile, cols)
    dh_one = upstream + dot("jrk,jrc->jkc", local_blocks, dagg)
    dz_one = (dh_one * slope_silu(z_one)).astype(BF)

    half = parts // 2
    own = width // half
    tiles = []
    for agg, dz in ((agg_one, dz_one), (agg_two, dz_two)):
        part = dot("qjrd,jrc->jqdc", agg, dz).astype(BF)
        tiles.append(part.reshape(rows, half, own, cols).transpose(1, 0, 2, 3))
    sent = jnp.concatenate(tiles, axis=0)
    got = lax.all_to_all(sent, DOM, split_axis=0, concat_axis=0, tiled=True)
    onehot = (
        all_types[:, :, None] == jnp.arange(experts, dtype=F32)[None, None, :]
    ).astype(BF)
    mine = dot("pje,pjdc->dec", onehot, got).astype(BF).reshape(own * experts, cols)

    copies = jnp.broadcast_to(mine[None], (half,) + mine.shape)
    same = lax.all_to_all(copies, ("y", "z"), split_axis=0, concat_axis=0, tiled=True)
    other = lax.ppermute(same, "c", [(0, 1), (1, 0)])
    core = lax.axis_index("c")
    even = jnp.where(core == 0, same, other)
    odd = jnp.where(core == 0, other, same)
    both = jnp.stack([even, odd], axis=1).reshape(2, width, experts, cols).astype(F32)
    return (h_two.reshape(-1, cols), h_one.reshape(-1, cols), both[0], both[1])


def solution(mesh):
    fine = Mesh(mesh.devices.reshape(8, 8, 2, 4), ("y", "z", "c", "rep"))
    in_specs = (
        P(DOM, "rep"),
        P(DOM, "rep"),
        P(DOM, None),
        P(DOM, None),
        P(DOM, None, None),
        P(DOM, None),
        P(DOM, None),
        P(None, None, "rep"),
        P(None, None, "rep"),
        P(DOM, "rep"),
    )
    out_specs = (P(DOM, "rep"), P(DOM, "rep"), P(None, None, "rep"), P(None, None, "rep"))
    return jax.shard_map(shards, mesh=fine, in_specs=in_specs, out_specs=out_specs, check_vma=False)
```

```python
import jax
import jax.numpy as jnp
import numpy as np
from jax import lax
from jax.experimental import pallas as pl
from jax.experimental.pallas import tpu as pltpu
from jax.sharding import PartitionSpec as P

DOM = "dom"
BF = jnp.bfloat16
F32 = jnp.float32


def slope_silu(value):
    sig = jax.nn.sigmoid(value)
    return sig * (1.0 + value * (1.0 - sig))


def dot(spec, a, b):
    return jnp.einsum(spec, a, b, preferred_element_type=F32)


def spread_rep(rows):
    copies = jnp.broadcast_to(rows[None], (4,) + rows.shape)
    return lax.all_to_all(copies, "rep", split_axis=0, concat_axis=0, tiled=True)


def grad_body(types, core, agg, dz, keep, send):
    reps, nodes, _ = agg.shape
    rows = types.shape[0]
    tile = nodes // rows
    half = keep.shape[1] // dz.shape[1]
    for target, side in ((send, 1 - core[0]), (keep, core[0])):
        wide = []
        for e in range(half):
            part = []
            for j in range(rows):
                block = dz[j * tile : (j + 1) * tile, :]
                hit = (types[j] == side * half + e).astype(F32)
                part.append((block.astype(F32) * hit).astype(BF))
            wide.append(jnp.concatenate(part, axis=0))
        wide = jnp.concatenate(wide, axis=1)
        for q in range(reps):
            cols = agg.shape[2]
            block = lax.dot_general(
                agg[q], wide, (((0,), (0,)), ((), ())), preferred_element_type=F32
            )
            target[q * cols : (q + 1) * cols, :] = block.astype(target.dtype)


def grad_halves(types, core, agg, dz):
    reps, nodes, cols = agg.shape
    half = 4 * cols
    smem = pl.BlockSpec(memory_space=pltpu.SMEM)
    vmem = pl.BlockSpec(memory_space=pltpu.VMEM)
    return pl.pallas_call(
        grad_body,
        out_shape=(
            jax.ShapeDtypeStruct((reps * cols, half), F32),
            jax.ShapeDtypeStruct((reps * cols, half), BF),
        ),
        in_specs=[smem, smem, vmem, vmem],
        out_specs=(vmem, vmem),
        compiler_params=pltpu.CompilerParams(vmem_limit_bytes=32 << 20),
        name="grad_halves",
    )(types, core, agg, dz)


def unpack_body(core, same, other, one, two):
    first = core[0] == 0
    for layer, out in enumerate((one, two)):
        half = out.shape[1] // 2
        cols = out.shape[2]
        for s in range(same.shape[0]):
            mine = same[s, layer].astype(F32)
            theirs = other[s, layer].astype(F32)
            low = jnp.where(first, mine, theirs)
            high = jnp.where(first, theirs, mine)
            rows = slice(s * mine.shape[0], (s + 1) * mine.shape[0])
            for e in range(half):
                out[rows, e, :] = low[:, e * cols : (e + 1) * cols]
                out[rows, half + e, :] = high[:, e * cols : (e + 1) * cols]


def unpack(core, same, other):
    chunks, layers, rows, span = same.shape
    cols = 128
    step = 8
    experts = 2 * span // cols
    block = pl.BlockSpec((step, layers, rows, span), lambda i: (i, 0, 0, 0))
    target = pl.BlockSpec((step * rows, experts, cols), lambda i: (i, 0, 0))
    shape = jax.ShapeDtypeStruct((chunks * rows, experts, cols), F32)
    return pl.pallas_call(
        unpack_body,
        grid=(chunks // step,),
        out_shape=(shape, shape),
        in_specs=[pl.BlockSpec(memory_space=pltpu.SMEM), block, block],
        out_specs=(target, target),
        name="unpack",
    )(core, same, other)


def rings():
    along_y = [[[(y * 8 + z) * 2 + c for y in range(8)] for z in range(8)] for c in range(2)]
    along_z = [[[(y * 8 + z) * 2 + c for z in range(8)] for y in range(8)] for c in range(2)]
    return along_y[0] + along_z[1], along_z[0] + along_y[1]


def exchange(blocks, groups):
    return lax.all_to_all(
        blocks, "dom", split_axis=0, concat_axis=0, axis_index_groups=groups, tiled=True
    )


def pair_sum(agg, dz, types, core):
    reps, rows, tile, width = agg.shape
    keep, send = grad_halves(
        types, core, agg.reshape(reps, rows * tile, width), dz.reshape(rows * tile, width)
    )
    came = lax.ppermute(send, "dom", [(p, p ^ 1) for p in range(128)])
    return (keep + came.astype(F32)).astype(BF).reshape(8, 64, -1)


def gather_sum(parts):
    return jnp.sum(parts.astype(F32), axis=0).astype(BF)


def spread(rows, groups):
    copies = jnp.broadcast_to(rows[None], (8,) + rows.shape)
    return exchange(copies, groups).reshape((-1,) + rows.shape[1:])


def shards(
    feats, hist_one, local_val, halo_val, halo_send, halo_tile, tile_type, w_one, w_two, grad_out
):
    tile = local_val.shape[1]
    rows = feats.shape[0] // tile
    cols = feats.shape[1]
    width, experts, _ = w_one.shape
    reps = width // cols
    parts, cap = halo_send.shape[1], halo_send.shape[2]
    nodes = feats.shape[0]
    local_blocks = local_val.reshape(rows, tile, tile)
    halo_blocks = halo_val.reshape(rows, tile, tile)
    halo_pick = halo_tile[0]
    types = tile_type[0]
    send_rows = halo_send[0]
    core = (lax.axis_index("dom") % 2).astype(jnp.int32).reshape(1)
    first, second = rings()

    index = jnp.stack([send_rows, send_rows + nodes], axis=1).reshape(-1)
    pick = (index[:, None] == jnp.arange(2 * nodes, dtype=jnp.int32)[None, :]).astype(BF)
    table = jnp.concatenate([feats, hist_one], axis=0)
    picked = dot("ab,bc->ac", pick, table).astype(BF).reshape(parts, 2 * cap, cols)
    landed = lax.all_to_all(picked, DOM, split_axis=0, concat_axis=0, tiled=True)
    landed = landed.reshape(rows, 2 * tile, cols)
    order = np.zeros((2, tile, 2 * tile), np.float32)
    for t in range(2):
        for k in range(tile):
            order[t, k, (k // cap) * 2 * cap + t * cap + k % cap] = 1.0
    wide = dot("jrk,tkm->tjrm", halo_blocks, jnp.asarray(order, BF)).astype(BF)
    halo = jnp.take(landed, halo_pick, axis=0)

    source = feats.reshape(rows, tile, cols)
    agg_own = (dot("jrk,jkc->jrc", local_blocks, source) + dot("jrk,jkc->jrc", wide[0], halo)).astype(BF)
    agg_one = spread_rep(agg_own.reshape(nodes, cols)).reshape(reps, rows, tile, cols)
    pick_one = jnp.take(w_one, types, axis=1).reshape(reps, cols, rows, cols)
    z_one = dot("qjrd,qdjc->jrc", agg_one, pick_one)
    h_one = (source.astype(F32) + jax.nn.silu(z_one)).astype(BF)

    agg_own = (dot("jrk,jkc->jrc", local_blocks, h_one) + dot("jrk,jkc->jrc", wide[1], halo)).astype(BF)
    agg_two = spread_rep(agg_own.reshape(nodes, cols)).reshape(reps, rows, tile, cols)
    pick_two = jnp.take(w_two, types, axis=1).reshape(reps, cols, rows, cols)
    z_two = dot("qjrd,qdjc->jrc", agg_two, pick_two)
    h_two = (h_one.astype(F32) + jax.nn.silu(z_two)).astype(BF)
    upstream = grad_out.reshape(rows, tile, cols).astype(F32)
    dz_two = (upstream * slope_silu(z_two)).astype(BF)
    sum_two = gather_sum(exchange(pair_sum(agg_two, dz_two, types, core), first))
    partial_back = dot("jrc,qdjc->qjrd", dz_two, pick_two).astype(BF).reshape(reps, nodes, cols)
    partial_back = lax.all_to_all(partial_back, "rep", split_axis=0, concat_axis=0, tiled=True)
    dagg = jnp.sum(partial_back.astype(F32), axis=0).astype(BF).reshape(rows, tile, cols)
    dh_one = upstream + dot("jrk,jrc->jkc", local_blocks, dagg)
    dz_one = (dh_one * slope_silu(z_one)).astype(BF)

    sum_one = gather_sum(exchange(pair_sum(agg_one, dz_one, types, core), first))
    span = sum_one.shape[1]
    both = jnp.stack([sum_one.reshape(8, 8, span), sum_two.reshape(8, 8, span)], axis=1)
    mine = gather_sum(exchange(both, second))
    some = spread(mine[None], second)
    same = spread(some, first).reshape(64, 2, 8, span)
    other = lax.ppermute(same, "dom", [(p, p ^ 1) for p in range(128)])
    grad_one, grad_two = unpack(core, same, other)
    return (h_two.reshape(-1, cols), h_one.reshape(-1, cols), grad_one, grad_two)


def solution(mesh):
    in_specs = (
        P(DOM, "rep"),
        P(DOM, "rep"),
        P(DOM, None),
        P(DOM, None),
        P(DOM, None, None),
        P(DOM, None),
        P(DOM, None),
        P(None, None, "rep"),
        P(None, None, "rep"),
        P(DOM, "rep"),
    )
    out_specs = (P(DOM, "rep"), P(DOM, "rep"), P(None, None, "rep"), P(None, None, "rep"))
    return jax.shard_map(shards, mesh=mesh, in_specs=in_specs, out_specs=out_specs, check_vma=False)
```

```python
import jax
import jax.numpy as jnp
import numpy as np
from jax import lax
from jax.experimental import pallas as pl
from jax.experimental.pallas import tpu as pltpu
from jax.sharding import PartitionSpec as P

DOM = "dom"
BF = jnp.bfloat16
F32 = jnp.float32


def slope_silu(value):
    sig = jax.nn.sigmoid(value)
    return sig * (1.0 + value * (1.0 - sig))


def dot(spec, a, b):
    return jnp.einsum(spec, a, b, preferred_element_type=F32)


def spread_rep(rows):
    copies = jnp.broadcast_to(rows[None], (4,) + rows.shape)
    return lax.all_to_all(copies, "rep", split_axis=0, concat_axis=0, tiled=True)


SMEM = pl.BlockSpec(memory_space=pltpu.SMEM)
VMEM = pl.BlockSpec(memory_space=pltpu.VMEM)
PARAMS = pltpu.CompilerParams(vmem_limit_bytes=40 << 20)


def grad_body(types, core, agg, dz, keep, send):
    reps, nodes, cols = agg.shape
    rows = types.shape[0]
    tile = nodes // rows
    experts = keep.shape[1] // dz.shape[1]
    wide = []
    for e in range(experts):
        part = []
        for j in range(rows):
            block = dz[j * tile : (j + 1) * tile, :]
            part.append((block.astype(F32) * (types[j] == e).astype(F32)).astype(BF))
        wide.append(jnp.concatenate(part, axis=0))
    wide = jnp.concatenate(wide, axis=1)
    for target, side in ((send, 1 - core[0]), (keep, core[0])):
        for i in range(reps // 2):
            block = lax.dot_general(
                agg[side * (reps // 2) + i],
                wide,
                (((0,), (0,)), ((), ())),
                preferred_element_type=F32,
            )
            target[i * cols : (i + 1) * cols, :] = block.astype(target.dtype)


def grad_halves(types, core, agg, dz):
    reps, nodes, cols = agg.shape
    shape = (reps * cols // 2, 8 * cols)
    return pl.pallas_call(
        grad_body,
        out_shape=(jax.ShapeDtypeStruct(shape, F32), jax.ShapeDtypeStruct(shape, BF)),
        in_specs=[SMEM, SMEM, VMEM, VMEM],
        out_specs=(VMEM, VMEM),
        compiler_params=PARAMS,
        name="grad_halves",
    )(types, core, agg, dz)


def add_up(parts):
    total = parts[0].astype(F32)
    for i in range(1, parts.shape[0]):
        total = total + parts[i].astype(F32)
    return total


def first_body(parts, copies):
    total = add_up(parts).astype(BF)
    for i in range(copies.shape[0]):
        copies[i] = total


def first_sum(parts):
    return pl.pallas_call(
        first_body,
        out_shape=jax.ShapeDtypeStruct((8,) + parts.shape[1:], BF),
        in_specs=[VMEM],
        out_specs=VMEM,
        compiler_params=PARAMS,
        name="first_sum",
    )(parts)


def second_body(parts, copies, table):
    rows, experts, cols = table.shape
    total = add_up(parts)
    for e in range(experts):
        table[:, e, :] = total[:, e * cols : (e + 1) * cols]
    laid = table[...].reshape(rows * experts, cols).astype(BF)
    for i in range(copies.shape[0]):
        copies[i] = laid


def second_sum(parts):
    _, rows, span = parts.shape
    cols = 128
    experts = span // cols
    return pl.pallas_call(
        second_body,
        out_shape=jax.ShapeDtypeStruct((8, rows * experts, cols), BF),
        in_specs=[VMEM],
        out_specs=VMEM,
        scratch_shapes=[pltpu.VMEM((rows, experts, cols), F32)],
        compiler_params=PARAMS,
        name="second_sum",
    )(parts)


def widen_body(core, same, other, one, two):
    step = pl.program_id(0)
    chunks = same.shape[0]
    own = core[0] == step // (chunks // 2)
    length = same.shape[1] // 2
    for i in range(2):
        at = lax.rem(step, chunks // 2) * 2 + i
        both = jnp.where(own, same[at].astype(F32), other[at].astype(F32))
        one[i * length : (i + 1) * length, :] = both[:length]
        two[i * length : (i + 1) * length, :] = both[length:]


def widen(core, same, other):
    chunks, length, cols = same.shape
    steps = chunks
    target = pl.BlockSpec((length, cols), lambda i: (i, 0))
    shape = jax.ShapeDtypeStruct((chunks * length, cols), F32)
    return pl.pallas_call(
        widen_body,
        grid=(steps,),
        out_shape=(shape, shape),
        in_specs=[SMEM, VMEM, VMEM],
        out_specs=(target, target),
        compiler_params=PARAMS,
        name="widen",
    )(core, same, other)


def rings():
    along_y = [[[(y * 8 + z) * 2 + c for y in range(8)] for z in range(8)] for c in range(2)]
    along_z = [[[(y * 8 + z) * 2 + c for z in range(8)] for y in range(8)] for c in range(2)]
    return along_y[0] + along_z[1], along_z[0] + along_y[1]


def exchange(blocks, groups):
    return lax.all_to_all(
        blocks, "dom", split_axis=0, concat_axis=0, axis_index_groups=groups, tiled=True
    )


def swap(rows):
    return lax.ppermute(rows, "dom", [(p, p ^ 1) for p in range(128)])


def pair_sum(agg, dz, types, core):
    reps, rows, tile, width = agg.shape
    keep, send = grad_halves(
        types, core, agg.reshape(reps, rows * tile, width), dz.reshape(rows * tile, width)
    )
    return (keep + swap(send).astype(F32)).astype(BF).reshape(8, 32, -1)


def shards(
    feats, hist_one, local_val, halo_val, halo_send, halo_tile, tile_type, w_one, w_two, grad_out
):
    tile = local_val.shape[1]
    rows = feats.shape[0] // tile
    cols = feats.shape[1]
    width, experts, _ = w_one.shape
    reps = width // cols
    parts, cap = halo_send.shape[1], halo_send.shape[2]
    nodes = feats.shape[0]
    local_blocks = local_val.reshape(rows, tile, tile)
    halo_blocks = halo_val.reshape(rows, tile, tile)
    halo_pick = halo_tile[0]
    types = tile_type[0]
    send_rows = halo_send[0]
    core = (lax.axis_index("dom") % 2).astype(jnp.int32).reshape(1)
    first, second = rings()

    index = jnp.stack([send_rows, send_rows + nodes], axis=1).reshape(-1)
    pick = (index[:, None] == jnp.arange(2 * nodes, dtype=jnp.int32)[None, :]).astype(BF)
    table = jnp.concatenate([feats, hist_one], axis=0)
    picked = dot("ab,bc->ac", pick, table).astype(BF).reshape(parts, 2 * cap, cols)
    landed = lax.all_to_all(picked, DOM, split_axis=0, concat_axis=0, tiled=True)
    landed = landed.reshape(rows, 2 * tile, cols)
    order = np.zeros((2, tile, 2 * tile), np.float32)
    for t in range(2):
        for k in range(tile):
            order[t, k, (k // cap) * 2 * cap + t * cap + k % cap] = 1.0
    wide = dot("jrk,tkm->tjrm", halo_blocks, jnp.asarray(order, BF)).astype(BF)
    halo = jnp.take(landed, halo_pick, axis=0)

    source = feats.reshape(rows, tile, cols)
    agg_own = (dot("jrk,jkc->jrc", local_blocks, source) + dot("jrk,jkc->jrc", wide[0], halo)).astype(BF)
    agg_one = spread_rep(agg_own.reshape(nodes, cols)).reshape(reps, rows, tile, cols)
    pick_one = jnp.take(w_one, types, axis=1).reshape(reps, cols, rows, cols)
    z_one = dot("qjrd,qdjc->jrc", agg_one, pick_one)
    h_one = (source.astype(F32) + jax.nn.silu(z_one)).astype(BF)

    agg_own = (dot("jrk,jkc->jrc", local_blocks, h_one) + dot("jrk,jkc->jrc", wide[1], halo)).astype(BF)
    agg_two = spread_rep(agg_own.reshape(nodes, cols)).reshape(reps, rows, tile, cols)
    pick_two = jnp.take(w_two, types, axis=1).reshape(reps, cols, rows, cols)
    z_two = dot("qjrd,qdjc->jrc", agg_two, pick_two)
    h_two = (h_one.astype(F32) + jax.nn.silu(z_two)).astype(BF)
    upstream = grad_out.reshape(rows, tile, cols).astype(F32)
    dz_two = (upstream * slope_silu(z_two)).astype(BF)
    pair_two = pair_sum(agg_two, dz_two, types, core)
    partial_back = dot("jrc,qdjc->qjrd", dz_two, pick_two).astype(BF).reshape(reps, nodes, cols)
    partial_back = lax.all_to_all(partial_back, "rep", split_axis=0, concat_axis=0, tiled=True)
    dagg = jnp.sum(partial_back.astype(F32), axis=0).astype(BF).reshape(rows, tile, cols)
    dh_one = upstream + dot("jrk,jrc->jkc", local_blocks, dagg)
    dz_one = (dh_one * slope_silu(z_one)).astype(BF)

    pair_one = pair_sum(agg_one, dz_one, types, core)
    both = exchange(jnp.concatenate([pair_one, pair_two], axis=1), first)
    both = exchange(first_sum(both), second)
    same = exchange(second_sum(both), first)
    grad_one, grad_two = widen(core, same, swap(same))
    grad_one, grad_two = grad_one.reshape(w_one.shape), grad_two.reshape(w_two.shape)
    return (h_two.reshape(-1, cols), h_one.reshape(-1, cols), grad_one, grad_two)


def solution(mesh):
    in_specs = (
        P(DOM, "rep"),
        P(DOM, "rep"),
        P(DOM, None),
        P(DOM, None),
        P(DOM, None, None),
        P(DOM, None),
        P(DOM, None),
        P(None, None, "rep"),
        P(None, None, "rep"),
        P(DOM, "rep"),
    )
    out_specs = (P(DOM, "rep"), P(DOM, "rep"), P(None, None, "rep"), P(None, None, "rep"))
    return jax.shard_map(shards, mesh=mesh, in_specs=in_specs, out_specs=out_specs, check_vma=False)
```

```python
import jax
import jax.numpy as jnp
from jax import lax
from jax.experimental import pallas as pl
from jax.experimental.pallas import tpu as pltpu
from jax.sharding import PartitionSpec as P

BF = jnp.bfloat16
F32 = jnp.float32
SMEM = pl.BlockSpec(memory_space=pltpu.SMEM)
VMEM = pl.BlockSpec(memory_space=pltpu.VMEM)
ANY = pl.BlockSpec(memory_space=pl.ANY)
PARAMS = pltpu.CompilerParams(vmem_limit_bytes=40 << 20)
PAIR = 2
RING = 16
CROSS = 4
REPS = 4
TILE = 128


def call(body, name, ins, outs, scratch=()):
    return pl.pallas_call(
        body,
        out_shape=tuple(jax.ShapeDtypeStruct(shape, kind) for shape, kind in outs),
        in_specs=list(ins),
        out_specs=tuple(VMEM for _ in outs),
        scratch_shapes=list(scratch),
        compiler_params=PARAMS,
        name=name,
    )


def dot(a, b, dims=((1,), (0,))):
    return lax.dot_general(a, b, (dims, ((), ())), preferred_element_type=F32)


def block(j):
    return slice(j * TILE, (j + 1) * TILE)


def iota(shape, axis):
    return lax.broadcasted_iota(jnp.int32, shape, axis)


def pick_body(send, feats, hist, out, rows):
    cap, parts = send.shape
    nodes, cols = feats.shape
    table = jnp.concatenate([feats[...], hist[...]], axis=1)
    for c in range(cap):
        hit = (iota((nodes, parts), 0) == send[c : c + 1, :]).astype(F32).astype(BF)
        got = dot(hit, table, ((0,), (0,)))
        rows[:, c, :] = got[:, :cols]
        rows[:, cap + c, :] = got[:, cols:]
    out[...] = rows[...].astype(BF)


def select_body(types, weights, out):
    rows, width, _ = out.shape
    experts = weights.shape[0] // width
    span = TILE // rows
    shape = (rows * span, span * experts)
    at, source = iota(shape, 0), iota(shape, 1)
    kind = jnp.zeros(shape, jnp.int32)
    for j in range(rows):
        kind = jnp.where(at // span == j, types[j], kind)
    hit = (source == (at % span) * experts + kind).astype(F32).astype(BF)
    for i in range(width // span):
        got = dot(hit, weights[i * span * experts : (i + 1) * span * experts, :]).astype(BF)
        for j in range(rows):
            out[j, i * span : (i + 1) * span, :] = got[j * span : (j + 1) * span]


def ready_body(local, halo_val, feats, base, wide):
    cap = wide.shape[2] // 2 // 32
    shape = (TILE, 2 * TILE)
    k, m = iota(shape, 0), iota(shape, 1)
    spot = (k // cap) * (2 * cap) + k % cap
    first = (m == spot).astype(F32).astype(BF)
    second = (m == spot + cap).astype(F32).astype(BF)
    for j in range(wide.shape[0]):
        base[block(j), :] = dot(local[block(j), :], feats[block(j), :])
        wide[j, :TILE, :] = dot(halo_val[block(j), :], first).astype(BF)
        wide[j, TILE:, :] = dot(halo_val[block(j), :], second).astype(BF)


def gather_body(pick, landed, wide, base, copies, part):
    for j in range(wide.shape[0]):
        both = dot(wide[j], landed[pick[j]])
        agg = (base[block(j), :] + both[:TILE]).astype(BF)
        part[block(j), :] = both[TILE:]
        for q in range(copies.shape[0]):
            copies[q, block(j), :] = agg


def forward(agg, weights, j):
    rows = jnp.concatenate([agg[q, block(j), :] for q in range(agg.shape[0])], axis=1)
    z = dot(rows, weights[j])
    sig = jax.nn.sigmoid(z)
    return z * sig, sig * (1.0 + z * (1.0 - sig))


def one_body(agg, weights, feats, local, part, hidden, slope, copies):
    for j in range(weights.shape[0]):
        act, bend = forward(agg, weights, j)
        slope[block(j), :] = bend
        h = (feats[block(j), :].astype(F32) + act).astype(BF)
        hidden[block(j), :] = h
        mixed = (dot(local[block(j), :], h) + part[block(j), :]).astype(BF)
        for q in range(copies.shape[0]):
            copies[q, block(j), :] = mixed


def two_body(agg, weights, h_one, grad, hidden, dz, back):
    cols = dz.shape[1]
    for j in range(weights.shape[0]):
        act, bend = forward(agg, weights, j)
        hidden[block(j), :] = (h_one[block(j), :].astype(F32) + act).astype(BF)
        d = (grad[block(j), :].astype(F32) * bend).astype(BF)
        dz[block(j), :] = d
        term = dot(d, weights[j], ((1,), (1,))).astype(BF)
        for q in range(back.shape[0]):
            back[q, block(j), :] = term[:, q * cols : (q + 1) * cols]


def write_grad(types, core, agg, dz, keep, send):
    reps, _, cols = agg.shape
    rows = types.shape[0]
    experts = keep.shape[1] // cols
    wide = []
    for e in range(experts):
        part = []
        for j in range(rows):
            part.append((dz[block(j), :].astype(F32) * (types[j] == e).astype(F32)).astype(BF))
        wide.append(jnp.concatenate(part, axis=0))
    wide = jnp.concatenate(wide, axis=1)
    for target, side in ((send, 1 - core[0]), (keep, core[0])):
        for i in range(reps // 2):
            got = dot(agg[side * (reps // 2) + i], wide, ((0,), (0,)))
            target[i * cols : (i + 1) * cols, :] = got.astype(target.dtype)


def back_body(types, core, parts, local, grad, slope, agg, keep, send, dz):
    for j in range(types.shape[0]):
        total = parts[0, block(j), :].astype(F32)
        for q in range(1, parts.shape[0]):
            total = total + parts[q, block(j), :].astype(F32)
        dh = grad[block(j), :].astype(F32) + dot(
            local[block(j), :], total.astype(BF), ((0,), (0,))
        )
        dz[block(j), :] = (dh * slope[block(j), :]).astype(BF)
    write_grad(types, core, agg, dz, keep, send)


def add_up(parts):
    total = parts[0].astype(F32)
    for i in range(1, parts.shape[0]):
        total = total + parts[i].astype(F32)
    return total


def first_body(parts, copies):
    total = add_up(parts).astype(BF)
    for i in range(copies.shape[0]):
        copies[i] = total


def second_body(parts, copies, table):
    rows, experts, cols = table.shape
    total = add_up(parts)
    for e in range(experts):
        table[:, e, :] = total[:, e * cols : (e + 1) * cols]
    laid = table[...].reshape(rows * experts, cols).astype(BF)
    for i in range(copies.shape[0]):
        copies[i] = laid


def widen_body(core, half, *refs):
    one, two = refs[-2:]
    step = pl.program_id(0)
    length = half.shape[1] // 2
    count = one.shape[0] // length
    for i in range(count):
        rows = half[step * count + i].astype(F32)
        one[i * length : (i + 1) * length, :] = rows[:length]
        two[i * length : (i + 1) * length, :] = rows[length:]


def widen(core, half, before=()):
    chunks, length, cols = half.shape
    steps = 4
    own = not before
    height = chunks // steps * (length // 2)
    target = pl.BlockSpec(
        (height, cols), lambda i, c: ((c[0] if own else 1 - c[0]) * steps + i, 0)
    )
    shape = jax.ShapeDtypeStruct((chunks * length, cols), F32)
    return pl.pallas_call(
        widen_body,
        grid_spec=pltpu.PrefetchScalarGridSpec(
            num_scalar_prefetch=1,
            grid=(steps,),
            in_specs=[VMEM] + [ANY] * len(before),
            out_specs=(target, target),
        ),
        out_shape=(shape, shape),
        input_output_aliases={} if own else {2: 0, 3: 1},
        compiler_params=PARAMS,
        name="widen_own" if own else "widen_other",
    )(core, half, *before)


def rings():
    def device(core, line, cross):
        y, z = (line, cross) if core == 0 else (cross, line)
        return (y * 8 + z) * 2 + core

    first = [
        [device(core, line, pair * PAIR + i) for i in range(PAIR) for line in range(8)]
        for core in range(2)
        for pair in range(8 // PAIR)
    ]
    second = [
        [device(core, line, pair * PAIR + i) for pair in range(8 // PAIR)]
        for core in range(2)
        for line in range(8)
        for i in range(PAIR)
    ]
    return first, second


def exchange(blocks, groups):
    return lax.all_to_all(
        blocks, "dom", split_axis=0, concat_axis=0, axis_index_groups=groups, tiled=True
    )


def across(blocks):
    return lax.all_to_all(blocks, "rep", split_axis=0, concat_axis=0, tiled=True)


def swap(rows):
    return lax.ppermute(rows, "dom", [(p, p ^ 1) for p in range(128)])


def shards(
    feats, hist_one, local_val, halo_val, halo_send, halo_tile, tile_type, w_one, w_two, grad_out
):
    nodes, cols = feats.shape
    rows = nodes // TILE
    width, experts, _ = w_one.shape
    parts, cap = halo_send.shape[1], halo_send.shape[2]
    pick, types = halo_tile[0], tile_type[0]
    core = lax.rem(lax.axis_index("dom"), 2).astype(jnp.int32).reshape(1)
    first, second = rings()
    flat = (nodes, cols)
    copied = (REPS, nodes, cols)

    (rows_out,) = call(
        pick_body,
        "pick",
        [VMEM] * 3,
        [((parts, 2 * cap, cols), BF)],
        [pltpu.VMEM((parts, 2 * cap, cols), F32)],
    )(jnp.swapaxes(halo_send[0], 0, 1), feats, hist_one)
    landed = lax.all_to_all(rows_out, "dom", split_axis=0, concat_axis=0, tiled=True)
    landed = landed.reshape(rows, 2 * TILE, cols)

    select = call(select_body, "select", [SMEM, VMEM], [((rows, width, cols), BF)])
    (pick_one,) = select(types, w_one.reshape(width * experts, cols))
    (pick_two,) = select(types, w_two.reshape(width * experts, cols))
    base, wide = call(
        ready_body, "ready", [VMEM] * 3, [(flat, F32), ((rows, 2 * TILE, 2 * TILE), BF)]
    )(local_val, halo_val, feats)

    copies, part = call(gather_body, "gather", [SMEM] + [VMEM] * 3, [(copied, BF), (flat, F32)])(
        pick, landed, wide, base
    )
    agg_one = across(copies)
    h_one, slope, copies = call(
        one_body, "one", [VMEM] * 5, [(flat, BF), (flat, F32), (copied, BF)]
    )(agg_one, pick_one, feats, local_val, part)
    agg_two = across(copies)
    h_two, dz_two, back = call(
        two_body, "two", [VMEM] * 4, [(flat, BF), (flat, BF), (copied, BF)]
    )(agg_two, pick_two, h_one, grad_out)
    back = across(back)

    half = (width // 2, experts * cols)
    keep_two, send_two = call(
        write_grad, "grad_two", [SMEM] * 2 + [VMEM] * 2, [(half, F32), (half, BF)]
    )(types, core, agg_two, dz_two)
    keep_one, send_one = call(
        back_body,
        "back",
        [SMEM] * 2 + [VMEM] * 5,
        [(half, F32), (half, BF)],
        [pltpu.VMEM(flat, BF)],
    )(types, core, back, local_val, grad_out, slope, agg_one)
    pair_one = (keep_one + swap(send_one).astype(F32)).astype(BF)
    pair_two = (keep_two + swap(send_two).astype(F32)).astype(BF)

    split = (RING, width // 2 // RING, experts * cols)
    both = jnp.concatenate([pair_one.reshape(split), pair_two.reshape(split)], axis=1)
    both = exchange(both, first)
    few = both.shape[1]
    (both,) = call(first_body, "first_sum", [VMEM], [((CROSS,) + both.shape[1:], BF)])(both)
    both = exchange(both, second)
    (both,) = call(
        second_body,
        "second_sum",
        [VMEM],
        [((RING, few * experts, cols), BF)],
        [pltpu.VMEM((few, experts, cols), F32)],
    )(both)
    same = exchange(both, first)
    grad_one, grad_two = widen(core, swap(same), widen(core, same))
    return h_two, h_one, grad_one.reshape(w_one.shape), grad_two.reshape(w_two.shape)


def solution(mesh):
    in_specs = (
        P("dom", "rep"),
        P("dom", "rep"),
        P("dom", None),
        P("dom", None),
        P("dom", None, None),
        P("dom", None),
        P("dom", None),
        P(None, None, "rep"),
        P(None, None, "rep"),
        P("dom", "rep"),
    )
    out_specs = (P("dom", "rep"), P("dom", "rep"), P(None, None, "rep"), P(None, None, "rep"))
    return jax.shard_map(shards, mesh=mesh, in_specs=in_specs, out_specs=out_specs, check_vma=False)
```

```python
import jax
import jax.numpy as jnp
from jax import lax
from jax.experimental import pallas as pl
from jax.experimental.pallas import tpu as pltpu
from jax.sharding import PartitionSpec as P

BF = jnp.bfloat16
F32 = jnp.float32
SMEM = pl.BlockSpec(memory_space=pltpu.SMEM)
VMEM = pl.BlockSpec(memory_space=pltpu.VMEM)
ANY = pl.BlockSpec(memory_space=pl.ANY)
FAR = pl.BlockSpec(memory_space=pltpu.HBM)
PARAMS = pltpu.CompilerParams(vmem_limit_bytes=40 << 20)
FULL = pltpu.CompilerParams(vmem_limit_bytes=60 << 20)
PAIR = 2
RING = 16
CROSS = 4
REPS = 4
TILE = 128


def call(body, name, ins, outs, scratch=(), params=PARAMS):
    return pl.pallas_call(
        body,
        out_shape=tuple(jax.ShapeDtypeStruct(shape, kind) for shape, kind in outs),
        in_specs=list(ins),
        out_specs=tuple(VMEM for _ in outs),
        scratch_shapes=list(scratch),
        compiler_params=params,
        name=name,
    )


def dot(a, b, dims=((1,), (0,))):
    return lax.dot_general(a, b, (dims, ((), ())), preferred_element_type=F32)


def block(j):
    return slice(j * TILE, (j + 1) * TILE)


def iota(shape, axis):
    return lax.broadcasted_iota(jnp.int32, shape, axis)


def fetch(sources, targets, sems):
    copies = [
        pltpu.make_async_copy(source, target, sems.at[i])
        for i, (source, target) in enumerate(zip(sources, targets))
    ]
    for copy in copies:
        copy.start()
    return copies


def pick_body(send_far, feats_far, hist_far, out, rows, send, table, sems):
    cap, parts = send.shape
    nodes, cols = feats_far.shape
    targets = (send, table.at[:, :cols], table.at[:, cols:])
    for copy in fetch((send_far, feats_far, hist_far), targets, sems):
        copy.wait()
    for c in range(cap):
        hit = (iota((nodes, parts), 0) == send[c : c + 1, :]).astype(F32).astype(BF)
        got = dot(hit, table[...], ((0,), (0,)))
        rows[:, c, :] = got[:, :cols]
        rows[:, cap + c, :] = got[:, cols:]
    out[...] = rows[...].astype(BF)


def select_rows(types, weights, out):
    rows, width, _ = out.shape
    experts = weights.shape[1]
    span = TILE // rows
    shape = (rows * span, span * experts)
    at, source = iota(shape, 0), iota(shape, 1)
    kind = jnp.zeros(shape, jnp.int32)
    for j in range(rows):
        kind = jnp.where(at // span == j, types[j], kind)
    hit = (source == (at % span) * experts + kind).astype(F32).astype(BF)
    for i in range(width // span):
        part = weights[i * span : (i + 1) * span].reshape(span * experts, -1)
        got = dot(hit, part).astype(BF)
        for j in range(rows):
            out[j, i * span : (i + 1) * span, :] = got[j * span : (j + 1) * span]


def ready_body(pick, types, *refs):
    far, (base, wide, one, two), near, sems = refs[:5], refs[5:9], refs[9:14], refs[14]
    copies = fetch(far, near, sems)
    local, halo_val, feats, w_one, w_two = near
    cap = wide.shape[2] // 2 // 32
    shape = (TILE, 2 * TILE)
    k, m = iota(shape, 0), iota(shape, 1)
    spot = (k // cap) * (2 * cap) + k % cap
    first = (m == spot).astype(F32).astype(BF)
    second = (m == spot + cap).astype(F32).astype(BF)
    for copy in copies[:3]:
        copy.wait()
    for j in range(wide.shape[0]):
        base[block(j), :] = dot(local[block(j), :], feats[block(j), :])
        wide[pick[j], :TILE, :] = dot(halo_val[block(j), :], first).astype(BF)
        wide[pick[j], TILE:, :] = dot(halo_val[block(j), :], second).astype(BF)
    copies[3].wait()
    select_rows(types, w_one, one)
    copies[4].wait()
    select_rows(types, w_two, two)


def gather_body(pick, landed, wide, base, copies, part):
    for j in range(wide.shape[0]):
        both = dot(wide[pick[j]], landed[pick[j]])
        agg = (base[block(j), :] + both[:TILE]).astype(BF)
        part[block(j), :] = both[TILE:]
        for q in range(copies.shape[0]):
            copies[q, block(j), :] = agg


def forward(agg, weights, j):
    rows = jnp.concatenate([agg[q, block(j), :] for q in range(agg.shape[0])], axis=1)
    z = dot(rows, weights[j])
    sig = jax.nn.sigmoid(z)
    return z * sig, sig * (1.0 + z * (1.0 - sig))


def one_body(agg, weights, feats, local, part, hidden, slope, copies):
    for j in range(weights.shape[0]):
        act, bend = forward(agg, weights, j)
        slope[block(j), :] = bend
        h = (feats[block(j), :].astype(F32) + act).astype(BF)
        hidden[block(j), :] = h
        mixed = (dot(local[block(j), :], h) + part[block(j), :]).astype(BF)
        for q in range(copies.shape[0]):
            copies[q, block(j), :] = mixed


def two_body(agg, weights, h_one, grad, hidden, dz, back):
    cols = dz.shape[1]
    for j in range(weights.shape[0]):
        act, bend = forward(agg, weights, j)
        hidden[block(j), :] = (h_one[block(j), :].astype(F32) + act).astype(BF)
        d = (grad[block(j), :].astype(F32) * bend).astype(BF)
        dz[block(j), :] = d
        term = dot(d, weights[j], ((1,), (1,))).astype(BF)
        for q in range(back.shape[0]):
            back[q, block(j), :] = term[:, q * cols : (q + 1) * cols]


def write_grad(types, core, agg, dz, keep, send):
    reps, _, cols = agg.shape
    rows = types.shape[0]
    experts = keep.shape[1] // cols
    wide = []
    for e in range(experts):
        part = []
        for j in range(rows):
            part.append((dz[block(j), :].astype(F32) * (types[j] == e).astype(F32)).astype(BF))
        wide.append(jnp.concatenate(part, axis=0))
    wide = jnp.concatenate(wide, axis=1)
    for target, side in ((send, 1 - core[0]), (keep, core[0])):
        for i in range(reps // 2):
            got = dot(agg[side * (reps // 2) + i], wide, ((0,), (0,)))
            target[i * cols : (i + 1) * cols, :] = got.astype(target.dtype)


def back_body(types, core, parts, local, grad, slope, agg, keep, send, dz):
    for j in range(types.shape[0]):
        total = parts[0, block(j), :].astype(F32)
        for q in range(1, parts.shape[0]):
            total = total + parts[q, block(j), :].astype(F32)
        dh = grad[block(j), :].astype(F32) + dot(
            local[block(j), :], total.astype(BF), ((0,), (0,))
        )
        dz[block(j), :] = (dh * slope[block(j), :]).astype(BF)
    write_grad(types, core, agg, dz, keep, send)


def add_up(parts):
    total = parts[0].astype(F32)
    for i in range(1, parts.shape[0]):
        total = total + parts[i].astype(F32)
    return total


def first_body(parts, copies):
    total = add_up(parts).astype(BF)
    for i in range(copies.shape[0]):
        copies[i] = total


def second_body(parts, copies, table):
    rows, experts, cols = table.shape
    total = add_up(parts)
    for e in range(experts):
        table[:, e, :] = total[:, e * cols : (e + 1) * cols]
    laid = table[...].reshape(rows * experts, cols).astype(BF)
    for i in range(copies.shape[0]):
        copies[i] = laid


def widen_body(core, half, *refs):
    one, two = refs[-2:]
    step = pl.program_id(0)
    length = half.shape[1] // 2
    count = one.shape[0] // length
    for i in range(count):
        rows = half[step * count + i].astype(F32)
        one[i * length : (i + 1) * length, :] = rows[:length]
        two[i * length : (i + 1) * length, :] = rows[length:]


def widen(core, half, before=()):
    chunks, length, cols = half.shape
    steps = 8
    own = not before
    height = chunks // steps * (length // 2)
    target = pl.BlockSpec(
        (height, cols), lambda i, c: ((c[0] if own else 1 - c[0]) * steps + i, 0)
    )
    shape = jax.ShapeDtypeStruct((chunks * length, cols), F32)
    return pl.pallas_call(
        widen_body,
        grid_spec=pltpu.PrefetchScalarGridSpec(
            num_scalar_prefetch=1,
            grid=(steps,),
            in_specs=[VMEM] + [ANY] * len(before),
            out_specs=(target, target),
        ),
        out_shape=(shape, shape),
        input_output_aliases={} if own else {2: 0, 3: 1},
        compiler_params=PARAMS,
        name="widen_own" if own else "widen_other",
    )(core, half, *before)


def rings():
    def device(core, line, cross):
        y, z = (line, cross) if core == 0 else (cross, line)
        return (y * 8 + z) * 2 + core

    first = [
        [device(core, line, pair * PAIR + i) for i in range(PAIR) for line in range(8)]
        for core in range(2)
        for pair in range(8 // PAIR)
    ]
    second = [
        [device(core, line, pair * PAIR + i) for pair in range(8 // PAIR)]
        for core in range(2)
        for line in range(8)
        for i in range(PAIR)
    ]
    return first, second


def exchange(blocks, groups):
    return lax.all_to_all(
        blocks, "dom", split_axis=0, concat_axis=0, axis_index_groups=groups, tiled=True
    )


def across(blocks):
    return lax.all_to_all(blocks, "rep", split_axis=0, concat_axis=0, tiled=True)


def swap(rows):
    return lax.ppermute(rows, "dom", [(p, p ^ 1) for p in range(128)])


def shards(
    feats, hist_one, local_val, halo_val, halo_send, halo_tile, tile_type, w_one, w_two, grad_out
):
    nodes, cols = feats.shape
    rows = nodes // TILE
    width, experts, _ = w_one.shape
    parts, cap = halo_send.shape[1], halo_send.shape[2]
    pick, types = halo_tile[0], tile_type[0]
    core = lax.rem(lax.axis_index("dom"), 2).astype(jnp.int32).reshape(1)
    first, second = rings()
    flat = (nodes, cols)
    copied = (REPS, nodes, cols)

    (rows_out,) = call(
        pick_body,
        "pick",
        [FAR] * 3,
        [((parts, 2 * cap, cols), BF)],
        [
            pltpu.VMEM((parts, 2 * cap, cols), F32),
            pltpu.VMEM((cap, parts), jnp.int32),
            pltpu.VMEM((nodes, 2 * cols), BF),
            pltpu.SemaphoreType.DMA((3,)),
        ],
        FULL,
    )(jnp.swapaxes(halo_send[0], 0, 1), feats, hist_one)
    landed = lax.all_to_all(rows_out, "dom", split_axis=0, concat_axis=0, tiled=True)
    landed = landed.reshape(rows, 2 * TILE, cols)

    chosen = (rows, width, cols)
    base, wide, pick_one, pick_two = call(
        ready_body,
        "ready",
        [SMEM] * 2 + [FAR] * 5,
        [(flat, F32), ((rows, 2 * TILE, 2 * TILE), BF), (chosen, BF), (chosen, BF)],
        [pltpu.VMEM(flat, BF)] * 3
        + [pltpu.VMEM(w_one.shape, BF)] * 2
        + [pltpu.SemaphoreType.DMA((5,))],
        FULL,
    )(pick, types, local_val, halo_val, feats, w_one, w_two)

    copies, part = call(gather_body, "gather", [SMEM] + [VMEM] * 3, [(copied, BF), (flat, F32)])(
        pick, landed, wide, base
    )
    agg_one = across(copies)
    h_one, slope, copies = call(
        one_body, "one", [VMEM] * 5, [(flat, BF), (flat, F32), (copied, BF)]
    )(agg_one, pick_one, feats, local_val, part)
    agg_two = across(copies)
    h_two, dz_two, back = call(
        two_body, "two", [VMEM] * 4, [(flat, BF), (flat, BF), (copied, BF)]
    )(agg_two, pick_two, h_one, grad_out)
    back = across(back)

    half = (width // 2, experts * cols)
    keep_two, send_two = call(
        write_grad, "grad_two", [SMEM] * 2 + [VMEM] * 2, [(half, F32), (half, BF)]
    )(types, core, agg_two, dz_two)
    keep_one, send_one = call(
        back_body,
        "back",
        [SMEM] * 2 + [VMEM] * 5,
        [(half, F32), (half, BF)],
        [pltpu.VMEM(flat, BF)],
    )(types, core, back, local_val, grad_out, slope, agg_one)
    pair_one = (keep_one + swap(send_one).astype(F32)).astype(BF)
    pair_two = (keep_two + swap(send_two).astype(F32)).astype(BF)

    split = (RING, width // 2 // RING, experts * cols)
    both = jnp.concatenate([pair_one.reshape(split), pair_two.reshape(split)], axis=1)
    both = exchange(both, first)
    few = both.shape[1]
    (both,) = call(first_body, "first_sum", [VMEM], [((CROSS,) + both.shape[1:], BF)])(both)
    both = exchange(both, second)
    (both,) = call(
        second_body,
        "second_sum",
        [VMEM],
        [((RING, few * experts, cols), BF)],
        [pltpu.VMEM((few, experts, cols), F32)],
    )(both)
    same = exchange(both, first)
    grad_one, grad_two = widen(core, swap(same), widen(core, same))
    return h_two, h_one, grad_one.reshape(w_one.shape), grad_two.reshape(w_two.shape)


def solution(mesh):
    in_specs = (
        P("dom", "rep"),
        P("dom", "rep"),
        P("dom", None),
        P("dom", None),
        P("dom", None, None),
        P("dom", None),
        P("dom", None),
        P(None, None, "rep"),
        P(None, None, "rep"),
        P("dom", "rep"),
    )
    out_specs = (P("dom", "rep"), P("dom", "rep"), P(None, None, "rep"), P(None, None, "rep"))
    return jax.shard_map(shards, mesh=mesh, in_specs=in_specs, out_specs=out_specs, check_vma=False)
```

```python
import jax
import jax.numpy as jnp
from jax import lax
from jax.experimental import pallas as pl
from jax.experimental.pallas import tpu as pltpu
from jax.sharding import PartitionSpec as P

BF = jnp.bfloat16
F32 = jnp.float32
SMEM = pl.BlockSpec(memory_space=pltpu.SMEM)
VMEM = pl.BlockSpec(memory_space=pltpu.VMEM)
ANY = pl.BlockSpec(memory_space=pl.ANY)
FAR = pl.BlockSpec(memory_space=pltpu.HBM)
PARAMS = pltpu.CompilerParams(vmem_limit_bytes=40 << 20)
FULL = pltpu.CompilerParams(vmem_limit_bytes=60 << 20)
PAIR = 2
RING = 16
CROSS = 4
REPS = 4
TILE = 128


def call(body, name, ins, outs, scratch=(), params=PARAMS):
    return pl.pallas_call(
        body,
        out_shape=tuple(jax.ShapeDtypeStruct(shape, kind) for shape, kind in outs),
        in_specs=list(ins),
        out_specs=tuple(VMEM for _ in outs),
        scratch_shapes=list(scratch),
        compiler_params=params,
        name=name,
    )


def dot(a, b, dims=((1,), (0,))):
    return lax.dot_general(a, b, (dims, ((), ())), preferred_element_type=F32)


def block(j):
    return slice(j * TILE, (j + 1) * TILE)


def iota(shape, axis):
    return lax.broadcasted_iota(jnp.int32, shape, axis)


def fetch(sources, targets, sems):
    copies = [
        pltpu.make_async_copy(source, target, sems.at[i])
        for i, (source, target) in enumerate(zip(sources, targets))
    ]
    for copy in copies:
        copy.start()
    return copies


def pick_body(send_far, feats_far, hist_far, out, rows, send, table, sems):
    cap, parts = send.shape
    nodes, cols = feats_far.shape
    targets = (send, table.at[:, :cols], table.at[:, cols:])
    for copy in fetch((send_far, feats_far, hist_far), targets, sems):
        copy.wait()
    for c in range(cap):
        hit = (iota((nodes, parts), 0) == send[c : c + 1, :]).astype(F32).astype(BF)
        got = dot(hit, table[...], ((0,), (0,)))
        rows[:, c, :] = got[:, :cols]
        rows[:, cap + c, :] = got[:, cols:]
    out[...] = rows[...].astype(BF)


def select_rows(types, weights, out):
    rows, width, _ = out.shape
    experts = weights.shape[1]
    span = TILE // rows
    shape = (rows * span, span * experts)
    at, source = iota(shape, 0), iota(shape, 1)
    kind = jnp.zeros(shape, jnp.int32)
    for j in range(rows):
        kind = jnp.where(at // span == j, types[j], kind)
    hit = (source == (at % span) * experts + kind).astype(F32).astype(BF)
    for i in range(width // span):
        part = weights[i * span : (i + 1) * span].reshape(span * experts, -1)
        got = dot(hit, part).astype(BF)
        for j in range(rows):
            out[j, i * span : (i + 1) * span, :] = got[j * span : (j + 1) * span]


def choose_body(types, w_one_far, w_two_far, one, two, w_one, w_two, sems):
    copies = fetch((w_one_far, w_two_far), (w_one, w_two), sems)
    copies[0].wait()
    select_rows(types, w_one, one)
    copies[1].wait()
    select_rows(types, w_two, two)


def ready_body(pick, local, halo_val, feats, base, wide):
    cap = wide.shape[2] // 2 // 32
    shape = (TILE, 2 * TILE)
    k, m = iota(shape, 0), iota(shape, 1)
    spot = (k // cap) * (2 * cap) + k % cap
    first = (m == spot).astype(F32).astype(BF)
    second = (m == spot + cap).astype(F32).astype(BF)
    for j in range(wide.shape[0]):
        base[block(j), :] = dot(local[block(j), :], feats[block(j), :])
        wide[pick[j], :TILE, :] = dot(halo_val[block(j), :], first).astype(BF)
        wide[pick[j], TILE:, :] = dot(halo_val[block(j), :], second).astype(BF)


def gather_body(pick, landed, wide, base, copies, part):
    for j in range(wide.shape[0]):
        both = dot(wide[pick[j]], landed[pick[j]])
        agg = (base[block(j), :] + both[:TILE]).astype(BF)
        part[block(j), :] = both[TILE:]
        for q in range(copies.shape[0]):
            copies[q, block(j), :] = agg


def forward(agg, weights, j):
    rows = jnp.concatenate([agg[q, block(j), :] for q in range(agg.shape[0])], axis=1)
    z = dot(rows, weights[j])
    sig = jax.nn.sigmoid(z)
    return z * sig, sig * (1.0 + z * (1.0 - sig))


def one_body(agg, weights, feats, local, part, hidden, near, slope, copies):
    for j in range(weights.shape[0]):
        act, bend = forward(agg, weights, j)
        slope[block(j), :] = bend
        h = (feats[block(j), :].astype(F32) + act).astype(BF)
        hidden[block(j), :] = h
        near[block(j), :] = h
        mixed = (dot(local[block(j), :], h) + part[block(j), :]).astype(BF)
        for q in range(copies.shape[0]):
            copies[q, block(j), :] = mixed


def two_body(agg, weights, h_one, grad, hidden, dz, back):
    cols = dz.shape[1]
    for j in range(weights.shape[0]):
        act, bend = forward(agg, weights, j)
        hidden[block(j), :] = (h_one[block(j), :].astype(F32) + act).astype(BF)
        d = (grad[block(j), :].astype(F32) * bend).astype(BF)
        dz[block(j), :] = d
        term = dot(d, weights[j], ((1,), (1,))).astype(BF)
        for q in range(back.shape[0]):
            back[q, block(j), :] = term[:, q * cols : (q + 1) * cols]


def write_grad(types, core, agg, dz, keep, send):
    reps, _, cols = agg.shape
    rows = types.shape[0]
    experts = keep.shape[1] // cols
    wide = []
    for e in range(experts):
        part = []
        for j in range(rows):
            part.append((dz[block(j), :].astype(F32) * (types[j] == e).astype(F32)).astype(BF))
        wide.append(jnp.concatenate(part, axis=0))
    wide = jnp.concatenate(wide, axis=1)
    for target, side in ((send, 1 - core[0]), (keep, core[0])):
        for i in range(reps // 2):
            got = dot(agg[side * (reps // 2) + i], wide, ((0,), (0,)))
            target[i * cols : (i + 1) * cols, :] = got.astype(target.dtype)


def back_body(types, core, parts, local, grad, slope, agg, keep, send, dz):
    for j in range(types.shape[0]):
        total = parts[0, block(j), :].astype(F32)
        for q in range(1, parts.shape[0]):
            total = total + parts[q, block(j), :].astype(F32)
        dh = grad[block(j), :].astype(F32) + dot(
            local[block(j), :], total.astype(BF), ((0,), (0,))
        )
        dz[block(j), :] = (dh * slope[block(j), :]).astype(BF)
    write_grad(types, core, agg, dz, keep, send)


def add_up(parts):
    total = parts[0].astype(F32)
    for i in range(1, parts.shape[0]):
        total = total + parts[i].astype(F32)
    return total


def first_body(parts, total):
    total[...] = add_up(parts).astype(BF)


def second_body(own, left, right, opposite, copies, table):
    rows, experts, cols = table.shape
    total = own[...].astype(F32) + opposite[...].astype(F32)
    total = total + (left[...].astype(F32) + right[...].astype(F32))
    for e in range(experts):
        table[:, e, :] = total[:, e * cols : (e + 1) * cols]
    laid = table[...].reshape(rows * experts, cols).astype(BF)
    for i in range(copies.shape[0]):
        copies[i] = laid


def widen_body(core, half, *refs):
    one, two = refs[-2:]
    step = pl.program_id(0)
    length = half.shape[1] // 2
    count = one.shape[0] // length
    for i in range(count):
        rows = half[step * count + i].astype(F32)
        one[i * length : (i + 1) * length, :] = rows[:length]
        two[i * length : (i + 1) * length, :] = rows[length:]


def widen(core, half, before=()):
    chunks, length, cols = half.shape
    steps = 2
    own = not before
    height = chunks // steps * (length // 2)
    target = pl.BlockSpec(
        (height, cols), lambda i, c: ((c[0] if own else 1 - c[0]) * steps + i, 0)
    )
    shape = jax.ShapeDtypeStruct((chunks * length, cols), F32)
    return pl.pallas_call(
        widen_body,
        grid_spec=pltpu.PrefetchScalarGridSpec(
            num_scalar_prefetch=1,
            grid=(steps,),
            in_specs=[VMEM] + [ANY] * len(before),
            out_specs=(target, target),
        ),
        out_shape=(shape, shape),
        input_output_aliases={} if own else {2: 0, 3: 1},
        compiler_params=PARAMS,
        name="widen_own" if own else "widen_other",
    )(core, half, *before)


def rings():
    def device(core, line, cross):
        y, z = (line, cross) if core == 0 else (cross, line)
        return (y * 8 + z) * 2 + core

    first = [
        [device(core, line, pair * PAIR + i) for i in range(PAIR) for line in range(8)]
        for core in range(2)
        for pair in range(8 // PAIR)
    ]
    second = [
        [device(core, line, pair * PAIR + i) for pair in range(8 // PAIR)]
        for core in range(2)
        for line in range(8)
        for i in range(PAIR)
    ]
    return first, second


def exchange(blocks, groups):
    return lax.all_to_all(
        blocks, "dom", split_axis=0, concat_axis=0, axis_index_groups=groups, tiled=True
    )


def across(blocks):
    return lax.all_to_all(blocks, "rep", split_axis=0, concat_axis=0, tiled=True)


def swap(rows):
    return lax.ppermute(rows, "dom", [(p, p ^ 1) for p in range(128)])


def shards(
    feats, hist_one, local_val, halo_val, halo_send, halo_tile, tile_type, w_one, w_two, grad_out
):
    nodes, cols = feats.shape
    rows = nodes // TILE
    width, experts, _ = w_one.shape
    parts, cap = halo_send.shape[1], halo_send.shape[2]
    pick, types = halo_tile[0], tile_type[0]
    core = lax.rem(lax.axis_index("dom"), 2).astype(jnp.int32).reshape(1)
    first, second = rings()
    flat = (nodes, cols)
    copied = (REPS, nodes, cols)

    (rows_out,) = call(
        pick_body,
        "pick",
        [FAR] * 3,
        [((parts, 2 * cap, cols), BF)],
        [
            pltpu.VMEM((parts, 2 * cap, cols), F32),
            pltpu.VMEM((cap, parts), jnp.int32),
            pltpu.VMEM((nodes, 2 * cols), BF),
            pltpu.SemaphoreType.DMA((3,)),
        ],
        FULL,
    )(jnp.swapaxes(halo_send[0], 0, 1), feats, hist_one)
    landed = lax.all_to_all(rows_out, "dom", split_axis=0, concat_axis=0, tiled=True)
    landed = landed.reshape(rows, 2 * TILE, cols)

    chosen = (rows, width, cols)
    pick_one, pick_two = call(
        choose_body,
        "choose",
        [SMEM] + [FAR] * 2,
        [(chosen, BF)] * 2,
        [pltpu.VMEM(w_one.shape, BF)] * 2 + [pltpu.SemaphoreType.DMA((2,))],
        FULL,
    )(types, w_one, w_two)
    base, wide = call(
        ready_body,
        "ready",
        [SMEM] + [VMEM] * 3,
        [(flat, F32), ((rows, 2 * TILE, 2 * TILE), BF)],
    )(pick, local_val, halo_val, feats)

    base, wide, pick_one, pick_two = lax.optimization_barrier((base, wide, pick_one, pick_two))
    copies, part = call(gather_body, "gather", [SMEM] + [VMEM] * 3, [(copied, BF), (flat, F32)])(
        pick, landed, wide, base
    )
    agg_one = across(copies)
    h_one, near, slope, copies = call(
        one_body, "one", [VMEM] * 5, [(flat, BF)] * 2 + [(flat, F32), (copied, BF)]
    )(agg_one, pick_one, feats, local_val, part)
    agg_two = across(copies)
    h_two, dz_two, back = call(
        two_body, "two", [VMEM] * 4, [(flat, BF), (flat, BF), (copied, BF)]
    )(agg_two, pick_two, near, grad_out)
    back = across(back)

    half = (width // 2, experts * cols)
    keep_two, send_two = call(
        write_grad, "grad_two", [SMEM] * 2 + [VMEM] * 2, [(half, F32), (half, BF)]
    )(types, core, agg_two, dz_two)
    keep_one, send_one = call(
        back_body,
        "back",
        [SMEM] * 2 + [VMEM] * 5,
        [(half, F32), (half, BF)],
        [pltpu.VMEM(flat, BF)],
    )(types, core, back, local_val, grad_out, slope, agg_one)
    pair_one = (keep_one + swap(send_one).astype(F32)).astype(BF)
    pair_two = (keep_two + swap(send_two).astype(F32)).astype(BF)

    split = (RING, width // 2 // RING, experts * cols)
    both = jnp.concatenate([pair_one.reshape(split), pair_two.reshape(split)], axis=1)
    both = exchange(both, first)
    few = both.shape[1]
    (own,) = call(first_body, "first_sum", [VMEM], [(both.shape[1:], BF)])(both)
    shifted = [
        lax.ppermute(
            own, "dom", [(g[i], g[(i + k) % CROSS]) for g in second for i in range(CROSS)]
        )
        for k in (2, 1, 3)
    ]
    opposite, left, right = shifted
    (both,) = call(
        second_body,
        "second_sum",
        [VMEM] * 4,
        [((RING, few * experts, cols), BF)],
        [pltpu.VMEM((few, experts, cols), F32)],
    )(own, left, right, opposite)
    same = exchange(both, first)
    grad_one, grad_two = widen(core, swap(same), widen(core, same))
    return h_two, h_one, grad_one.reshape(w_one.shape), grad_two.reshape(w_two.shape)


def solution(mesh):
    in_specs = (
        P("dom", "rep"),
        P("dom", "rep"),
        P("dom", None),
        P("dom", None),
        P("dom", None, None),
        P("dom", None),
        P("dom", None),
        P(None, None, "rep"),
        P(None, None, "rep"),
        P("dom", "rep"),
    )
    out_specs = (P("dom", "rep"), P("dom", "rep"), P(None, None, "rep"), P(None, None, "rep"))
    return jax.shard_map(shards, mesh=mesh, in_specs=in_specs, out_specs=out_specs, check_vma=False)
```

```python
import jax
import jax.numpy as jnp
from jax import lax
from jax.experimental import pallas as pl
from jax.experimental.pallas import tpu as pltpu
from jax.sharding import PartitionSpec as P

BF = jnp.bfloat16
F32 = jnp.float32
SMEM = pl.BlockSpec(memory_space=pltpu.SMEM)
VMEM = pl.BlockSpec(memory_space=pltpu.VMEM)
ANY = pl.BlockSpec(memory_space=pl.ANY)
FAR = pl.BlockSpec(memory_space=pltpu.HBM)
PARAMS = pltpu.CompilerParams(vmem_limit_bytes=40 << 20)
FULL = pltpu.CompilerParams(vmem_limit_bytes=60 << 20)
PAIR = 2
RING = 16
CROSS = 4
REPS = 4
TILE = 128


def call(body, name, ins, outs, scratch=(), params=PARAMS):
    return pl.pallas_call(
        body,
        out_shape=tuple(jax.ShapeDtypeStruct(shape, kind) for shape, kind in outs),
        in_specs=list(ins),
        out_specs=tuple(VMEM for _ in outs),
        scratch_shapes=list(scratch),
        compiler_params=params,
        name=name,
    )


def dot(a, b, dims=((1,), (0,))):
    return lax.dot_general(a, b, (dims, ((), ())), preferred_element_type=F32)


def block(j):
    return slice(j * TILE, (j + 1) * TILE)


def iota(shape, axis):
    return lax.broadcasted_iota(jnp.int32, shape, axis)


def fetch(sources, targets, sems):
    copies = [
        pltpu.make_async_copy(source, target, sems.at[i])
        for i, (source, target) in enumerate(zip(sources, targets))
    ]
    for copy in copies:
        copy.start()
    return copies


def pick_body(send_far, feats_far, hist_far, out, rows, send, table, sems):
    cap, parts = send.shape
    nodes, cols = feats_far.shape
    targets = (send, table.at[:, :cols], table.at[:, cols:])
    for copy in fetch((send_far, feats_far, hist_far), targets, sems):
        copy.wait()
    for c in range(cap):
        hit = (iota((nodes, parts), 0) == send[c : c + 1, :]).astype(F32).astype(BF)
        got = dot(hit, table[...], ((0,), (0,)))
        rows[:, c, :] = got[:, :cols]
        rows[:, cap + c, :] = got[:, cols:]
    out[...] = rows[...].astype(BF)


def select_rows(types, weights, out):
    rows, width, _ = out.shape
    experts = weights.shape[1]
    span = TILE // rows
    shape = (rows * span, span * experts)
    at, source = iota(shape, 0), iota(shape, 1)
    kind = jnp.zeros(shape, jnp.int32)
    for j in range(rows):
        kind = jnp.where(at // span == j, types[j], kind)
    hit = (source == (at % span) * experts + kind).astype(F32).astype(BF)
    for i in range(width // span):
        part = weights[i * span : (i + 1) * span].reshape(span * experts, -1)
        got = dot(hit, part).astype(BF)
        for j in range(rows):
            out[j, i * span : (i + 1) * span, :] = got[j * span : (j + 1) * span]


def choose_body(types, w_one_far, w_two_far, one, two, w_one, w_two, sems):
    copies = fetch((w_one_far, w_two_far), (w_one, w_two), sems)
    copies[0].wait()
    select_rows(types, w_one, one)
    copies[1].wait()
    select_rows(types, w_two, two)


def ready_body(pick, local, halo_val, feats, base, wide):
    cap = wide.shape[2] // 2 // 32
    shape = (TILE, 2 * TILE)
    k, m = iota(shape, 0), iota(shape, 1)
    spot = (k // cap) * (2 * cap) + k % cap
    first = (m == spot).astype(F32).astype(BF)
    second = (m == spot + cap).astype(F32).astype(BF)
    for j in range(wide.shape[0]):
        base[block(j), :] = dot(local[block(j), :], feats[block(j), :])
        wide[pick[j], :TILE, :] = dot(halo_val[block(j), :], first).astype(BF)
        wide[pick[j], TILE:, :] = dot(halo_val[block(j), :], second).astype(BF)


def gather_body(pick, landed, wide, base, copies, part):
    for j in range(wide.shape[0]):
        both = dot(wide[pick[j]], landed[pick[j]])
        agg = (base[block(j), :] + both[:TILE]).astype(BF)
        part[block(j), :] = both[TILE:]
        for q in range(copies.shape[0]):
            copies[q, block(j), :] = agg


def forward(agg, weights, j):
    rows = jnp.concatenate([agg[q, block(j), :] for q in range(agg.shape[0])], axis=1)
    z = dot(rows, weights[j])
    sig = jax.nn.sigmoid(z)
    return z * sig, sig * (1.0 + z * (1.0 - sig))


def one_body(agg, weights, feats, local, part, hidden, near, slope, copies):
    for j in range(weights.shape[0]):
        act, bend = forward(agg, weights, j)
        slope[block(j), :] = bend
        h = (feats[block(j), :].astype(F32) + act).astype(BF)
        hidden[block(j), :] = h
        near[block(j), :] = h
        mixed = (dot(local[block(j), :], h) + part[block(j), :]).astype(BF)
        for q in range(copies.shape[0]):
            copies[q, block(j), :] = mixed


def two_body(agg, weights, h_one, grad, hidden, dz, back):
    cols = dz.shape[1]
    for j in range(weights.shape[0]):
        act, bend = forward(agg, weights, j)
        hidden[block(j), :] = (h_one[block(j), :].astype(F32) + act).astype(BF)
        d = (grad[block(j), :].astype(F32) * bend).astype(BF)
        dz[block(j), :] = d
        term = dot(d, weights[j], ((1,), (1,))).astype(BF)
        for q in range(back.shape[0]):
            back[q, block(j), :] = term[:, q * cols : (q + 1) * cols]


def write_grad(types, core, agg, dz, keep, send):
    reps, _, cols = agg.shape
    rows = types.shape[0]
    experts = keep.shape[1] // cols
    wide = []
    for e in range(experts):
        part = []
        for j in range(rows):
            part.append((dz[block(j), :].astype(F32) * (types[j] == e).astype(F32)).astype(BF))
        wide.append(jnp.concatenate(part, axis=0))
    wide = jnp.concatenate(wide, axis=1)
    for target, side in ((send, 1 - core[0]), (keep, core[0])):
        for i in range(reps // 2):
            got = dot(agg[side * (reps // 2) + i], wide, ((0,), (0,)))
            target[i * cols : (i + 1) * cols, :] = got.astype(target.dtype)


def back_body(types, core, parts, local, grad, slope, agg, keep, send, dz):
    for j in range(types.shape[0]):
        total = parts[0, block(j), :].astype(F32)
        for q in range(1, parts.shape[0]):
            total = total + parts[q, block(j), :].astype(F32)
        dh = grad[block(j), :].astype(F32) + dot(
            local[block(j), :], total.astype(BF), ((0,), (0,))
        )
        dz[block(j), :] = (dh * slope[block(j), :]).astype(BF)
    write_grad(types, core, agg, dz, keep, send)


def add_up(parts):
    total = parts[0].astype(F32)
    for i in range(1, parts.shape[0]):
        total = total + parts[i].astype(F32)
    return total


def first_body(parts, copies):
    total = add_up(parts).astype(BF)
    for i in range(copies.shape[0]):
        copies[i] = total


def second_body(parts, copies, table):
    rows, experts, cols = table.shape
    total = add_up(parts)
    for e in range(experts):
        table[:, e, :] = total[:, e * cols : (e + 1) * cols]
    laid = table[...].reshape(rows * experts, cols).astype(BF)
    for i in range(copies.shape[0]):
        copies[i] = laid


def widen_body(core, half, *refs):
    one, two = refs[-2:]
    step = pl.program_id(0)
    length = half.shape[1] // 2
    count = one.shape[0] // length
    for i in range(count):
        rows = half[step * count + i].astype(F32)
        one[i * length : (i + 1) * length, :] = rows[:length]
        two[i * length : (i + 1) * length, :] = rows[length:]


def widen(core, half, before=()):
    chunks, length, cols = half.shape
    steps = 2
    own = not before
    height = chunks // steps * (length // 2)
    target = pl.BlockSpec(
        (height, cols), lambda i, c: ((c[0] if own else 1 - c[0]) * steps + i, 0)
    )
    shape = jax.ShapeDtypeStruct((chunks * length, cols), F32)
    return pl.pallas_call(
        widen_body,
        grid_spec=pltpu.PrefetchScalarGridSpec(
            num_scalar_prefetch=1,
            grid=(steps,),
            in_specs=[VMEM] + [ANY] * len(before),
            out_specs=(target, target),
        ),
        out_shape=(shape, shape),
        input_output_aliases={} if own else {2: 0, 3: 1},
        compiler_params=PARAMS,
        name="widen_own" if own else "widen_other",
    )(core, half, *before)


def rings():
    def device(core, line, cross):
        y, z = (line, cross) if core == 0 else (cross, line)
        return (y * 8 + z) * 2 + core

    first = [
        [device(core, line, pair * PAIR + i) for i in range(PAIR) for line in range(8)]
        for core in range(2)
        for pair in range(8 // PAIR)
    ]
    second = [
        [device(core, line, pair * PAIR + i) for pair in range(8 // PAIR)]
        for core in range(2)
        for line in range(8)
        for i in range(PAIR)
    ]
    return first, second


def exchange(blocks, groups):
    return lax.all_to_all(
        blocks, "dom", split_axis=0, concat_axis=0, axis_index_groups=groups, tiled=True
    )


def across(blocks):
    return lax.all_to_all(blocks, "rep", split_axis=0, concat_axis=0, tiled=True)


def swap(rows):
    return lax.ppermute(rows, "dom", [(p, p ^ 1) for p in range(128)])


def shards(
    feats, hist_one, local_val, halo_val, halo_send, halo_tile, tile_type, w_one, w_two, grad_out
):
    nodes, cols = feats.shape
    rows = nodes // TILE
    width, experts, _ = w_one.shape
    parts, cap = halo_send.shape[1], halo_send.shape[2]
    pick, types = halo_tile[0], tile_type[0]
    core = lax.rem(lax.axis_index("dom"), 2).astype(jnp.int32).reshape(1)
    first, second = rings()
    flat = (nodes, cols)
    copied = (REPS, nodes, cols)

    (rows_out,) = call(
        pick_body,
        "pick",
        [FAR] * 3,
        [((parts, 2 * cap, cols), BF)],
        [
            pltpu.VMEM((parts, 2 * cap, cols), F32),
            pltpu.VMEM((cap, parts), jnp.int32),
            pltpu.VMEM((nodes, 2 * cols), BF),
            pltpu.SemaphoreType.DMA((3,)),
        ],
        FULL,
    )(jnp.swapaxes(halo_send[0], 0, 1), feats, hist_one)
    landed = lax.all_to_all(rows_out, "dom", split_axis=0, concat_axis=0, tiled=True)
    landed = landed.reshape(rows, 2 * TILE, cols)

    chosen = (rows, width, cols)
    pick_one, pick_two = call(
        choose_body,
        "choose",
        [SMEM] + [FAR] * 2,
        [(chosen, BF)] * 2,
        [pltpu.VMEM(w_one.shape, BF)] * 2 + [pltpu.SemaphoreType.DMA((2,))],
        FULL,
    )(types, w_one, w_two)
    base, wide = call(
        ready_body,
        "ready",
        [SMEM] + [VMEM] * 3,
        [(flat, F32), ((rows, 2 * TILE, 2 * TILE), BF)],
    )(pick, local_val, halo_val, feats)

    base, wide, pick_one, pick_two = lax.optimization_barrier((base, wide, pick_one, pick_two))
    copies, part = call(gather_body, "gather", [SMEM] + [VMEM] * 3, [(copied, BF), (flat, F32)])(
        pick, landed, wide, base
    )
    agg_one = across(copies)
    h_one, near, slope, copies = call(
        one_body, "one", [VMEM] * 5, [(flat, BF)] * 2 + [(flat, F32), (copied, BF)]
    )(agg_one, pick_one, feats, local_val, part)
    agg_two = across(copies)
    h_two, dz_two, back = call(
        two_body, "two", [VMEM] * 4, [(flat, BF), (flat, BF), (copied, BF)]
    )(agg_two, pick_two, near, grad_out)
    back = across(back)

    half = (width // 2, experts * cols)
    keep_two, send_two = call(
        write_grad, "grad_two", [SMEM] * 2 + [VMEM] * 2, [(half, F32), (half, BF)]
    )(types, core, agg_two, dz_two)
    keep_one, send_one = call(
        back_body,
        "back",
        [SMEM] * 2 + [VMEM] * 5,
        [(half, F32), (half, BF)],
        [pltpu.VMEM(flat, BF)],
    )(types, core, back, local_val, grad_out, slope, agg_one)
    pair_one = (keep_one + swap(send_one).astype(F32)).astype(BF)
    pair_two = (keep_two + swap(send_two).astype(F32)).astype(BF)

    split = (RING, width // 2 // RING, experts * cols)
    both = jnp.concatenate([pair_one.reshape(split), pair_two.reshape(split)], axis=1)
    both = exchange(both, first)
    few = both.shape[1]
    (both,) = call(first_body, "first_sum", [VMEM], [((CROSS,) + both.shape[1:], BF)])(both)
    both = exchange(both, second)
    (both,) = call(
        second_body,
        "second_sum",
        [VMEM],
        [((RING, few * experts, cols), BF)],
        [pltpu.VMEM((few, experts, cols), F32)],
    )(both)
    same = exchange(both, first)
    grad_one, grad_two = widen(core, swap(same), widen(core, same))
    return h_two, h_one, grad_one.reshape(w_one.shape), grad_two.reshape(w_two.shape)


def solution(mesh):
    in_specs = (
        P("dom", "rep"),
        P("dom", "rep"),
        P("dom", None),
        P("dom", None),
        P("dom", None, None),
        P("dom", None),
        P("dom", None),
        P(None, None, "rep"),
        P(None, None, "rep"),
        P("dom", "rep"),
    )
    out_specs = (P("dom", "rep"), P("dom", "rep"), P(None, None, "rep"), P(None, None, "rep"))
    return jax.shard_map(shards, mesh=mesh, in_specs=in_specs, out_specs=out_specs, check_vma=False)
```

```python
import jax
import jax.numpy as jnp
from jax import lax
from jax.experimental import pallas as pl
from jax.experimental.pallas import tpu as pltpu
from jax.sharding import PartitionSpec as P

BF = jnp.bfloat16
F32 = jnp.float32
SMEM = pl.BlockSpec(memory_space=pltpu.SMEM)
VMEM = pl.BlockSpec(memory_space=pltpu.VMEM)
ANY = pl.BlockSpec(memory_space=pl.ANY)
FAR = pl.BlockSpec(memory_space=pltpu.HBM)
PARAMS = pltpu.CompilerParams(vmem_limit_bytes=40 << 20)
FULL = pltpu.CompilerParams(vmem_limit_bytes=60 << 20)
PAIR = 2
RING = 16
CROSS = 4
REPS = 4
TILE = 128


def call(body, name, ins, outs, scratch=(), params=PARAMS):
    return pl.pallas_call(
        body,
        out_shape=tuple(jax.ShapeDtypeStruct(shape, kind) for shape, kind in outs),
        in_specs=list(ins),
        out_specs=tuple(VMEM for _ in outs),
        scratch_shapes=list(scratch),
        compiler_params=params,
        name=name,
    )


def dot(a, b, dims=((1,), (0,))):
    return lax.dot_general(a, b, (dims, ((), ())), preferred_element_type=F32)


def block(j):
    return slice(j * TILE, (j + 1) * TILE)


def iota(shape, axis):
    return lax.broadcasted_iota(jnp.int32, shape, axis)


def fetch(sources, targets, sems):
    copies = [
        pltpu.make_async_copy(source, target, sems.at[i])
        for i, (source, target) in enumerate(zip(sources, targets))
    ]
    for copy in copies:
        copy.start()
    return copies


def pick_body(core, send_far, feats_far, hist_far, out, rows, send, table, sems):
    cap, parts = send.shape
    nodes, cols = feats_far.shape
    chips = parts // 2
    copies = fetch(
        (send_far, feats_far, hist_far), (send, table.at[:, :cols], table.at[:, cols:]), sems
    )
    at, source = iota((parts, parts), 0), iota((parts, parts), 1)
    side = jnp.where(at < chips, core[0], 1 - core[0])
    order = (source == (at % chips) * 2 + side).astype(F32).astype(BF)
    for copy in copies:
        copy.wait()
    for c in range(cap):
        hit = (iota((nodes, parts), 0) == send[c : c + 1, :]).astype(F32).astype(BF)
        got = dot(order, dot(hit, table[...], ((0,), (0,))).astype(BF))
        for k in range(2):
            half = got[k * chips : (k + 1) * chips]
            rows[:, 2 * k * cap + c, :] = half[:, :cols]
            rows[:, (2 * k + 1) * cap + c, :] = half[:, cols:]
    out[...] = rows[...].astype(BF)


def select_rows(types, weights, out):
    rows, width, _ = out.shape
    experts = weights.shape[1]
    span = TILE // rows
    shape = (rows * span, span * experts)
    at, source = iota(shape, 0), iota(shape, 1)
    kind = jnp.zeros(shape, jnp.int32)
    for j in range(rows):
        kind = jnp.where(at // span == j, types[j], kind)
    hit = (source == (at % span) * experts + kind).astype(F32).astype(BF)
    for i in range(width // span):
        part = weights[i * span : (i + 1) * span].reshape(span * experts, -1)
        got = dot(hit, part).astype(BF)
        for j in range(rows):
            out[j, i * span : (i + 1) * span, :] = got[j * span : (j + 1) * span]


def choose_body(types, far, out, near, sems):
    (copy,) = fetch((far,), (near,), sems)
    copy.wait()
    select_rows(types, near, out)


def ready_body(core, pick, local, halo_val, feats, base, wide):
    cap = wide.shape[2] // 2 // 32
    shape = (TILE, 2 * TILE)
    k, m = iota(shape, 0), iota(shape, 1)
    half = jnp.where((k // cap) % 2 == core[0], 0, TILE)
    spot = half + (k // cap // 2) * (2 * cap) + k % cap
    first = (m == spot).astype(F32).astype(BF)
    second = (m == spot + cap).astype(F32).astype(BF)
    for j in range(wide.shape[0]):
        base[block(j), :] = dot(local[block(j), :], feats[block(j), :])
        wide[pick[j], :TILE, :] = dot(halo_val[block(j), :], first).astype(BF)
        wide[pick[j], TILE:, :] = dot(halo_val[block(j), :], second).astype(BF)


def gather_body(pick, landed, other, wide, base, copies, part):
    for j in range(wide.shape[0]):
        halo = jnp.concatenate([landed[pick[j]], other[pick[j]]], axis=0)
        both = dot(wide[pick[j]], halo)
        agg = (base[block(j), :] + both[:TILE]).astype(BF)
        part[block(j), :] = both[TILE:]
        for q in range(copies.shape[0]):
            copies[q, block(j), :] = agg


def forward(agg, weights, j):
    rows = jnp.concatenate([agg[q, block(j), :] for q in range(agg.shape[0])], axis=1)
    z = dot(rows, weights[j])
    sig = jax.nn.sigmoid(z)
    return z * sig, sig * (1.0 + z * (1.0 - sig))


def one_body(agg, weights, feats, local, part, hidden, near, slope, copies):
    for j in range(weights.shape[0]):
        act, bend = forward(agg, weights, j)
        slope[block(j), :] = bend
        h = (feats[block(j), :].astype(F32) + act).astype(BF)
        hidden[block(j), :] = h
        near[block(j), :] = h
        mixed = (dot(local[block(j), :], h) + part[block(j), :]).astype(BF)
        for q in range(copies.shape[0]):
            copies[q, block(j), :] = mixed


def two_body(agg, weights, h_one, grad, hidden, dz, back):
    cols = dz.shape[1]
    for j in range(weights.shape[0]):
        act, bend = forward(agg, weights, j)
        hidden[block(j), :] = (h_one[block(j), :].astype(F32) + act).astype(BF)
        d = (grad[block(j), :].astype(F32) * bend).astype(BF)
        dz[block(j), :] = d
        term = dot(d, weights[j], ((1,), (1,))).astype(BF)
        for q in range(back.shape[0]):
            back[q, block(j), :] = term[:, q * cols : (q + 1) * cols]


def write_grad(types, core, agg, dz, keep, send):
    reps, _, cols = agg.shape
    rows = types.shape[0]
    experts = keep.shape[1] // cols
    wide = []
    for e in range(experts):
        part = []
        for j in range(rows):
            part.append((dz[block(j), :].astype(F32) * (types[j] == e).astype(F32)).astype(BF))
        wide.append(jnp.concatenate(part, axis=0))
    wide = jnp.concatenate(wide, axis=1)
    for target, side in ((send, 1 - core[0]), (keep, core[0])):
        for i in range(reps // 2):
            got = dot(agg[side * (reps // 2) + i], wide, ((0,), (0,)))
            target[i * cols : (i + 1) * cols, :] = got.astype(target.dtype)


def back_body(types, core, parts, local, grad, slope, agg, keep, send, dz):
    for j in range(types.shape[0]):
        total = parts[0, block(j), :].astype(F32)
        for q in range(1, parts.shape[0]):
            total = total + parts[q, block(j), :].astype(F32)
        dh = grad[block(j), :].astype(F32) + dot(
            local[block(j), :], total.astype(BF), ((0,), (0,))
        )
        dz[block(j), :] = (dh * slope[block(j), :]).astype(BF)
    write_grad(types, core, agg, dz, keep, send)


def add_up(parts):
    total = parts[0].astype(F32)
    for i in range(1, parts.shape[0]):
        total = total + parts[i].astype(F32)
    return total


def first_body(parts, copies):
    total = add_up(parts).astype(BF)
    for i in range(copies.shape[0]):
        copies[i] = total


def second_body(parts, copies, table):
    rows, experts, cols = table.shape
    total = add_up(parts)
    for e in range(experts):
        table[:, e, :] = total[:, e * cols : (e + 1) * cols]
    laid = table[...].reshape(rows * experts, cols).astype(BF)
    for i in range(copies.shape[0]):
        copies[i] = laid


def widen_body(core, half, *refs):
    one, two = refs[-2:]
    step = pl.program_id(0)
    length = half.shape[1] // 2
    count = one.shape[0] // length
    for i in range(count):
        rows = half[step * count + i].astype(F32)
        one[i * length : (i + 1) * length, :] = rows[:length]
        two[i * length : (i + 1) * length, :] = rows[length:]


def widen(core, half, before=()):
    chunks, length, cols = half.shape
    steps = 2
    own = not before
    height = chunks // steps * (length // 2)
    target = pl.BlockSpec(
        (height, cols), lambda i, c: ((c[0] if own else 1 - c[0]) * steps + i, 0)
    )
    shape = jax.ShapeDtypeStruct((chunks * length, cols), F32)
    return pl.pallas_call(
        widen_body,
        grid_spec=pltpu.PrefetchScalarGridSpec(
            num_scalar_prefetch=1,
            grid=(steps,),
            in_specs=[VMEM] + [ANY] * len(before),
            out_specs=(target, target),
        ),
        out_shape=(shape, shape),
        input_output_aliases={} if own else {2: 0, 3: 1},
        compiler_params=PARAMS,
        name="widen_own" if own else "widen_other",
    )(core, half, *before)


def rings():
    def device(core, line, cross):
        y, z = (line, cross) if core == 0 else (cross, line)
        return (y * 8 + z) * 2 + core

    first = [
        [device(core, line, pair * PAIR + i) for i in range(PAIR) for line in range(8)]
        for core in range(2)
        for pair in range(8 // PAIR)
    ]
    second = [
        [device(core, line, pair * PAIR + i) for pair in range(8 // PAIR)]
        for core in range(2)
        for line in range(8)
        for i in range(PAIR)
    ]
    return first, second


def exchange(blocks, groups):
    return lax.all_to_all(
        blocks, "dom", split_axis=0, concat_axis=0, axis_index_groups=groups, tiled=True
    )


def across(blocks):
    return lax.all_to_all(blocks, "rep", split_axis=0, concat_axis=0, tiled=True)


def swap(rows):
    return lax.ppermute(rows, "dom", [(p, p ^ 1) for p in range(128)])


def shards(
    feats, hist_one, local_val, halo_val, halo_send, halo_tile, tile_type, w_one, w_two, grad_out
):
    nodes, cols = feats.shape
    rows = nodes // TILE
    width, experts, _ = w_one.shape
    parts, cap = halo_send.shape[1], halo_send.shape[2]
    pick, types = halo_tile[0], tile_type[0]
    core = lax.rem(lax.axis_index("dom"), 2).astype(jnp.int32).reshape(1)
    first, second = rings()
    flat = (nodes, cols)
    copied = (REPS, nodes, cols)

    (rows_out,) = call(
        pick_body,
        "pick",
        [SMEM] + [FAR] * 3,
        [((parts // 2, 4 * cap, cols), BF)],
        [
            pltpu.VMEM((parts // 2, 4 * cap, cols), F32),
            pltpu.VMEM((cap, parts), jnp.int32),
            pltpu.VMEM((nodes, 2 * cols), BF),
            pltpu.SemaphoreType.DMA((3,)),
        ],
        FULL,
    )(core, jnp.swapaxes(halo_send[0], 0, 1), feats, hist_one)
    alike = [[2 * chip + c for chip in range(parts // 2)] for c in range(2)]
    landed = exchange(rows_out, alike)
    flat_halo = (rows, TILE, cols)
    chosen = (rows, width, cols)
    choose = call(
        choose_body,
        "choose",
        [SMEM, FAR],
        [(chosen, BF)],
        [pltpu.VMEM(w_one.shape, BF), pltpu.SemaphoreType.DMA((1,))],
        FULL,
    )
    (pick_one,) = choose(types, w_one)
    (pick_two,) = choose(types, w_two)
    base, wide = call(
        ready_body,
        "ready",
        [SMEM] * 2 + [VMEM] * 3,
        [(flat, F32), ((rows, 2 * TILE, 2 * TILE), BF)],
    )(core, pick, local_val, halo_val, feats)

    landed, base, wide, pick_one = lax.optimization_barrier((landed, base, wide, pick_one))
    other = swap(landed[:, 2 * cap :]).reshape(flat_halo)
    landed = landed[:, : 2 * cap].reshape(flat_halo)
    base, pick_two = lax.optimization_barrier((base, pick_two))
    copies, part = call(gather_body, "gather", [SMEM] + [VMEM] * 4, [(copied, BF), (flat, F32)])(
        pick, landed, other, wide, base
    )
    agg_one = across(copies)
    h_one, near, slope, copies = call(
        one_body, "one", [VMEM] * 5, [(flat, BF)] * 2 + [(flat, F32), (copied, BF)]
    )(agg_one, pick_one, feats, local_val, part)
    agg_two = across(copies)
    h_two, dz_two, back = call(
        two_body, "two", [VMEM] * 4, [(flat, BF), (flat, BF), (copied, BF)]
    )(agg_two, pick_two, near, grad_out)
    back = across(back)

    half = (width // 2, experts * cols)
    keep_two, send_two = call(
        write_grad, "grad_two", [SMEM] * 2 + [VMEM] * 2, [(half, F32), (half, BF)]
    )(types, core, agg_two, dz_two)
    keep_one, send_one = call(
        back_body,
        "back",
        [SMEM] * 2 + [VMEM] * 5,
        [(half, F32), (half, BF)],
        [pltpu.VMEM(flat, BF)],
    )(types, core, back, local_val, grad_out, slope, agg_one)
    pair_one = (keep_one + swap(send_one).astype(F32)).astype(BF)
    pair_two = (keep_two + swap(send_two).astype(F32)).astype(BF)

    split = (RING, width // 2 // RING, experts * cols)
    both = jnp.concatenate([pair_one.reshape(split), pair_two.reshape(split)], axis=1)
    both = exchange(both, first)
    few = both.shape[1]
    (both,) = call(first_body, "first_sum", [VMEM], [((CROSS,) + both.shape[1:], BF)])(both)
    both = exchange(both, second)
    (both,) = call(
        second_body,
        "second_sum",
        [VMEM],
        [((RING, few * experts, cols), BF)],
        [pltpu.VMEM((few, experts, cols), F32)],
    )(both)
    same = exchange(both, first)
    grad_one, grad_two = widen(core, swap(same), widen(core, same))
    return h_two, h_one, grad_one.reshape(w_one.shape), grad_two.reshape(w_two.shape)


def solution(mesh):
    in_specs = (
        P("dom", "rep"),
        P("dom", "rep"),
        P("dom", None),
        P("dom", None),
        P("dom", None, None),
        P("dom", None),
        P("dom", None),
        P(None, None, "rep"),
        P(None, None, "rep"),
        P("dom", "rep"),
    )
    out_specs = (P("dom", "rep"), P("dom", "rep"), P(None, None, "rep"), P(None, None, "rep"))
    return jax.shard_map(shards, mesh=mesh, in_specs=in_specs, out_specs=out_specs, check_vma=False)
```

```python
import functools

import jax
import jax.numpy as jnp
from jax import lax
from jax.experimental import pallas as pl
from jax.experimental.pallas import tpu as pltpu
from jax.sharding import PartitionSpec as P

BF = jnp.bfloat16
F32 = jnp.float32
SMEM = pl.BlockSpec(memory_space=pltpu.SMEM)
VMEM = pl.BlockSpec(memory_space=pltpu.VMEM)
ANY = pl.BlockSpec(memory_space=pl.ANY)
FAR = pl.BlockSpec(memory_space=pltpu.HBM)
PARAMS = pltpu.CompilerParams(vmem_limit_bytes=40 << 20)
FULL = pltpu.CompilerParams(vmem_limit_bytes=60 << 20)
PAIR = 2
RING = 16
CROSS = 4
REPS = 4
TILE = 128


def call(body, name, ins, outs, scratch=(), params=PARAMS, places=None):
    return pl.pallas_call(
        body,
        out_shape=tuple(jax.ShapeDtypeStruct(shape, kind) for shape, kind in outs),
        in_specs=list(ins),
        out_specs=places or tuple(VMEM for _ in outs),
        scratch_shapes=list(scratch),
        compiler_params=params,
        name=name,
    )


def dot(a, b, dims=((1,), (0,))):
    return lax.dot_general(a, b, (dims, ((), ())), preferred_element_type=F32)


def block(j):
    return slice(j * TILE, (j + 1) * TILE)


def iota(shape, axis):
    return lax.broadcasted_iota(jnp.int32, shape, axis)


def fetch(sources, targets, sems):
    copies = [
        pltpu.make_async_copy(source, target, sems.at[i])
        for i, (source, target) in enumerate(zip(sources, targets))
    ]
    for copy in copies:
        copy.start()
    return copies


def pick_body(send_far, feats_far, hist_far, out, rows, send, table, sems):
    cap, parts = send.shape
    nodes, cols = feats_far.shape
    targets = (send, table.at[:, :cols], table.at[:, cols:])
    copies = fetch((send_far, feats_far, hist_far), targets, sems)
    copies[0].wait()
    spot = iota((nodes, parts), 0)
    hits = [(spot == send[c : c + 1, :]).astype(F32).astype(BF) for c in range(cap)]
    for copy in copies[1:]:
        copy.wait()
    for c, hit in enumerate(hits):
        got = dot(hit, table[...], ((0,), (0,)))
        rows[:, c, :] = got[:, :cols]
        rows[:, cap + c, :] = got[:, cols:]
    out[...] = rows[...].astype(BF)


def select_rows(types, weights, out):
    rows, width, _ = out.shape
    experts = weights.shape[1]
    span = TILE // rows
    shape = (rows * span, span * experts)
    at, source = iota(shape, 0), iota(shape, 1)
    kind = jnp.zeros(shape, jnp.int32)
    for j in range(rows):
        kind = jnp.where(at // span == j, types[j], kind)
    hit = (source == (at % span) * experts + kind).astype(F32).astype(BF)
    for i in range(width // span):
        part = weights[i * span : (i + 1) * span].reshape(span * experts, -1)
        got = dot(hit, part).astype(BF)
        for j in range(rows):
            out[j, i * span : (i + 1) * span, :] = got[j * span : (j + 1) * span]


def choose_body(types, w_one_far, w_two_far, one, two, w_one, w_two, sems):
    copies = fetch((w_one_far, w_two_far), (w_one, w_two), sems)
    copies[0].wait()
    select_rows(types, w_one, one)
    copies[1].wait()
    select_rows(types, w_two, two)


def ready_body(pick, local, halo_val, feats, base, wide):
    cap = wide.shape[2] // 2 // 32
    shape = (TILE, 2 * TILE)
    k, m = iota(shape, 0), iota(shape, 1)
    spot = (k // cap) * (2 * cap) + k % cap
    first = (m == spot).astype(F32).astype(BF)
    second = (m == spot + cap).astype(F32).astype(BF)
    for j in range(wide.shape[0]):
        base[block(j), :] = dot(local[block(j), :], feats[block(j), :])
        wide[pick[j], :TILE, :] = dot(halo_val[block(j), :], first).astype(BF)
        wide[pick[j], TILE:, :] = dot(halo_val[block(j), :], second).astype(BF)


def gather_body(pick, landed, wide, base, copies, part):
    for j in range(wide.shape[0]):
        both = dot(wide[pick[j]], landed[pick[j]])
        agg = (base[block(j), :] + both[:TILE]).astype(BF)
        part[block(j), :] = both[TILE:]
        for q in range(copies.shape[0]):
            copies[q, block(j), :] = agg


def forward(agg, weights, j):
    rows = jnp.concatenate([agg[q, block(j), :] for q in range(agg.shape[0])], axis=1)
    z = dot(rows, weights[j])
    sig = jax.nn.sigmoid(z)
    return z * sig, sig * (1.0 + z * (1.0 - sig))


def one_body(agg, weights, feats, local, part, hidden, near, slope, copies):
    for j in range(weights.shape[0]):
        act, bend = forward(agg, weights, j)
        slope[block(j), :] = bend
        h = (feats[block(j), :].astype(F32) + act).astype(BF)
        hidden[block(j), :] = h
        near[block(j), :] = h
        mixed = (dot(local[block(j), :], h) + part[block(j), :]).astype(BF)
        for q in range(copies.shape[0]):
            copies[q, block(j), :] = mixed


def two_body(agg, weights, h_one, grad, hidden, dz, back, near, sems):
    cols = dz.shape[1]
    copies = []
    for j in range(weights.shape[0]):
        act, bend = forward(agg, weights, j)
        hidden[block(j), :] = (h_one[block(j), :].astype(F32) + act).astype(BF)
        d = (grad[block(j), :].astype(F32) * bend).astype(BF)
        dz[block(j), :] = d
        term = dot(d, weights[j], ((1,), (1,))).astype(BF)
        for q in range(back.shape[0]):
            near[q, block(j), :] = term[:, q * cols : (q + 1) * cols]
        spot = (slice(None), pl.ds(j * TILE, TILE))
        copies.append(pltpu.make_async_copy(near.at[spot], back.at[spot], sems.at[j]))
        copies[-1].start()
    for copy in copies:
        copy.wait()


def grad_rows(types, side, agg, dz, target):
    reps, _, cols = agg.shape
    rows = types.shape[0]
    experts = target.shape[1] // cols
    wide = []
    for e in range(experts):
        part = []
        for j in range(rows):
            part.append((dz[block(j), :].astype(F32) * (types[j] == e).astype(F32)).astype(BF))
        wide.append(jnp.concatenate(part, axis=0))
    wide = jnp.concatenate(wide, axis=1)
    for i in range(reps // 2):
        got = dot(agg[side * (reps // 2) + i], wide, ((0,), (0,)))
        target[i * cols : (i + 1) * cols, :] = got.astype(target.dtype)


def both_body(types, core, agg, dz, keep, send):
    grad_rows(types, 1 - core[0], agg, dz, send)
    grad_rows(types, core[0], agg, dz, keep)


def keep_body(types, core, agg, dz, keep):
    grad_rows(types, core[0], agg, dz, keep)


def back_body(types, core, parts, local, grad, slope, agg, dz, send):
    for j in range(types.shape[0]):
        total = parts[0, block(j), :].astype(F32)
        for q in range(1, parts.shape[0]):
            total = total + parts[q, block(j), :].astype(F32)
        dh = grad[block(j), :].astype(F32) + dot(
            local[block(j), :], total.astype(BF), ((0,), (0,))
        )
        dz[block(j), :] = (dh * slope[block(j), :]).astype(BF)
    grad_rows(types, 1 - core[0], agg, dz, send)


def add_up(parts):
    total = parts[0].astype(F32)
    for i in range(1, parts.shape[0]):
        total = total + parts[i].astype(F32)
    return total


def first_body(parts, copies):
    total = add_up(parts).astype(BF)
    for i in range(copies.shape[0]):
        copies[i] = total


def second_body(parts, copies, table):
    rows, experts, cols = table.shape
    total = add_up(parts)
    for e in range(experts):
        table[:, e, :] = total[:, e * cols : (e + 1) * cols]
    laid = table[...].reshape(rows * experts, cols).astype(BF)
    for i in range(copies.shape[0]):
        copies[i] = laid


def widen_body(own, core, half, *refs):
    one, two, wide, sems = refs[-4:]
    chunks, length, _ = half.shape
    length = length // 2
    side = core[0] if own else 1 - core[0]
    start = pl.multiple_of(side * (chunks * length), chunks * length)
    count = 2
    copies = []
    for i in range(chunks // count):
        for k in range(count):
            at = i * count + k
            rows = half[at].astype(F32)
            wide[0, at * length : (at + 1) * length, :] = rows[:length]
            wide[1, at * length : (at + 1) * length, :] = rows[length:]
        span = count * length
        for layer, target in enumerate((one, two)):
            copies.append(
                pltpu.make_async_copy(
                    wide.at[layer, pl.ds(i * span, span)],
                    target.at[pl.ds(start + i * span, span)],
                    sems.at[2 * i + layer],
                )
            )
            copies[-1].start()
    for copy in copies:
        copy.wait()


def widen(core, half, before=()):
    chunks, length, cols = half.shape
    own = not before
    shape = jax.ShapeDtypeStruct((chunks * length, cols), F32)
    return pl.pallas_call(
        functools.partial(widen_body, own),
        in_specs=[SMEM, VMEM] + [ANY] * len(before),
        out_specs=(ANY, ANY),
        out_shape=(shape, shape),
        scratch_shapes=[
            pltpu.VMEM((2, chunks * length // 2, cols), F32),
            pltpu.SemaphoreType.DMA((chunks,)),
        ],
        input_output_aliases={} if own else {2: 0, 3: 1},
        compiler_params=PARAMS,
        name="widen_own" if own else "widen_other",
    )(core, half, *before)


def rings():
    def device(core, line, cross):
        y, z = (line, cross) if core == 0 else (cross, line)
        return (y * 8 + z) * 2 + core

    first = [
        [device(core, line, pair * PAIR + i) for i in range(PAIR) for line in range(8)]
        for core in range(2)
        for pair in range(8 // PAIR)
    ]
    second = [
        [device(core, line, pair * PAIR + i) for pair in range(8 // PAIR)]
        for core in range(2)
        for line in range(8)
        for i in range(PAIR)
    ]
    return first, second


def exchange(blocks, groups):
    return lax.all_to_all(
        blocks, "dom", split_axis=0, concat_axis=0, axis_index_groups=groups, tiled=True
    )


def across(blocks):
    return lax.all_to_all(blocks, "rep", split_axis=0, concat_axis=0, tiled=True)


def swap(rows):
    return lax.ppermute(rows, "dom", [(p, p ^ 1) for p in range(128)])


def shards(
    feats, hist_one, local_val, halo_val, halo_send, halo_tile, tile_type, w_one, w_two, grad_out
):
    nodes, cols = feats.shape
    rows = nodes // TILE
    width, experts, _ = w_one.shape
    parts, cap = halo_send.shape[1], halo_send.shape[2]
    pick, types = halo_tile[0], tile_type[0]
    core = lax.rem(lax.axis_index("dom"), 2).astype(jnp.int32).reshape(1)
    first, second = rings()
    flat = (nodes, cols)
    copied = (REPS, nodes, cols)

    (rows_out,) = call(
        pick_body,
        "pick",
        [FAR] * 3,
        [((parts, 2 * cap, cols), BF)],
        [
            pltpu.VMEM((parts, 2 * cap, cols), F32),
            pltpu.VMEM((cap, parts), jnp.int32),
            pltpu.VMEM((nodes, 2 * cols), BF),
            pltpu.SemaphoreType.DMA((3,)),
        ],
        FULL,
    )(jnp.swapaxes(halo_send[0], 0, 1), feats, hist_one)
    landed = lax.all_to_all(rows_out, "dom", split_axis=0, concat_axis=0, tiled=True)
    landed = landed.reshape(rows, 2 * TILE, cols)

    chosen = (rows, width, cols)
    pick_one, pick_two = call(
        choose_body,
        "choose",
        [SMEM] + [FAR] * 2,
        [(chosen, BF)] * 2,
        [pltpu.VMEM(w_one.shape, BF)] * 2 + [pltpu.SemaphoreType.DMA((2,))],
        FULL,
    )(types, w_one, w_two)
    base, wide = call(
        ready_body,
        "ready",
        [SMEM] + [VMEM] * 3,
        [(flat, F32), ((rows, 2 * TILE, 2 * TILE), BF)],
    )(pick, local_val, halo_val, feats)

    base, wide, pick_one, pick_two = lax.optimization_barrier((base, wide, pick_one, pick_two))
    copies, part = call(gather_body, "gather", [SMEM] + [VMEM] * 3, [(copied, BF), (flat, F32)])(
        pick, landed, wide, base
    )
    agg_one = across(copies)
    h_one, near, slope, copies = call(
        one_body, "one", [VMEM] * 5, [(flat, BF)] * 2 + [(flat, F32), (copied, BF)]
    )(agg_one, pick_one, feats, local_val, part)
    agg_two = across(copies)
    h_two, dz_two, back = call(
        two_body,
        "two",
        [VMEM] * 4,
        [(flat, BF), (flat, BF), (copied, BF)],
        [pltpu.VMEM(copied, BF), pltpu.SemaphoreType.DMA((rows,))],
        places=(VMEM, VMEM, ANY),
    )(agg_two, pick_two, near, grad_out)
    back = across(back)

    half = (width // 2, experts * cols)
    keep_two, send_two = call(
        both_body, "grad_two", [SMEM] * 2 + [VMEM] * 2, [(half, F32), (half, BF)]
    )(types, core, agg_two, dz_two)
    dz_one, send_one = call(
        back_body, "back", [SMEM] * 2 + [VMEM] * 5, [(flat, BF), (half, BF)]
    )(types, core, back, local_val, grad_out, slope, agg_one)
    (keep_one,) = call(keep_body, "grad_one", [SMEM] * 2 + [VMEM] * 2, [(half, F32)])(
        types, core, agg_one, dz_one
    )
    pair_one = (keep_one + swap(send_one).astype(F32)).astype(BF)
    pair_two = (keep_two + swap(send_two).astype(F32)).astype(BF)

    split = (RING, width // 2 // RING, experts * cols)
    both = jnp.concatenate([pair_one.reshape(split), pair_two.reshape(split)], axis=1)
    both = exchange(both, first)
    few = both.shape[1]
    (both,) = call(first_body, "first_sum", [VMEM], [((CROSS,) + both.shape[1:], BF)])(both)
    both = exchange(both, second)
    (both,) = call(
        second_body,
        "second_sum",
        [VMEM],
        [((RING, few * experts, cols), BF)],
        [pltpu.VMEM((few, experts, cols), F32)],
    )(both)
    same = exchange(both, first)
    grad_one, grad_two = widen(core, swap(same), widen(core, same))
    return h_two, h_one, grad_one.reshape(w_one.shape), grad_two.reshape(w_two.shape)


def solution(mesh):
    in_specs = (
        P("dom", "rep"),
        P("dom", "rep"),
        P("dom", None),
        P("dom", None),
        P("dom", None, None),
        P("dom", None),
        P("dom", None),
        P(None, None, "rep"),
        P(None, None, "rep"),
        P("dom", "rep"),
    )
    out_specs = (P("dom", "rep"), P("dom", "rep"), P(None, None, "rep"), P(None, None, "rep"))
    return jax.shard_map(shards, mesh=mesh, in_specs=in_specs, out_specs=out_specs, check_vma=False)
```

```python
import jax
import jax.numpy as jnp
from jax import lax
from jax.experimental import pallas as pl
from jax.experimental.pallas import tpu as pltpu
from jax.sharding import PartitionSpec as P

BF = jnp.bfloat16
F32 = jnp.float32
SMEM = pl.BlockSpec(memory_space=pltpu.SMEM)
VMEM = pl.BlockSpec(memory_space=pltpu.VMEM)
ANY = pl.BlockSpec(memory_space=pl.ANY)
FAR = pl.BlockSpec(memory_space=pltpu.HBM)
PARAMS = pltpu.CompilerParams(vmem_limit_bytes=40 << 20)
FULL = pltpu.CompilerParams(vmem_limit_bytes=60 << 20)
PAIR = 2
RING = 16
CROSS = 4
REPS = 4
TILE = 128


def call(body, name, ins, outs, scratch=(), params=PARAMS):
    return pl.pallas_call(
        body,
        out_shape=tuple(jax.ShapeDtypeStruct(shape, kind) for shape, kind in outs),
        in_specs=list(ins),
        out_specs=tuple(VMEM for _ in outs),
        scratch_shapes=list(scratch),
        compiler_params=params,
        name=name,
    )


def dot(a, b, dims=((1,), (0,))):
    return lax.dot_general(a, b, (dims, ((), ())), preferred_element_type=F32)


def block(j):
    return slice(j * TILE, (j + 1) * TILE)


def iota(shape, axis):
    return lax.broadcasted_iota(jnp.int32, shape, axis)


def fetch(sources, targets, sems):
    copies = [
        pltpu.make_async_copy(source, target, sems.at[i])
        for i, (source, target) in enumerate(zip(sources, targets))
    ]
    for copy in copies:
        copy.start()
    return copies


def pick_body(send_far, feats_far, hist_far, out, rows, send, table, sems):
    cap, parts = send.shape
    nodes, cols = feats_far.shape
    targets = (send, table.at[:, :cols], table.at[:, cols:])
    for copy in fetch((send_far, feats_far, hist_far), targets, sems):
        copy.wait()
    for c in range(cap):
        hit = (iota((nodes, parts), 0) == send[c : c + 1, :]).astype(F32).astype(BF)
        got = dot(hit, table[...], ((0,), (0,)))
        rows[:, c, :] = got[:, :cols]
        rows[:, cap + c, :] = got[:, cols:]
    out[...] = rows[...].astype(BF)


def select_rows(types, weights, out):
    rows, width, _ = out.shape
    experts = weights.shape[1]
    span = TILE // rows
    shape = (rows * span, span * experts)
    at, source = iota(shape, 0), iota(shape, 1)
    kind = jnp.zeros(shape, jnp.int32)
    for j in range(rows):
        kind = jnp.where(at // span == j, types[j], kind)
    hit = (source == (at % span) * experts + kind).astype(F32).astype(BF)
    for i in range(width // span):
        part = weights[i * span : (i + 1) * span].reshape(span * experts, -1)
        got = dot(hit, part).astype(BF)
        for j in range(rows):
            out[j, i * span : (i + 1) * span, :] = got[j * span : (j + 1) * span]


def choose_body(types, w_one_far, w_two_far, one, two, w_one, w_two, sems):
    copies = fetch((w_one_far, w_two_far), (w_one, w_two), sems)
    copies[0].wait()
    select_rows(types, w_one, one)
    copies[1].wait()
    select_rows(types, w_two, two)


def ready_body(pick, local, halo_val, feats, base, wide):
    cap = wide.shape[2] // 2 // 32
    shape = (TILE, 2 * TILE)
    k, m = iota(shape, 0), iota(shape, 1)
    spot = (k // cap) * (2 * cap) + k % cap
    first = (m == spot).astype(F32).astype(BF)
    second = (m == spot + cap).astype(F32).astype(BF)
    for j in range(wide.shape[0]):
        base[block(j), :] = dot(local[block(j), :], feats[block(j), :])
        wide[pick[j], :TILE, :] = dot(halo_val[block(j), :], first).astype(BF)
        wide[pick[j], TILE:, :] = dot(halo_val[block(j), :], second).astype(BF)


def gather_body(pick, landed, wide, base, copies, part):
    rows = range(wide.shape[0])
    both = [dot(wide[pick[j]], landed[pick[j]]) for j in rows]
    for j in rows:
        agg = (base[block(j), :] + both[j][:TILE]).astype(BF)
        part[block(j), :] = both[j][TILE:]
        for q in range(copies.shape[0]):
            copies[q, block(j), :] = agg


def products(agg, weights):
    out = []
    for j in range(weights.shape[0]):
        rows = jnp.concatenate([agg[q, block(j), :] for q in range(agg.shape[0])], axis=1)
        out.append(dot(rows, weights[j]))
    return out


def activate(z):
    sig = jax.nn.sigmoid(z)
    return z * sig, sig * (1.0 + z * (1.0 - sig))


def one_body(agg, weights, feats, local, part, hidden, near, slope, copies):
    hs = []
    for j, z in enumerate(products(agg, weights)):
        act, bend = activate(z)
        slope[block(j), :] = bend
        hs.append((feats[block(j), :].astype(F32) + act).astype(BF))
        hidden[block(j), :] = hs[j]
        near[block(j), :] = hs[j]
    mixed = [dot(local[block(j), :], h) for j, h in enumerate(hs)]
    for j, term in enumerate(mixed):
        term = (term + part[block(j), :]).astype(BF)
        for q in range(copies.shape[0]):
            copies[q, block(j), :] = term


def two_body(agg, weights, h_one, grad, hidden, dz, back):
    cols = dz.shape[1]
    ds = []
    for j, z in enumerate(products(agg, weights)):
        act, bend = activate(z)
        hidden[block(j), :] = (h_one[block(j), :].astype(F32) + act).astype(BF)
        ds.append((grad[block(j), :].astype(F32) * bend).astype(BF))
        dz[block(j), :] = ds[j]
    for j, d in enumerate(ds):
        term = dot(d, weights[j], ((1,), (1,))).astype(BF)
        for q in range(back.shape[0]):
            back[q, block(j), :] = term[:, q * cols : (q + 1) * cols]


def write_grad(types, core, agg, dz, keep, send):
    reps, _, cols = agg.shape
    rows = types.shape[0]
    experts = keep.shape[1] // cols
    wide = []
    for e in range(experts):
        part = []
        for j in range(rows):
            part.append((dz[block(j), :].astype(F32) * (types[j] == e).astype(F32)).astype(BF))
        wide.append(jnp.concatenate(part, axis=0))
    wide = jnp.concatenate(wide, axis=1)
    for target, side in ((send, 1 - core[0]), (keep, core[0])):
        for i in range(reps // 2):
            got = dot(agg[side * (reps // 2) + i], wide, ((0,), (0,)))
            target[i * cols : (i + 1) * cols, :] = got.astype(target.dtype)


def back_body(types, core, parts, local, grad, slope, agg, keep, send, dz):
    rows = range(types.shape[0])
    totals = []
    for j in rows:
        total = parts[0, block(j), :].astype(F32)
        for q in range(1, parts.shape[0]):
            total = total + parts[q, block(j), :].astype(F32)
        totals.append(total.astype(BF))
    terms = [dot(local[block(j), :], totals[j], ((0,), (0,))) for j in rows]
    for j in rows:
        dh = grad[block(j), :].astype(F32) + terms[j]
        dz[block(j), :] = (dh * slope[block(j), :]).astype(BF)
    write_grad(types, core, agg, dz, keep, send)


def add_up(parts):
    total = parts[0].astype(F32)
    for i in range(1, parts.shape[0]):
        total = total + parts[i].astype(F32)
    return total


def first_body(parts, copies):
    total = add_up(parts).astype(BF)
    for i in range(copies.shape[0]):
        copies[i] = total


def second_body(parts, copies, table):
    rows, experts, cols = table.shape
    total = add_up(parts)
    for e in range(experts):
        table[:, e, :] = total[:, e * cols : (e + 1) * cols]
    laid = table[...].reshape(rows * experts, cols).astype(BF)
    for i in range(copies.shape[0]):
        copies[i] = laid


def widen_body(core, half, *refs):
    one, two = refs[-2:]
    step = pl.program_id(0)
    length = half.shape[1] // 2
    count = one.shape[0] // length
    for i in range(count):
        rows = half[step * count + i].astype(F32)
        one[i * length : (i + 1) * length, :] = rows[:length]
        two[i * length : (i + 1) * length, :] = rows[length:]


def widen(core, half, before=()):
    chunks, length, cols = half.shape
    steps = 2
    own = not before
    height = chunks // steps * (length // 2)
    target = pl.BlockSpec(
        (height, cols), lambda i, c: ((c[0] if own else 1 - c[0]) * steps + i, 0)
    )
    shape = jax.ShapeDtypeStruct((chunks * length, cols), F32)
    return pl.pallas_call(
        widen_body,
        grid_spec=pltpu.PrefetchScalarGridSpec(
            num_scalar_prefetch=1,
            grid=(steps,),
            in_specs=[VMEM] + [ANY] * len(before),
            out_specs=(target, target),
        ),
        out_shape=(shape, shape),
        input_output_aliases={} if own else {2: 0, 3: 1},
        compiler_params=PARAMS,
        name="widen_own" if own else "widen_other",
    )(core, half, *before)


def rings():
    def device(core, line, cross):
        y, z = (line, cross) if core == 0 else (cross, line)
        return (y * 8 + z) * 2 + core

    first = [
        [device(core, line, pair * PAIR + i) for i in range(PAIR) for line in range(8)]
        for core in range(2)
        for pair in range(8 // PAIR)
    ]
    second = [
        [device(core, line, pair * PAIR + i) for pair in range(8 // PAIR)]
        for core in range(2)
        for line in range(8)
        for i in range(PAIR)
    ]
    return first, second


def exchange(blocks, groups):
    return lax.all_to_all(
        blocks, "dom", split_axis=0, concat_axis=0, axis_index_groups=groups, tiled=True
    )


def across(blocks):
    return lax.all_to_all(blocks, "rep", split_axis=0, concat_axis=0, tiled=True)


def swap(rows):
    return lax.ppermute(rows, "dom", [(p, p ^ 1) for p in range(128)])


def shards(
    feats, hist_one, local_val, halo_val, halo_send, halo_tile, tile_type, w_one, w_two, grad_out
):
    nodes, cols = feats.shape
    rows = nodes // TILE
    width, experts, _ = w_one.shape
    parts, cap = halo_send.shape[1], halo_send.shape[2]
    pick, types = halo_tile[0], tile_type[0]
    core = lax.rem(lax.axis_index("dom"), 2).astype(jnp.int32).reshape(1)
    first, second = rings()
    flat = (nodes, cols)
    copied = (REPS, nodes, cols)

    (rows_out,) = call(
        pick_body,
        "pick",
        [FAR] * 3,
        [((parts, 2 * cap, cols), BF)],
        [
            pltpu.VMEM((parts, 2 * cap, cols), F32),
            pltpu.VMEM((cap, parts), jnp.int32),
            pltpu.VMEM((nodes, 2 * cols), BF),
            pltpu.SemaphoreType.DMA((3,)),
        ],
        FULL,
    )(jnp.swapaxes(halo_send[0], 0, 1), feats, hist_one)
    landed = lax.all_to_all(rows_out, "dom", split_axis=0, concat_axis=0, tiled=True)
    landed = landed.reshape(rows, 2 * TILE, cols)

    chosen = (rows, width, cols)
    pick_one, pick_two = call(
        choose_body,
        "choose",
        [SMEM] + [FAR] * 2,
        [(chosen, BF)] * 2,
        [pltpu.VMEM(w_one.shape, BF)] * 2 + [pltpu.SemaphoreType.DMA((2,))],
        FULL,
    )(types, w_one, w_two)
    base, wide = call(
        ready_body,
        "ready",
        [SMEM] + [VMEM] * 3,
        [(flat, F32), ((rows, 2 * TILE, 2 * TILE), BF)],
    )(pick, local_val, halo_val, feats)

    base, wide, pick_one, pick_two = lax.optimization_barrier((base, wide, pick_one, pick_two))
    copies, part = call(gather_body, "gather", [SMEM] + [VMEM] * 3, [(copied, BF), (flat, F32)])(
        pick, landed, wide, base
    )
    agg_one = across(copies)
    h_one, near, slope, copies = call(
        one_body, "one", [VMEM] * 5, [(flat, BF)] * 2 + [(flat, F32), (copied, BF)]
    )(agg_one, pick_one, feats, local_val, part)
    agg_two = across(copies)
    h_two, dz_two, back = call(
        two_body, "two", [VMEM] * 4, [(flat, BF), (flat, BF), (copied, BF)]
    )(agg_two, pick_two, near, grad_out)
    back = across(back)

    half = (width // 2, experts * cols)
    keep_two, send_two = call(
        write_grad, "grad_two", [SMEM] * 2 + [VMEM] * 2, [(half, F32), (half, BF)]
    )(types, core, agg_two, dz_two)
    keep_one, send_one = call(
        back_body,
        "back",
        [SMEM] * 2 + [VMEM] * 5,
        [(half, F32), (half, BF)],
        [pltpu.VMEM(flat, BF)],
    )(types, core, back, local_val, grad_out, slope, agg_one)
    pair_one = (keep_one + swap(send_one).astype(F32)).astype(BF)
    pair_two = (keep_two + swap(send_two).astype(F32)).astype(BF)

    split = (RING, width // 2 // RING, experts * cols)
    both = jnp.concatenate([pair_one.reshape(split), pair_two.reshape(split)], axis=1)
    both = exchange(both, first)
    few = both.shape[1]
    (both,) = call(first_body, "first_sum", [VMEM], [((CROSS,) + both.shape[1:], BF)])(both)
    both = exchange(both, second)
    (both,) = call(
        second_body,
        "second_sum",
        [VMEM],
        [((RING, few * experts, cols), BF)],
        [pltpu.VMEM((few, experts, cols), F32)],
    )(both)
    same = exchange(both, first)
    grad_one, grad_two = widen(core, swap(same), widen(core, same))
    return h_two, h_one, grad_one.reshape(w_one.shape), grad_two.reshape(w_two.shape)


def solution(mesh):
    in_specs = (
        P("dom", "rep"),
        P("dom", "rep"),
        P("dom", None),
        P("dom", None),
        P("dom", None, None),
        P("dom", None),
        P("dom", None),
        P(None, None, "rep"),
        P(None, None, "rep"),
        P("dom", "rep"),
    )
    out_specs = (P("dom", "rep"), P("dom", "rep"), P(None, None, "rep"), P(None, None, "rep"))
    return jax.shard_map(shards, mesh=mesh, in_specs=in_specs, out_specs=out_specs, check_vma=False)
```

```python
import jax
import jax.numpy as jnp
from jax import lax
from jax.experimental import pallas as pl
from jax.experimental.pallas import tpu as pltpu
from jax.sharding import PartitionSpec as P

BF = jnp.bfloat16
F32 = jnp.float32
SMEM = pl.BlockSpec(memory_space=pltpu.SMEM)
VMEM = pl.BlockSpec(memory_space=pltpu.VMEM)
ANY = pl.BlockSpec(memory_space=pl.ANY)
FAR = pl.BlockSpec(memory_space=pltpu.HBM)
PARAMS = pltpu.CompilerParams(vmem_limit_bytes=40 << 20)
FULL = pltpu.CompilerParams(vmem_limit_bytes=60 << 20)
PAIR = 2
RING = 16
CROSS = 4
REPS = 4
TILE = 128


def call(body, name, ins, outs, scratch=(), params=PARAMS):
    return pl.pallas_call(
        body,
        out_shape=tuple(jax.ShapeDtypeStruct(shape, kind) for shape, kind in outs),
        in_specs=list(ins),
        out_specs=tuple(VMEM for _ in outs),
        scratch_shapes=list(scratch),
        compiler_params=params,
        name=name,
    )


def dot(a, b, dims=((1,), (0,))):
    return lax.dot_general(a, b, (dims, ((), ())), preferred_element_type=F32)


def block(j):
    return slice(j * TILE, (j + 1) * TILE)


def iota(shape, axis):
    return lax.broadcasted_iota(jnp.int32, shape, axis)


def fetch(sources, targets, sems):
    copies = [
        pltpu.make_async_copy(source, target, sems.at[i])
        for i, (source, target) in enumerate(zip(sources, targets))
    ]
    for copy in copies:
        copy.start()
    return copies


def pick_body(send_far, feats_far, hist_far, out, rows, send, table, sems):
    cap, parts = send.shape
    nodes, cols = feats_far.shape
    targets = (send, table.at[:, :cols], table.at[:, cols:])
    copies = fetch((send_far, feats_far, hist_far), targets, sems)
    copies[0].wait()
    spot = iota((nodes, parts), 0)
    hits = [(spot == send[c : c + 1, :]).astype(F32).astype(BF) for c in range(cap)]
    hits = jnp.concatenate(hits, axis=1)
    for copy in copies[1:]:
        copy.wait()
    got = dot(hits, table[...], ((0,), (0,)))
    for c in range(cap):
        rows[:, c, :] = got[block(c), :cols]
        rows[:, cap + c, :] = got[block(c), cols:]
    out[...] = rows[...].astype(BF)


def select_rows(types, weights, out):
    rows, width, _ = out.shape
    experts = weights.shape[1]
    span = TILE // rows
    shape = (rows * span, span * experts)
    at, source = iota(shape, 0), iota(shape, 1)
    kind = jnp.zeros(shape, jnp.int32)
    for j in range(rows):
        kind = jnp.where(at // span == j, types[j], kind)
    hit = (source == (at % span) * experts + kind).astype(F32).astype(BF)
    for i in range(width // span):
        part = weights[i * span : (i + 1) * span].reshape(span * experts, -1)
        got = dot(hit, part).astype(BF)
        for j in range(rows):
            out[j, i * span : (i + 1) * span, :] = got[j * span : (j + 1) * span]


def choose_body(types, w_one_far, w_two_far, one, two, w_one, w_two, sems):
    copies = fetch((w_one_far, w_two_far), (w_one, w_two), sems)
    copies[0].wait()
    select_rows(types, w_one, one)
    copies[1].wait()
    select_rows(types, w_two, two)


def ready_body(pick, local, halo_val, feats, base, wide):
    cap = wide.shape[2] // 2 // 32
    shape = (TILE, 2 * TILE)
    k, m = iota(shape, 0), iota(shape, 1)
    spot = (k // cap) * (2 * cap) + k % cap
    first = (m == spot).astype(F32).astype(BF)
    second = (m == spot + cap).astype(F32).astype(BF)
    for j in range(wide.shape[0]):
        base[block(j), :] = dot(local[block(j), :], feats[block(j), :])
        wide[pick[j], :TILE, :] = dot(halo_val[block(j), :], first).astype(BF)
        wide[pick[j], TILE:, :] = dot(halo_val[block(j), :], second).astype(BF)


def gather_body(pick, landed, wide, base, copies, part):
    rows = range(wide.shape[0])
    both = [dot(wide[pick[j]], landed[pick[j]]) for j in rows]
    for j in rows:
        agg = (base[block(j), :] + both[j][:TILE]).astype(BF)
        part[block(j), :] = both[j][TILE:]
        for q in range(copies.shape[0]):
            copies[q, block(j), :] = agg


def products(agg, weights):
    out = []
    for j in range(weights.shape[0]):
        rows = jnp.concatenate([agg[q, block(j), :] for q in range(agg.shape[0])], axis=1)
        out.append(dot(rows, weights[j]))
    return out


def activate(z):
    sig = jax.nn.sigmoid(z)
    return z * sig, sig * (1.0 + z * (1.0 - sig))


def one_body(agg, weights, feats, local, part, near, slope, copies):
    hs = []
    for j, z in enumerate(products(agg, weights)):
        act, bend = activate(z)
        slope[block(j), :] = bend
        hs.append((feats[block(j), :].astype(F32) + act).astype(BF))
        near[block(j), :] = hs[j]
    mixed = [dot(local[block(j), :], h) for j, h in enumerate(hs)]
    for j, term in enumerate(mixed):
        term = (term + part[block(j), :]).astype(BF)
        for q in range(copies.shape[0]):
            copies[q, block(j), :] = term


def two_body(agg, weights, h_one, grad, hidden, dz, back):
    cols = dz.shape[1]
    ds = []
    for j, z in enumerate(products(agg, weights)):
        act, bend = activate(z)
        hidden[block(j), :] = (h_one[block(j), :].astype(F32) + act).astype(BF)
        ds.append((grad[block(j), :].astype(F32) * bend).astype(BF))
        dz[block(j), :] = ds[j]
    for j, d in enumerate(ds):
        term = dot(d, weights[j], ((1,), (1,))).astype(BF)
        for q in range(back.shape[0]):
            back[q, block(j), :] = term[:, q * cols : (q + 1) * cols]


def write_grad(types, core, agg, dz, keep, send):
    reps, _, cols = agg.shape
    rows = types.shape[0]
    experts = keep.shape[1] // cols
    wide = []
    for e in range(experts):
        part = []
        for j in range(rows):
            part.append((dz[block(j), :].astype(F32) * (types[j] == e).astype(F32)).astype(BF))
        wide.append(jnp.concatenate(part, axis=0))
    wide = jnp.concatenate(wide, axis=1)
    for target, side in ((send, 1 - core[0]), (keep, core[0])):
        for i in range(reps // 2):
            got = dot(agg[side * (reps // 2) + i], wide, ((0,), (0,)))
            target[i * cols : (i + 1) * cols, :] = got.astype(target.dtype)


def two_grad_body(types, core, agg, dz, near_one, near_two, keep, send, h_one, h_two):
    h_one[...] = near_one[...]
    h_two[...] = near_two[...]
    write_grad(types, core, agg, dz, keep, send)


def back_body(types, core, parts, local, grad, slope, agg, keep, send, dz):
    rows = range(types.shape[0])
    totals = []
    for j in rows:
        total = parts[0, block(j), :].astype(F32)
        for q in range(1, parts.shape[0]):
            total = total + parts[q, block(j), :].astype(F32)
        totals.append(total.astype(BF))
    terms = [dot(local[block(j), :], totals[j], ((0,), (0,))) for j in rows]
    for j in rows:
        dh = grad[block(j), :].astype(F32) + terms[j]
        dz[block(j), :] = (dh * slope[block(j), :]).astype(BF)
    write_grad(types, core, agg, dz, keep, send)


def add_up(parts):
    total = parts[0].astype(F32)
    for i in range(1, parts.shape[0]):
        total = total + parts[i].astype(F32)
    return total


def first_body(parts, copies):
    total = add_up(parts).astype(BF)
    for i in range(copies.shape[0]):
        copies[i] = total


def second_body(parts, copies, table):
    rows, experts, cols = table.shape
    total = add_up(parts)
    for e in range(experts):
        table[:, e, :] = total[:, e * cols : (e + 1) * cols]
    laid = table[...].reshape(rows * experts, cols).astype(BF)
    for i in range(copies.shape[0]):
        copies[i] = laid


def widen_body(core, half, *refs):
    one, two = refs[-2:]
    step = pl.program_id(0)
    length = half.shape[1] // 2
    count = one.shape[0] // length
    for i in range(count):
        rows = half[step * count + i].astype(F32)
        one[i * length : (i + 1) * length, :] = rows[:length]
        two[i * length : (i + 1) * length, :] = rows[length:]


def widen(core, half, before=()):
    chunks, length, cols = half.shape
    steps = 2
    own = not before
    height = chunks // steps * (length // 2)
    target = pl.BlockSpec(
        (height, cols), lambda i, c: ((c[0] if own else 1 - c[0]) * steps + i, 0)
    )
    shape = jax.ShapeDtypeStruct((chunks * length, cols), F32)
    return pl.pallas_call(
        widen_body,
        grid_spec=pltpu.PrefetchScalarGridSpec(
            num_scalar_prefetch=1,
            grid=(steps,),
            in_specs=[VMEM] + [ANY] * len(before),
            out_specs=(target, target),
        ),
        out_shape=(shape, shape),
        input_output_aliases={} if own else {2: 0, 3: 1},
        compiler_params=PARAMS,
        name="widen_own" if own else "widen_other",
    )(core, half, *before)


def rings():
    def device(core, line, cross):
        y, z = (line, cross) if core == 0 else (cross, line)
        return (y * 8 + z) * 2 + core

    first = [
        [device(core, line, pair * PAIR + i) for i in range(PAIR) for line in range(8)]
        for core in range(2)
        for pair in range(8 // PAIR)
    ]
    second = [
        [device(core, line, pair * PAIR + i) for pair in range(8 // PAIR)]
        for core in range(2)
        for line in range(8)
        for i in range(PAIR)
    ]
    return first, second


def exchange(blocks, groups):
    return lax.all_to_all(
        blocks, "dom", split_axis=0, concat_axis=0, axis_index_groups=groups, tiled=True
    )


def across(blocks):
    return lax.all_to_all(blocks, "rep", split_axis=0, concat_axis=0, tiled=True)


def swap(rows):
    return lax.ppermute(rows, "dom", [(p, p ^ 1) for p in range(128)])


def shards(
    feats, hist_one, local_val, halo_val, halo_send, halo_tile, tile_type, w_one, w_two, grad_out
):
    nodes, cols = feats.shape
    rows = nodes // TILE
    width, experts, _ = w_one.shape
    parts, cap = halo_send.shape[1], halo_send.shape[2]
    pick, types = halo_tile[0], tile_type[0]
    core = lax.rem(lax.axis_index("dom"), 2).astype(jnp.int32).reshape(1)
    first, second = rings()
    flat = (nodes, cols)
    copied = (REPS, nodes, cols)

    (rows_out,) = call(
        pick_body,
        "pick",
        [FAR] * 3,
        [((parts, 2 * cap, cols), BF)],
        [
            pltpu.VMEM((parts, 2 * cap, cols), F32),
            pltpu.VMEM((cap, parts), jnp.int32),
            pltpu.VMEM((nodes, 2 * cols), BF),
            pltpu.SemaphoreType.DMA((3,)),
        ],
        FULL,
    )(jnp.swapaxes(halo_send[0], 0, 1), feats, hist_one)
    landed = lax.all_to_all(rows_out, "dom", split_axis=0, concat_axis=0, tiled=True)
    landed = landed.reshape(rows, 2 * TILE, cols)

    chosen = (rows, width, cols)
    pick_one, pick_two = call(
        choose_body,
        "choose",
        [SMEM] + [FAR] * 2,
        [(chosen, BF)] * 2,
        [pltpu.VMEM(w_one.shape, BF)] * 2 + [pltpu.SemaphoreType.DMA((2,))],
        FULL,
    )(types, w_one, w_two)
    base, wide = call(
        ready_body,
        "ready",
        [SMEM] + [VMEM] * 3,
        [(flat, F32), ((rows, 2 * TILE, 2 * TILE), BF)],
    )(pick, local_val, halo_val, feats)

    base, wide, pick_one, pick_two = lax.optimization_barrier((base, wide, pick_one, pick_two))
    copies, part = call(gather_body, "gather", [SMEM] + [VMEM] * 3, [(copied, BF), (flat, F32)])(
        pick, landed, wide, base
    )
    agg_one = across(copies)
    near_one, slope, copies = call(
        one_body, "one", [VMEM] * 5, [(flat, BF), (flat, F32), (copied, BF)]
    )(agg_one, pick_one, feats, local_val, part)
    agg_two = across(copies)
    near_two, dz_two, back = call(
        two_body, "two", [VMEM] * 4, [(flat, BF), (flat, BF), (copied, BF)]
    )(agg_two, pick_two, near_one, grad_out)
    back = across(back)

    half = (width // 2, experts * cols)
    keep_two, send_two, h_one, h_two = call(
        two_grad_body,
        "grad_two",
        [SMEM] * 2 + [VMEM] * 4,
        [(half, F32), (half, BF), (flat, BF), (flat, BF)],
    )(types, core, agg_two, dz_two, near_one, near_two)
    keep_one, send_one = call(
        back_body,
        "back",
        [SMEM] * 2 + [VMEM] * 5,
        [(half, F32), (half, BF)],
        [pltpu.VMEM(flat, BF)],
    )(types, core, back, local_val, grad_out, slope, agg_one)
    pair_one = (keep_one + swap(send_one).astype(F32)).astype(BF)
    pair_two = (keep_two + swap(send_two).astype(F32)).astype(BF)

    split = (RING, width // 2 // RING, experts * cols)
    both = jnp.concatenate([pair_one.reshape(split), pair_two.reshape(split)], axis=1)
    both = exchange(both, first)
    few = both.shape[1]
    (both,) = call(first_body, "first_sum", [VMEM], [((CROSS,) + both.shape[1:], BF)])(both)
    both = exchange(both, second)
    (both,) = call(
        second_body,
        "second_sum",
        [VMEM],
        [((RING, few * experts, cols), BF)],
        [pltpu.VMEM((few, experts, cols), F32)],
    )(both)
    same = exchange(both, first)
    grad_one, grad_two = widen(core, swap(same), widen(core, same))
    return h_two, h_one, grad_one.reshape(w_one.shape), grad_two.reshape(w_two.shape)


def solution(mesh):
    in_specs = (
        P("dom", "rep"),
        P("dom", "rep"),
        P("dom", None),
        P("dom", None),
        P("dom", None, None),
        P("dom", None),
        P("dom", None),
        P(None, None, "rep"),
        P(None, None, "rep"),
        P("dom", "rep"),
    )
    out_specs = (P("dom", "rep"), P("dom", "rep"), P(None, None, "rep"), P(None, None, "rep"))
    return jax.shard_map(shards, mesh=mesh, in_specs=in_specs, out_specs=out_specs, check_vma=False)
```

```python
import jax
import jax.numpy as jnp
from jax import lax
from jax.experimental import pallas as pl
from jax.experimental.pallas import tpu as pltpu
from jax.sharding import PartitionSpec as P

BF = jnp.bfloat16
F32 = jnp.float32
SMEM = pl.BlockSpec(memory_space=pltpu.SMEM)
VMEM = pl.BlockSpec(memory_space=pltpu.VMEM)
ANY = pl.BlockSpec(memory_space=pl.ANY)
FAR = pl.BlockSpec(memory_space=pltpu.HBM)
PARAMS = pltpu.CompilerParams(vmem_limit_bytes=40 << 20)
FULL = pltpu.CompilerParams(vmem_limit_bytes=60 << 20)
PAIR = 2
RING = 16
CROSS = 4
REPS = 4
TILE = 128


def call(body, name, ins, outs, scratch=(), params=PARAMS):
    return pl.pallas_call(
        body,
        out_shape=tuple(jax.ShapeDtypeStruct(shape, kind) for shape, kind in outs),
        in_specs=list(ins),
        out_specs=tuple(VMEM for _ in outs),
        scratch_shapes=list(scratch),
        compiler_params=params,
        name=name,
    )


def dot(a, b, dims=((1,), (0,))):
    return lax.dot_general(a, b, (dims, ((), ())), preferred_element_type=F32)


def block(j):
    return slice(j * TILE, (j + 1) * TILE)


def iota(shape, axis):
    return lax.broadcasted_iota(jnp.int32, shape, axis)


def fetch(sources, targets, sems):
    copies = [
        pltpu.make_async_copy(source, target, sems.at[i])
        for i, (source, target) in enumerate(zip(sources, targets))
    ]
    for copy in copies:
        copy.start()
    return copies


def pick_body(send_far, feats_far, hist_far, out, rows, send, table, sems):
    cap, parts = send.shape
    nodes, cols = feats_far.shape
    targets = (send, table.at[:, :cols], table.at[:, cols:])
    copies = fetch((send_far, feats_far, hist_far), targets, sems)
    copies[0].wait()
    spot = iota((nodes, parts), 0)
    hits = [(spot == send[c : c + 1, :]).astype(F32).astype(BF) for c in range(cap)]
    hits = jnp.concatenate(hits, axis=1)
    for copy in copies[1:]:
        copy.wait()
    got = dot(hits, table[...], ((0,), (0,)))
    for c in range(cap):
        rows[:, c, :] = got[block(c), :cols]
        rows[:, cap + c, :] = got[block(c), cols:]
    out[...] = rows[...].astype(BF)


def select_rows(types, weights, out):
    rows, width, _ = out.shape
    experts = weights.shape[1]
    span = TILE // rows
    shape = (rows * span, span * experts)
    at, source = iota(shape, 0), iota(shape, 1)
    kind = jnp.zeros(shape, jnp.int32)
    for j in range(rows):
        kind = jnp.where(at // span == j, types[j], kind)
    hit = (source == (at % span) * experts + kind).astype(F32).astype(BF)
    for i in range(width // span):
        part = weights[i * span : (i + 1) * span].reshape(span * experts, -1)
        got = dot(hit, part).astype(BF)
        for j in range(rows):
            out[j, i * span : (i + 1) * span, :] = got[j * span : (j + 1) * span]


def choose_body(types, w_one_far, w_two_far, one, two, w_one, w_two, sems):
    copies = fetch((w_one_far, w_two_far), (w_one, w_two), sems)
    copies[0].wait()
    select_rows(types, w_one, one)
    copies[1].wait()
    select_rows(types, w_two, two)


def ready_body(pick, local, halo_val, feats, base, wide):
    cap = wide.shape[2] // 2 // 32
    shape = (TILE, 2 * TILE)
    k, m = iota(shape, 0), iota(shape, 1)
    spot = (k // cap) * (2 * cap) + k % cap
    first = (m == spot).astype(F32).astype(BF)
    second = (m == spot + cap).astype(F32).astype(BF)
    for j in range(wide.shape[0]):
        base[block(j), :] = dot(local[block(j), :], feats[block(j), :])
        wide[pick[j], :TILE, :] = dot(halo_val[block(j), :], first).astype(BF)
        wide[pick[j], TILE:, :] = dot(halo_val[block(j), :], second).astype(BF)


def gather_body(pick, landed, wide, base, copies, part):
    rows = range(wide.shape[0])
    both = [dot(wide[pick[j]], landed[pick[j]]) for j in rows]
    for j in rows:
        agg = (base[block(j), :] + both[j][:TILE]).astype(BF)
        part[block(j), :] = both[j][TILE:]
        for q in range(copies.shape[0]):
            copies[q, block(j), :] = agg


def products(agg, weights):
    out = []
    for j in range(weights.shape[0]):
        rows = jnp.concatenate([agg[q, block(j), :] for q in range(agg.shape[0])], axis=1)
        out.append(dot(rows, weights[j]))
    return out


def activate(z):
    sig = jax.nn.sigmoid(z)
    return z * sig, sig * (1.0 + z * (1.0 - sig))


def one_body(agg, weights, feats, local, part, near, slope, copies):
    hs = []
    for j, z in enumerate(products(agg, weights)):
        act, bend = activate(z)
        slope[block(j), :] = bend
        hs.append((feats[block(j), :].astype(F32) + act).astype(BF))
        near[block(j), :] = hs[j]
    mixed = [dot(local[block(j), :], h) for j, h in enumerate(hs)]
    for j, term in enumerate(mixed):
        term = (term + part[block(j), :]).astype(BF)
        for q in range(copies.shape[0]):
            copies[q, block(j), :] = term


def two_body(agg, weights, h_one, grad, hidden, dz, back):
    cols = dz.shape[1]
    ds = []
    for j, z in enumerate(products(agg, weights)):
        act, bend = activate(z)
        hidden[block(j), :] = (h_one[block(j), :].astype(F32) + act).astype(BF)
        ds.append((grad[block(j), :].astype(F32) * bend).astype(BF))
        dz[block(j), :] = ds[j]
    for j, d in enumerate(ds):
        term = dot(d, weights[j], ((1,), (1,))).astype(BF)
        for q in range(back.shape[0]):
            back[q, block(j), :] = term[:, q * cols : (q + 1) * cols]


def write_grad(types, core, agg, dz, keep, send, dims):
    reps = agg.shape[0]
    cols = dz.shape[1]
    rows = types.shape[0]
    zero = jnp.zeros((TILE, cols), BF)
    experts = keep.shape[1] // cols
    wide = []
    for e in range(experts):
        part = []
        for j in range(rows):
            part.append(lax.select(types[j] == e, dz[block(j), :], zero))
        wide.append(jnp.concatenate(part, axis=0))
    wide = jnp.concatenate(wide, axis=1)
    for target, side in ((send, 1 - core[0]), (keep, core[0])):
        for i in range(reps // 2):
            got = dot(agg[side * (reps // 2) + i], wide, dims)
            target[i * cols : (i + 1) * cols, :] = got.astype(target.dtype)


def two_grad_body(types, core, agg, dz, near_one, near_two, keep, send, h_one, h_two):
    h_one[...] = near_one[...]
    h_two[...] = near_two[...]
    write_grad(types, core, agg, dz, keep, send, ((0,), (0,)))


def turn_body(agg, turned):
    for q in range(agg.shape[0]):
        turned[q] = jnp.transpose(agg[q])


def back_body(types, core, parts, local, grad, slope, agg, keep, send, dz):
    rows = range(types.shape[0])
    totals = []
    for j in rows:
        total = parts[0, block(j), :].astype(F32)
        for q in range(1, parts.shape[0]):
            total = total + parts[q, block(j), :].astype(F32)
        totals.append(total.astype(BF))
    terms = [dot(local[block(j), :], totals[j], ((0,), (0,))) for j in rows]
    for j in rows:
        dh = grad[block(j), :].astype(F32) + terms[j]
        dz[block(j), :] = (dh * slope[block(j), :]).astype(BF)
    write_grad(types, core, agg, dz, keep, send, ((1,), (0,)))


def add_up(parts):
    total = parts[0].astype(F32)
    for i in range(1, parts.shape[0]):
        total = total + parts[i].astype(F32)
    return total


def first_body(parts, copies):
    total = add_up(parts).astype(BF)
    for i in range(copies.shape[0]):
        copies[i] = total


def second_body(parts, copies, table):
    rows, experts, cols = table.shape
    total = add_up(parts)
    for e in range(experts):
        table[:, e, :] = total[:, e * cols : (e + 1) * cols]
    laid = table[...].reshape(rows * experts, cols).astype(BF)
    for i in range(copies.shape[0]):
        copies[i] = laid


def widen_body(core, half, *refs):
    one, two = refs[-2:]
    step = pl.program_id(0)
    length = half.shape[1] // 2
    count = one.shape[0] // length
    for i in range(count):
        rows = half[step * count + i].astype(F32)
        one[i * length : (i + 1) * length, :] = rows[:length]
        two[i * length : (i + 1) * length, :] = rows[length:]


def widen(core, half, before=()):
    chunks, length, cols = half.shape
    steps = 2
    own = not before
    height = chunks // steps * (length // 2)
    target = pl.BlockSpec(
        (height, cols), lambda i, c: ((c[0] if own else 1 - c[0]) * steps + i, 0)
    )
    shape = jax.ShapeDtypeStruct((chunks * length, cols), F32)
    return pl.pallas_call(
        widen_body,
        grid_spec=pltpu.PrefetchScalarGridSpec(
            num_scalar_prefetch=1,
            grid=(steps,),
            in_specs=[VMEM] + [ANY] * len(before),
            out_specs=(target, target),
        ),
        out_shape=(shape, shape),
        input_output_aliases={} if own else {2: 0, 3: 1},
        compiler_params=PARAMS,
        name="widen_own" if own else "widen_other",
    )(core, half, *before)


def rings():
    def device(core, line, cross):
        y, z = (line, cross) if core == 0 else (cross, line)
        return (y * 8 + z) * 2 + core

    first = [
        [device(core, line, pair * PAIR + i) for i in range(PAIR) for line in range(8)]
        for core in range(2)
        for pair in range(8 // PAIR)
    ]
    second = [
        [device(core, line, pair * PAIR + i) for pair in range(8 // PAIR)]
        for core in range(2)
        for line in range(8)
        for i in range(PAIR)
    ]
    return first, second


def exchange(blocks, groups):
    return lax.all_to_all(
        blocks, "dom", split_axis=0, concat_axis=0, axis_index_groups=groups, tiled=True
    )


def across(blocks):
    return lax.all_to_all(blocks, "rep", split_axis=0, concat_axis=0, tiled=True)


def swap(rows):
    return lax.ppermute(rows, "dom", [(p, p ^ 1) for p in range(128)])


def shards(
    feats, hist_one, local_val, halo_val, halo_send, halo_tile, tile_type, w_one, w_two, grad_out
):
    nodes, cols = feats.shape
    rows = nodes // TILE
    width, experts, _ = w_one.shape
    parts, cap = halo_send.shape[1], halo_send.shape[2]
    pick, types = halo_tile[0], tile_type[0]
    core = lax.rem(lax.axis_index("dom"), 2).astype(jnp.int32).reshape(1)
    first, second = rings()
    flat = (nodes, cols)
    copied = (REPS, nodes, cols)

    (rows_out,) = call(
        pick_body,
        "pick",
        [FAR] * 3,
        [((parts, 2 * cap, cols), BF)],
        [
            pltpu.VMEM((parts, 2 * cap, cols), F32),
            pltpu.VMEM((cap, parts), jnp.int32),
            pltpu.VMEM((nodes, 2 * cols), BF),
            pltpu.SemaphoreType.DMA((3,)),
        ],
        FULL,
    )(jnp.swapaxes(halo_send[0], 0, 1), feats, hist_one)
    landed = lax.all_to_all(rows_out, "dom", split_axis=0, concat_axis=0, tiled=True)
    landed = landed.reshape(rows, 2 * TILE, cols)

    chosen = (rows, width, cols)
    pick_one, pick_two = call(
        choose_body,
        "choose",
        [SMEM] + [FAR] * 2,
        [(chosen, BF)] * 2,
        [pltpu.VMEM(w_one.shape, BF)] * 2 + [pltpu.SemaphoreType.DMA((2,))],
        FULL,
    )(types, w_one, w_two)
    base, wide = call(
        ready_body,
        "ready",
        [SMEM] + [VMEM] * 3,
        [(flat, F32), ((rows, 2 * TILE, 2 * TILE), BF)],
    )(pick, local_val, halo_val, feats)

    base, wide, pick_one, pick_two = lax.optimization_barrier((base, wide, pick_one, pick_two))
    copies, part = call(gather_body, "gather", [SMEM] + [VMEM] * 3, [(copied, BF), (flat, F32)])(
        pick, landed, wide, base
    )
    agg_one = across(copies)
    near_one, slope, copies = call(
        one_body, "one", [VMEM] * 5, [(flat, BF), (flat, F32), (copied, BF)]
    )(agg_one, pick_one, feats, local_val, part)
    agg_two = across(copies)
    near_two, dz_two, back = call(
        two_body, "two", [VMEM] * 4, [(flat, BF), (flat, BF), (copied, BF)]
    )(agg_two, pick_two, near_one, grad_out)
    back = across(back)

    half = (width // 2, experts * cols)
    keep_two, send_two, h_one, h_two = call(
        two_grad_body,
        "grad_two",
        [SMEM] * 2 + [VMEM] * 4,
        [(half, F32), (half, BF), (flat, BF), (flat, BF)],
    )(types, core, agg_two, dz_two, near_one, near_two)
    agg_one, keep_two = lax.optimization_barrier((agg_one, keep_two))
    (turned,) = call(turn_body, "turn", [VMEM], [((REPS, cols, nodes), BF)])(agg_one)
    keep_one, send_one = call(
        back_body,
        "back",
        [SMEM] * 2 + [VMEM] * 5,
        [(half, F32), (half, BF)],
        [pltpu.VMEM(flat, BF)],
    )(types, core, back, local_val, grad_out, slope, turned)
    pair_one = (keep_one + swap(send_one).astype(F32)).astype(BF)
    pair_two = (keep_two + swap(send_two).astype(F32)).astype(BF)

    split = (RING, width // 2 // RING, experts * cols)
    both = jnp.concatenate([pair_one.reshape(split), pair_two.reshape(split)], axis=1)
    both = exchange(both, first)
    few = both.shape[1]
    (both,) = call(first_body, "first_sum", [VMEM], [((CROSS,) + both.shape[1:], BF)])(both)
    both = exchange(both, second)
    (both,) = call(
        second_body,
        "second_sum",
        [VMEM],
        [((RING, few * experts, cols), BF)],
        [pltpu.VMEM((few, experts, cols), F32)],
    )(both)
    same = exchange(both, first)
    grad_one, grad_two = widen(core, swap(same), widen(core, same))
    return h_two, h_one, grad_one.reshape(w_one.shape), grad_two.reshape(w_two.shape)


def solution(mesh):
    in_specs = (
        P("dom", "rep"),
        P("dom", "rep"),
        P("dom", None),
        P("dom", None),
        P("dom", None, None),
        P("dom", None),
        P("dom", None),
        P(None, None, "rep"),
        P(None, None, "rep"),
        P("dom", "rep"),
    )
    out_specs = (P("dom", "rep"), P("dom", "rep"), P(None, None, "rep"), P(None, None, "rep"))
    return jax.shard_map(shards, mesh=mesh, in_specs=in_specs, out_specs=out_specs, check_vma=False)
```

```python
import jax
import jax.numpy as jnp
from jax import lax
from jax.experimental import pallas as pl
from jax.experimental.pallas import tpu as pltpu
from jax.sharding import PartitionSpec as P

BF = jnp.bfloat16
F32 = jnp.float32
SMEM = pl.BlockSpec(memory_space=pltpu.SMEM)
VMEM = pl.BlockSpec(memory_space=pltpu.VMEM)
ANY = pl.BlockSpec(memory_space=pl.ANY)
FAR = pl.BlockSpec(memory_space=pltpu.HBM)
PARAMS = pltpu.CompilerParams(vmem_limit_bytes=40 << 20)
FULL = pltpu.CompilerParams(vmem_limit_bytes=60 << 20)
PAIR = 2
RING = 16
CROSS = 4
REPS = 4
TILE = 128


def call(body, name, ins, outs, scratch=(), params=PARAMS):
    return pl.pallas_call(
        body,
        out_shape=tuple(jax.ShapeDtypeStruct(shape, kind) for shape, kind in outs),
        in_specs=list(ins),
        out_specs=tuple(VMEM for _ in outs),
        scratch_shapes=list(scratch),
        compiler_params=params,
        name=name,
    )


def dot(a, b, dims=((1,), (0,))):
    return lax.dot_general(a, b, (dims, ((), ())), preferred_element_type=F32)


def block(j):
    return slice(j * TILE, (j + 1) * TILE)


def iota(shape, axis):
    return lax.broadcasted_iota(jnp.int32, shape, axis)


def fetch(sources, targets, sems):
    copies = [
        pltpu.make_async_copy(source, target, sems.at[i])
        for i, (source, target) in enumerate(zip(sources, targets))
    ]
    for copy in copies:
        copy.start()
    return copies


def pick_body(send_far, feats_far, hist_far, out, rows, send, table, sems):
    cap, parts = send.shape
    nodes, cols = feats_far.shape
    targets = (send, table.at[:, :cols], table.at[:, cols:])
    copies = fetch((send_far, feats_far, hist_far), targets, sems)
    copies[0].wait()
    spot = iota((nodes, parts), 0)
    hits = [(spot == send[c : c + 1, :]).astype(F32).astype(BF) for c in range(cap)]
    hits = jnp.concatenate(hits, axis=1)
    for copy in copies[1:]:
        copy.wait()
    got = dot(hits, table[...], ((0,), (0,)))
    for c in range(cap):
        rows[:, c, :] = got[block(c), :cols]
        rows[:, cap + c, :] = got[block(c), cols:]
    out[...] = rows[...].astype(BF)


def select_rows(types, weights, out):
    rows, width, _ = out.shape
    experts = weights.shape[1]
    span = TILE // rows
    shape = (rows * span, span * experts)
    at, source = iota(shape, 0), iota(shape, 1)
    kind = jnp.zeros(shape, jnp.int32)
    for j in range(rows):
        kind = jnp.where(at // span == j, types[j], kind)
    hit = (source == (at % span) * experts + kind).astype(F32).astype(BF)
    for i in range(width // span):
        part = weights[i * span : (i + 1) * span].reshape(span * experts, -1)
        got = dot(hit, part).astype(BF)
        for j in range(rows):
            out[j, i * span : (i + 1) * span, :] = got[j * span : (j + 1) * span]


def choose_body(types, w_one_far, w_two_far, one, two, w_one, w_two, sems):
    copies = fetch((w_one_far, w_two_far), (w_one, w_two), sems)
    copies[0].wait()
    select_rows(types, w_one, one)
    copies[1].wait()
    select_rows(types, w_two, two)


def ready_body(pick, local, halo_val, feats, base, wide):
    cap = wide.shape[2] // 2 // 32
    shape = (TILE, 2 * TILE)
    k, m = iota(shape, 0), iota(shape, 1)
    spot = (k // cap) * (2 * cap) + k % cap
    first = (m == spot).astype(F32).astype(BF)
    second = (m == spot + cap).astype(F32).astype(BF)
    for j in range(wide.shape[0]):
        base[block(j), :] = dot(local[block(j), :], feats[block(j), :])
        wide[pick[j], :TILE, :] = dot(halo_val[block(j), :], first).astype(BF)
        wide[pick[j], TILE:, :] = dot(halo_val[block(j), :], second).astype(BF)


def gather_body(pick, landed, wide, base, copies, part):
    rows = range(wide.shape[0])
    both = [dot(wide[pick[j]], landed[pick[j]]) for j in rows]
    for j in rows:
        agg = (base[block(j), :] + both[j][:TILE]).astype(BF)
        part[block(j), :] = both[j][TILE:]
        for q in range(copies.shape[0]):
            copies[q, block(j), :] = agg


def products(agg, weights):
    out = []
    for j in range(weights.shape[0]):
        rows = jnp.concatenate([agg[q, block(j), :] for q in range(agg.shape[0])], axis=1)
        out.append(dot(rows, weights[j]))
    return out


def activate(z):
    sig = jax.nn.sigmoid(z)
    return z * sig, sig * (1.0 + z * (1.0 - sig))


def one_body(agg, weights, feats, local, part, near, slope, copies):
    hs = []
    for j, z in enumerate(products(agg, weights)):
        act, bend = activate(z)
        slope[block(j), :] = bend
        hs.append((feats[block(j), :].astype(F32) + act).astype(BF))
        near[block(j), :] = hs[j]
    mixed = [dot(local[block(j), :], h) for j, h in enumerate(hs)]
    for j, term in enumerate(mixed):
        term = (term + part[block(j), :]).astype(BF)
        for q in range(copies.shape[0]):
            copies[q, block(j), :] = term


def two_body(agg, weights, h_one, grad, hidden, dz, back):
    cols = dz.shape[1]
    ds = []
    for j, z in enumerate(products(agg, weights)):
        act, bend = activate(z)
        hidden[block(j), :] = (h_one[block(j), :].astype(F32) + act).astype(BF)
        ds.append((grad[block(j), :].astype(F32) * bend).astype(BF))
        dz[block(j), :] = ds[j]
    for j, d in enumerate(ds):
        term = dot(d, weights[j], ((1,), (1,))).astype(BF)
        for q in range(back.shape[0]):
            back[q, block(j), :] = term[:, q * cols : (q + 1) * cols]


def write_grad(types, core, agg, dz, keep, send, dims):
    reps = agg.shape[0]
    cols = dz.shape[1]
    rows = types.shape[0]
    zero = jnp.zeros((TILE, cols), BF)
    experts = keep.shape[1] // cols
    wide = []
    for e in range(experts):
        part = []
        for j in range(rows):
            part.append(lax.select(types[j] == e, dz[block(j), :], zero))
        wide.append(jnp.concatenate(part, axis=0))
    wide = jnp.concatenate(wide, axis=1)
    sides = (1 - core[0], core[0])
    order = [agg[side * (reps // 2) + i] for side in sides for i in range(reps // 2)]
    got = dot(jnp.concatenate(order, axis=1 - dims[0][0]), wide, dims)
    middle = send.shape[0]
    send[...] = got[:middle].astype(send.dtype)
    keep[...] = got[middle:]


def two_grad_body(types, core, agg, dz, near_one, near_two, keep, send, h_one, h_two):
    h_one[...] = near_one[...]
    h_two[...] = near_two[...]
    write_grad(types, core, agg, dz, keep, send, ((0,), (0,)))


def turn_body(agg, turned):
    for q in range(agg.shape[0]):
        turned[q] = jnp.transpose(agg[q])


def back_body(types, core, parts, local, grad, slope, agg, keep, send, dz):
    rows = range(types.shape[0])
    totals = []
    for j in rows:
        total = parts[0, block(j), :].astype(F32)
        for q in range(1, parts.shape[0]):
            total = total + parts[q, block(j), :].astype(F32)
        totals.append(total.astype(BF))
    terms = [dot(local[block(j), :], totals[j], ((0,), (0,))) for j in rows]
    for j in rows:
        dh = grad[block(j), :].astype(F32) + terms[j]
        dz[block(j), :] = (dh * slope[block(j), :]).astype(BF)
    write_grad(types, core, agg, dz, keep, send, ((1,), (0,)))


def add_up(parts):
    total = parts[0].astype(F32)
    for i in range(1, parts.shape[0]):
        total = total + parts[i].astype(F32)
    return total


def first_body(parts, copies):
    total = add_up(parts).astype(BF)
    for i in range(copies.shape[0]):
        copies[i] = total


def second_body(parts, copies, table):
    rows, experts, cols = table.shape
    total = add_up(parts)
    for e in range(experts):
        table[:, e, :] = total[:, e * cols : (e + 1) * cols]
    laid = table[...].reshape(rows * experts, cols).astype(BF)
    for i in range(copies.shape[0]):
        copies[i] = laid


def widen_body(core, half, *refs):
    one, two = refs[-2:]
    step = pl.program_id(0)
    length = half.shape[1] // 2
    count = one.shape[0] // length
    for i in range(count):
        rows = half[step * count + i].astype(F32)
        one[i * length : (i + 1) * length, :] = rows[:length]
        two[i * length : (i + 1) * length, :] = rows[length:]


def widen(core, half, before=()):
    chunks, length, cols = half.shape
    steps = 2
    own = not before
    height = chunks // steps * (length // 2)
    target = pl.BlockSpec(
        (height, cols), lambda i, c: ((c[0] if own else 1 - c[0]) * steps + i, 0)
    )
    shape = jax.ShapeDtypeStruct((chunks * length, cols), F32)
    return pl.pallas_call(
        widen_body,
        grid_spec=pltpu.PrefetchScalarGridSpec(
            num_scalar_prefetch=1,
            grid=(steps,),
            in_specs=[VMEM] + [ANY] * len(before),
            out_specs=(target, target),
        ),
        out_shape=(shape, shape),
        input_output_aliases={} if own else {2: 0, 3: 1},
        compiler_params=PARAMS,
        name="widen_own" if own else "widen_other",
    )(core, half, *before)


def rings():
    def device(core, line, cross):
        y, z = (line, cross) if core == 0 else (cross, line)
        return (y * 8 + z) * 2 + core

    first = [
        [device(core, line, pair * PAIR + i) for i in range(PAIR) for line in range(8)]
        for core in range(2)
        for pair in range(8 // PAIR)
    ]
    second = [
        [device(core, line, pair * PAIR + i) for pair in range(8 // PAIR)]
        for core in range(2)
        for line in range(8)
        for i in range(PAIR)
    ]
    return first, second


def exchange(blocks, groups):
    return lax.all_to_all(
        blocks, "dom", split_axis=0, concat_axis=0, axis_index_groups=groups, tiled=True
    )


def across(blocks):
    return lax.all_to_all(blocks, "rep", split_axis=0, concat_axis=0, tiled=True)


def swap(rows):
    return lax.ppermute(rows, "dom", [(p, p ^ 1) for p in range(128)])


def shards(
    feats, hist_one, local_val, halo_val, halo_send, halo_tile, tile_type, w_one, w_two, grad_out
):
    nodes, cols = feats.shape
    rows = nodes // TILE
    width, experts, _ = w_one.shape
    parts, cap = halo_send.shape[1], halo_send.shape[2]
    pick, types = halo_tile[0], tile_type[0]
    core = lax.rem(lax.axis_index("dom"), 2).astype(jnp.int32).reshape(1)
    first, second = rings()
    flat = (nodes, cols)
    copied = (REPS, nodes, cols)

    (rows_out,) = call(
        pick_body,
        "pick",
        [FAR] * 3,
        [((parts, 2 * cap, cols), BF)],
        [
            pltpu.VMEM((parts, 2 * cap, cols), F32),
            pltpu.VMEM((cap, parts), jnp.int32),
            pltpu.VMEM((nodes, 2 * cols), BF),
            pltpu.SemaphoreType.DMA((3,)),
        ],
        FULL,
    )(jnp.swapaxes(halo_send[0], 0, 1), feats, hist_one)
    landed = lax.all_to_all(rows_out, "dom", split_axis=0, concat_axis=0, tiled=True)
    landed = landed.reshape(rows, 2 * TILE, cols)

    chosen = (rows, width, cols)
    pick_one, pick_two = call(
        choose_body,
        "choose",
        [SMEM] + [FAR] * 2,
        [(chosen, BF)] * 2,
        [pltpu.VMEM(w_one.shape, BF)] * 2 + [pltpu.SemaphoreType.DMA((2,))],
        FULL,
    )(types, w_one, w_two)
    base, wide = call(
        ready_body,
        "ready",
        [SMEM] + [VMEM] * 3,
        [(flat, F32), ((rows, 2 * TILE, 2 * TILE), BF)],
    )(pick, local_val, halo_val, feats)

    base, wide, pick_one, pick_two = lax.optimization_barrier((base, wide, pick_one, pick_two))
    copies, part = call(gather_body, "gather", [SMEM] + [VMEM] * 3, [(copied, BF), (flat, F32)])(
        pick, landed, wide, base
    )
    agg_one = across(copies)
    near_one, slope, copies = call(
        one_body, "one", [VMEM] * 5, [(flat, BF), (flat, F32), (copied, BF)]
    )(agg_one, pick_one, feats, local_val, part)
    agg_two = across(copies)
    near_two, dz_two, back = call(
        two_body, "two", [VMEM] * 4, [(flat, BF), (flat, BF), (copied, BF)]
    )(agg_two, pick_two, near_one, grad_out)
    back = across(back)

    half = (width // 2, experts * cols)
    keep_two, send_two, h_one, h_two = call(
        two_grad_body,
        "grad_two",
        [SMEM] * 2 + [VMEM] * 4,
        [(half, F32), (half, BF), (flat, BF), (flat, BF)],
    )(types, core, agg_two, dz_two, near_one, near_two)
    agg_one, keep_two = lax.optimization_barrier((agg_one, keep_two))
    (turned,) = call(turn_body, "turn", [VMEM], [((REPS, cols, nodes), BF)])(agg_one)
    keep_one, send_one = call(
        back_body,
        "back",
        [SMEM] * 2 + [VMEM] * 5,
        [(half, F32), (half, BF)],
        [pltpu.VMEM(flat, BF)],
    )(types, core, back, local_val, grad_out, slope, turned)
    pair_one = (keep_one + swap(send_one).astype(F32)).astype(BF)
    pair_two = (keep_two + swap(send_two).astype(F32)).astype(BF)

    split = (RING, width // 2 // RING, experts * cols)
    both = jnp.concatenate([pair_one.reshape(split), pair_two.reshape(split)], axis=1)
    both = exchange(both, first)
    few = both.shape[1]
    (both,) = call(first_body, "first_sum", [VMEM], [((CROSS,) + both.shape[1:], BF)])(both)
    both = exchange(both, second)
    (both,) = call(
        second_body,
        "second_sum",
        [VMEM],
        [((RING, few * experts, cols), BF)],
        [pltpu.VMEM((few, experts, cols), F32)],
    )(both)
    same = exchange(both, first)
    grad_one, grad_two = widen(core, swap(same), widen(core, same))
    return h_two, h_one, grad_one.reshape(w_one.shape), grad_two.reshape(w_two.shape)


def solution(mesh):
    in_specs = (
        P("dom", "rep"),
        P("dom", "rep"),
        P("dom", None),
        P("dom", None),
        P("dom", None, None),
        P("dom", None),
        P("dom", None),
        P(None, None, "rep"),
        P(None, None, "rep"),
        P("dom", "rep"),
    )
    out_specs = (P("dom", "rep"), P("dom", "rep"), P(None, None, "rep"), P(None, None, "rep"))
    return jax.shard_map(shards, mesh=mesh, in_specs=in_specs, out_specs=out_specs, check_vma=False)
```

```python
import jax
import jax.numpy as jnp
from jax import lax
from jax.experimental import pallas as pl
from jax.experimental.pallas import tpu as pltpu
from jax.sharding import PartitionSpec as P

BF = jnp.bfloat16
F32 = jnp.float32
SMEM = pl.BlockSpec(memory_space=pltpu.SMEM)
VMEM = pl.BlockSpec(memory_space=pltpu.VMEM)
ANY = pl.BlockSpec(memory_space=pl.ANY)
FAR = pl.BlockSpec(memory_space=pltpu.HBM)
PARAMS = pltpu.CompilerParams(vmem_limit_bytes=40 << 20)
FULL = pltpu.CompilerParams(vmem_limit_bytes=60 << 20)
PAIR = 2
RING = 16
CROSS = 4
REPS = 4
TILE = 128


def call(body, name, ins, outs, scratch=(), params=PARAMS):
    return pl.pallas_call(
        body,
        out_shape=tuple(jax.ShapeDtypeStruct(shape, kind) for shape, kind in outs),
        in_specs=list(ins),
        out_specs=tuple(VMEM for _ in outs),
        scratch_shapes=list(scratch),
        compiler_params=params,
        name=name,
    )


def dot(a, b, dims=((1,), (0,))):
    return lax.dot_general(a, b, (dims, ((), ())), preferred_element_type=F32)


def block(j):
    return slice(j * TILE, (j + 1) * TILE)


def iota(shape, axis):
    return lax.broadcasted_iota(jnp.int32, shape, axis)


def fetch(sources, targets, sems):
    copies = [
        pltpu.make_async_copy(source, target, sems.at[i])
        for i, (source, target) in enumerate(zip(sources, targets))
    ]
    for copy in copies:
        copy.start()
    return copies


def pick_body(send_far, feats_far, hist_far, out, rows, send, table, sems):
    cap, parts = send.shape
    nodes, cols = feats_far.shape
    targets = (send, table.at[:, :cols], table.at[:, cols:])
    copies = fetch((send_far, feats_far, hist_far), targets, sems)
    copies[0].wait()
    spot = iota((nodes, parts), 0)
    hits = [(spot == send[c : c + 1, :]).astype(F32).astype(BF) for c in range(cap)]
    hits = jnp.concatenate(hits, axis=1)
    for copy in copies[1:]:
        copy.wait()
    got = dot(hits, table[...], ((0,), (0,)))
    for c in range(cap):
        rows[:, c, :] = got[block(c), :cols]
        rows[:, cap + c, :] = got[block(c), cols:]
    out[...] = rows[...].astype(BF)


def select_rows(types, weights, out):
    rows, width, _ = out.shape
    experts = weights.shape[1]
    span = TILE // rows
    shape = (rows * span, span * experts)
    at, source = iota(shape, 0), iota(shape, 1)
    kind = jnp.zeros(shape, jnp.int32)
    for j in range(rows):
        kind = jnp.where(at // span == j, types[j], kind)
    hit = (source == (at % span) * experts + kind).astype(F32).astype(BF)
    for i in range(width // span):
        part = weights[i * span : (i + 1) * span].reshape(span * experts, -1)
        got = dot(hit, part).astype(BF)
        for j in range(rows):
            out[j, i * span : (i + 1) * span, :] = got[j * span : (j + 1) * span]


def choose_body(types, w_one_far, w_two_far, one, two, w_one, w_two, sems):
    copies = fetch((w_one_far, w_two_far), (w_one, w_two), sems)
    copies[0].wait()
    select_rows(types, w_one, one)
    copies[1].wait()
    select_rows(types, w_two, two)


def ready_body(pick, local, halo_val, feats, base, wide):
    cap = wide.shape[2] // 2 // 32
    shape = (TILE, 2 * TILE)
    k, m = iota(shape, 0), iota(shape, 1)
    spot = (k // cap) * (2 * cap) + k % cap
    first = (m == spot).astype(F32).astype(BF)
    second = (m == spot + cap).astype(F32).astype(BF)
    for j in range(wide.shape[0]):
        base[block(j), :] = dot(local[block(j), :], feats[block(j), :])
        wide[pick[j], :TILE, :] = dot(halo_val[block(j), :], first).astype(BF)
        wide[pick[j], TILE:, :] = dot(halo_val[block(j), :], second).astype(BF)


def gather_body(pick, landed, wide, base, copies, part):
    rows = range(wide.shape[0])
    both = [dot(wide[pick[j]], landed[pick[j]]) for j in rows]
    for j in rows:
        agg = (base[block(j), :] + both[j][:TILE]).astype(BF)
        part[block(j), :] = both[j][TILE:]
        for q in range(copies.shape[0]):
            copies[q, block(j), :] = agg


def products(agg, weights):
    out = []
    for j in range(weights.shape[0]):
        rows = jnp.concatenate([agg[q, block(j), :] for q in range(agg.shape[0])], axis=1)
        out.append(dot(rows, weights[j]))
    return out


def activate(z):
    sig = jax.nn.sigmoid(z)
    return z * sig, sig * (1.0 + z * (1.0 - sig))


def one_body(agg, weights, feats, local, part, near, slope, copies):
    hs = []
    for j, z in enumerate(products(agg, weights)):
        act, bend = activate(z)
        slope[block(j), :] = bend
        hs.append((feats[block(j), :].astype(F32) + act).astype(BF))
        near[block(j), :] = hs[j]
    mixed = [dot(local[block(j), :], h) for j, h in enumerate(hs)]
    for j, term in enumerate(mixed):
        term = (term + part[block(j), :]).astype(BF)
        for q in range(copies.shape[0]):
            copies[q, block(j), :] = term


def two_body(agg, weights, h_one, grad, hidden, dz, back):
    cols = dz.shape[1]
    ds = []
    for j, z in enumerate(products(agg, weights)):
        act, bend = activate(z)
        hidden[block(j), :] = (h_one[block(j), :].astype(F32) + act).astype(BF)
        ds.append((grad[block(j), :].astype(F32) * bend).astype(BF))
        dz[block(j), :] = ds[j]
    for j, d in enumerate(ds):
        term = dot(d, weights[j], ((1,), (1,))).astype(BF)
        for q in range(back.shape[0]):
            back[q, block(j), :] = term[:, q * cols : (q + 1) * cols]


def write_grad(types, core, agg, dz, keep, send):
    reps, _, cols = agg.shape
    rows = types.shape[0]
    experts = keep.shape[1] // cols
    wide = []
    for e in range(experts):
        part = []
        for j in range(rows):
            part.append((dz[block(j), :].astype(F32) * (types[j] == e).astype(F32)).astype(BF))
        wide.append(jnp.concatenate(part, axis=0))
    wide = jnp.concatenate(wide, axis=1)
    for target, side in ((send, 1 - core[0]), (keep, core[0])):
        for i in range(reps // 2):
            got = dot(agg[side * (reps // 2) + i], wide, ((0,), (0,)))
            target[i * cols : (i + 1) * cols, :] = got.astype(target.dtype)


def two_grad_body(types, core, agg, dz, near_one, near_two, keep, send, h_one, h_two):
    h_one[...] = near_one[...]
    h_two[...] = near_two[...]
    write_grad(types, core, agg, dz, keep, send)


def back_body(types, core, parts, local, grad, slope, agg, keep, send, dz):
    rows = range(types.shape[0])
    totals = []
    for j in rows:
        total = parts[0, block(j), :].astype(F32)
        for q in range(1, parts.shape[0]):
            total = total + parts[q, block(j), :].astype(F32)
        totals.append(total.astype(BF))
    terms = [dot(local[block(j), :], totals[j], ((0,), (0,))) for j in rows]
    for j in rows:
        dh = grad[block(j), :].astype(F32) + terms[j]
        dz[block(j), :] = (dh * slope[block(j), :]).astype(BF)
    write_grad(types, core, agg, dz, keep, send)


def add_up(parts):
    total = parts[0].astype(F32)
    for i in range(1, parts.shape[0]):
        total = total + parts[i].astype(F32)
    return total


def first_body(parts, copies):
    total = add_up(parts).astype(BF)
    for i in range(copies.shape[0]):
        copies[i] = total


def second_body(parts, copies, table):
    rows, experts, cols = table.shape
    total = add_up(parts)
    for e in range(experts):
        table[:, e, :] = total[:, e * cols : (e + 1) * cols]
    laid = table[...].reshape(rows * experts, cols).astype(BF)
    for i in range(copies.shape[0]):
        copies[i] = laid


def widen_body(core, half, *refs):
    one, two = refs[-2:]
    step = pl.program_id(0)
    length = half.shape[1] // 2
    count = one.shape[0] // length
    for i in range(count):
        rows = half[step * count + i].astype(F32)
        one[i * length : (i + 1) * length, :] = rows[:length]
        two[i * length : (i + 1) * length, :] = rows[length:]


def widen(core, half, before=()):
    chunks, length, cols = half.shape
    steps = 2
    own = not before
    height = chunks // steps * (length // 2)
    target = pl.BlockSpec(
        (height, cols), lambda i, c: ((c[0] if own else 1 - c[0]) * steps + i, 0)
    )
    shape = jax.ShapeDtypeStruct((chunks * length, cols), F32)
    return pl.pallas_call(
        widen_body,
        grid_spec=pltpu.PrefetchScalarGridSpec(
            num_scalar_prefetch=1,
            grid=(steps,),
            in_specs=[VMEM] + [ANY] * len(before),
            out_specs=(target, target),
        ),
        out_shape=(shape, shape),
        input_output_aliases={} if own else {2: 0, 3: 1},
        compiler_params=PARAMS,
        name="widen_own" if own else "widen_other",
    )(core, half, *before)


def rings():
    def device(core, line, cross):
        y, z = (line, cross) if core == 0 else (cross, line)
        return (y * 8 + z) * 2 + core

    first = [
        [device(core, line, pair * PAIR + i) for line in range(8) for i in range(PAIR)]
        for core in range(2)
        for pair in range(8 // PAIR)
    ]
    second = [
        [device(core, line, pair * PAIR + i) for pair in range(8 // PAIR)]
        for core in range(2)
        for line in range(8)
        for i in range(PAIR)
    ]
    return first, second


def exchange(blocks, groups):
    return lax.all_to_all(
        blocks, "dom", split_axis=0, concat_axis=0, axis_index_groups=groups, tiled=True
    )


def across(blocks):
    return lax.all_to_all(blocks, "rep", split_axis=0, concat_axis=0, tiled=True)


def swap(rows):
    return lax.ppermute(rows, "dom", [(p, p ^ 1) for p in range(128)])


def shards(
    feats, hist_one, local_val, halo_val, halo_send, halo_tile, tile_type, w_one, w_two, grad_out
):
    nodes, cols = feats.shape
    rows = nodes // TILE
    width, experts, _ = w_one.shape
    parts, cap = halo_send.shape[1], halo_send.shape[2]
    pick, types = halo_tile[0], tile_type[0]
    core = lax.rem(lax.axis_index("dom"), 2).astype(jnp.int32).reshape(1)
    first, second = rings()
    flat = (nodes, cols)
    copied = (REPS, nodes, cols)

    (rows_out,) = call(
        pick_body,
        "pick",
        [FAR] * 3,
        [((parts, 2 * cap, cols), BF)],
        [
            pltpu.VMEM((parts, 2 * cap, cols), F32),
            pltpu.VMEM((cap, parts), jnp.int32),
            pltpu.VMEM((nodes, 2 * cols), BF),
            pltpu.SemaphoreType.DMA((3,)),
        ],
        FULL,
    )(jnp.swapaxes(halo_send[0], 0, 1), feats, hist_one)
    landed = lax.all_to_all(rows_out, "dom", split_axis=0, concat_axis=0, tiled=True)
    landed = landed.reshape(rows, 2 * TILE, cols)

    chosen = (rows, width, cols)
    pick_one, pick_two = call(
        choose_body,
        "choose",
        [SMEM] + [FAR] * 2,
        [(chosen, BF)] * 2,
        [pltpu.VMEM(w_one.shape, BF)] * 2 + [pltpu.SemaphoreType.DMA((2,))],
        FULL,
    )(types, w_one, w_two)
    base, wide = call(
        ready_body,
        "ready",
        [SMEM] + [VMEM] * 3,
        [(flat, F32), ((rows, 2 * TILE, 2 * TILE), BF)],
    )(pick, local_val, halo_val, feats)

    base, wide, pick_one, pick_two = lax.optimization_barrier((base, wide, pick_one, pick_two))
    copies, part = call(gather_body, "gather", [SMEM] + [VMEM] * 3, [(copied, BF), (flat, F32)])(
        pick, landed, wide, base
    )
    agg_one = across(copies)
    near_one, slope, copies = call(
        one_body, "one", [VMEM] * 5, [(flat, BF), (flat, F32), (copied, BF)]
    )(agg_one, pick_one, feats, local_val, part)
    agg_two = across(copies)
    near_two, dz_two, back = call(
        two_body, "two", [VMEM] * 4, [(flat, BF), (flat, BF), (copied, BF)]
    )(agg_two, pick_two, near_one, grad_out)
    back = across(back)

    half = (width // 2, experts * cols)
    keep_two, send_two, h_one, h_two = call(
        two_grad_body,
        "grad_two",
        [SMEM] * 2 + [VMEM] * 4,
        [(half, F32), (half, BF), (flat, BF), (flat, BF)],
    )(types, core, agg_two, dz_two, near_one, near_two)
    keep_one, send_one = call(
        back_body,
        "back",
        [SMEM] * 2 + [VMEM] * 5,
        [(half, F32), (half, BF)],
        [pltpu.VMEM(flat, BF)],
    )(types, core, back, local_val, grad_out, slope, agg_one)
    pair_one = (keep_one + swap(send_one).astype(F32)).astype(BF)
    pair_two = (keep_two + swap(send_two).astype(F32)).astype(BF)

    split = (RING, width // 2 // RING, experts * cols)
    both = jnp.concatenate([pair_one.reshape(split), pair_two.reshape(split)], axis=1)
    both = exchange(both, first)
    few = both.shape[1]
    (both,) = call(first_body, "first_sum", [VMEM], [((CROSS,) + both.shape[1:], BF)])(both)
    both = exchange(both, second)
    (both,) = call(
        second_body,
        "second_sum",
        [VMEM],
        [((RING, few * experts, cols), BF)],
        [pltpu.VMEM((few, experts, cols), F32)],
    )(both)
    same = exchange(both, first)
    grad_one, grad_two = widen(core, swap(same), widen(core, same))
    return h_two, h_one, grad_one.reshape(w_one.shape), grad_two.reshape(w_two.shape)


def solution(mesh):
    in_specs = (
        P("dom", "rep"),
        P("dom", "rep"),
        P("dom", None),
        P("dom", None),
        P("dom", None, None),
        P("dom", None),
        P("dom", None),
        P(None, None, "rep"),
        P(None, None, "rep"),
        P("dom", "rep"),
    )
    out_specs = (P("dom", "rep"), P("dom", "rep"), P(None, None, "rep"), P(None, None, "rep"))
    return jax.shard_map(shards, mesh=mesh, in_specs=in_specs, out_specs=out_specs, check_vma=False)
```

```python
import jax
import jax.numpy as jnp
from jax import lax
from jax.experimental import pallas as pl
from jax.experimental.pallas import tpu as pltpu
from jax.sharding import PartitionSpec as P

BF = jnp.bfloat16
F32 = jnp.float32
SMEM = pl.BlockSpec(memory_space=pltpu.SMEM)
VMEM = pl.BlockSpec(memory_space=pltpu.VMEM)
ANY = pl.BlockSpec(memory_space=pl.ANY)
FAR = pl.BlockSpec(memory_space=pltpu.HBM)
PARAMS = pltpu.CompilerParams(vmem_limit_bytes=40 << 20)
FULL = pltpu.CompilerParams(vmem_limit_bytes=60 << 20)
PAIR = 2
RING = 16
CROSS = 4
REPS = 4
TILE = 128


def call(body, name, ins, outs, scratch=(), params=PARAMS):
    return pl.pallas_call(
        body,
        out_shape=tuple(jax.ShapeDtypeStruct(shape, kind) for shape, kind in outs),
        in_specs=list(ins),
        out_specs=tuple(VMEM for _ in outs),
        scratch_shapes=list(scratch),
        compiler_params=params,
        name=name,
    )


def dot(a, b, dims=((1,), (0,))):
    return lax.dot_general(a, b, (dims, ((), ())), preferred_element_type=F32)


def block(j):
    return slice(j * TILE, (j + 1) * TILE)


def iota(shape, axis):
    return lax.broadcasted_iota(jnp.int32, shape, axis)


def fetch(sources, targets, sems):
    copies = [
        pltpu.make_async_copy(source, target, sems.at[i])
        for i, (source, target) in enumerate(zip(sources, targets))
    ]
    for copy in copies:
        copy.start()
    return copies


def pick_body(send_far, feats_far, hist_far, out, rows, send, table, sems):
    cap, parts = send.shape
    nodes, cols = feats_far.shape
    targets = (send, table.at[:, :cols], table.at[:, cols:])
    copies = fetch((send_far, feats_far, hist_far), targets, sems)
    copies[0].wait()
    spot = iota((nodes, parts), 0)
    hits = [(spot == send[c : c + 1, :]).astype(F32).astype(BF) for c in range(cap)]
    hits = jnp.concatenate(hits, axis=1)
    for copy in copies[1:]:
        copy.wait()
    got = dot(hits, table[...], ((0,), (0,)))
    for c in range(cap):
        rows[:, c, :] = got[block(c), :cols]
        rows[:, cap + c, :] = got[block(c), cols:]
    out[...] = rows[...].astype(BF)


def select_rows(types, weights, out):
    rows, width, _ = out.shape
    experts = weights.shape[1]
    span = TILE // rows
    shape = (rows * span, span * experts)
    at, source = iota(shape, 0), iota(shape, 1)
    kind = jnp.zeros(shape, jnp.int32)
    for j in range(rows):
        kind = jnp.where(at // span == j, types[j], kind)
    hit = (source == (at % span) * experts + kind).astype(F32).astype(BF)
    for i in range(width // span):
        part = weights[i * span : (i + 1) * span].reshape(span * experts, -1)
        got = dot(hit, part).astype(BF)
        for j in range(rows):
            out[j, i * span : (i + 1) * span, :] = got[j * span : (j + 1) * span]


def choose_body(types, w_one_far, w_two_far, one, two, w_one, w_two, sems):
    copies = fetch((w_one_far, w_two_far), (w_one, w_two), sems)
    copies[0].wait()
    select_rows(types, w_one, one)
    copies[1].wait()
    select_rows(types, w_two, two)


def ready_body(pick, local, halo_val, feats, base, wide):
    cap = wide.shape[2] // 2 // 32
    shape = (TILE, 2 * TILE)
    k, m = iota(shape, 0), iota(shape, 1)
    spot = (k // cap) * (2 * cap) + k % cap
    first = (m == spot).astype(F32).astype(BF)
    second = (m == spot + cap).astype(F32).astype(BF)
    for j in range(wide.shape[0]):
        base[block(j), :] = dot(local[block(j), :], feats[block(j), :])
        wide[pick[j], :TILE, :] = dot(halo_val[block(j), :], first).astype(BF)
        wide[pick[j], TILE:, :] = dot(halo_val[block(j), :], second).astype(BF)


def gather_body(pick, landed, wide, base, copies, part):
    rows = range(wide.shape[0])
    both = [dot(wide[pick[j]], landed[pick[j]]) for j in rows]
    for j in rows:
        agg = (base[block(j), :] + both[j][:TILE]).astype(BF)
        part[block(j), :] = both[j][TILE:]
        for q in range(copies.shape[0]):
            copies[q, block(j), :] = agg


def products(agg, weights):
    out = []
    for j in range(weights.shape[0]):
        rows = jnp.concatenate([agg[q, block(j), :] for q in range(agg.shape[0])], axis=1)
        out.append(dot(rows, weights[j]))
    return out


def activate(z):
    sig = jax.nn.sigmoid(z)
    return z * sig, sig * (1.0 + z * (1.0 - sig))


def one_body(agg, weights, feats, local, part, near, slope, copies):
    hs = []
    for j, z in enumerate(products(agg, weights)):
        act, bend = activate(z)
        slope[block(j), :] = bend
        hs.append((feats[block(j), :].astype(F32) + act).astype(BF))
        near[block(j), :] = hs[j]
    mixed = [dot(local[block(j), :], h) for j, h in enumerate(hs)]
    for j, term in enumerate(mixed):
        term = (term + part[block(j), :]).astype(BF)
        for q in range(copies.shape[0]):
            copies[q, block(j), :] = term


def two_body(agg, weights, h_one, grad, hidden, dz, back):
    cols = dz.shape[1]
    ds = []
    for j, z in enumerate(products(agg, weights)):
        act, bend = activate(z)
        hidden[block(j), :] = (h_one[block(j), :].astype(F32) + act).astype(BF)
        ds.append((grad[block(j), :].astype(F32) * bend).astype(BF))
        dz[block(j), :] = ds[j]
    for j, d in enumerate(ds):
        term = dot(d, weights[j], ((1,), (1,))).astype(BF)
        for q in range(back.shape[0]):
            back[q, block(j), :] = term[:, q * cols : (q + 1) * cols]


def write_grad(types, core, agg, dz, keep, send, dims):
    reps = agg.shape[0]
    cols = dz.shape[1]
    rows = types.shape[0]
    zero = jnp.zeros((TILE, cols), BF)
    experts = keep.shape[1] // cols
    wide = []
    for e in range(experts):
        part = []
        for j in range(rows):
            part.append(lax.select(types[j] == e, dz[block(j), :], zero))
        wide.append(jnp.concatenate(part, axis=0))
    wide = jnp.concatenate(wide, axis=1)
    for target, side in ((send, 1 - core[0]), (keep, core[0])):
        for i in range(reps // 2):
            got = dot(agg[side * (reps // 2) + i], wide, dims)
            target[i * cols : (i + 1) * cols, :] = got.astype(target.dtype)


def two_grad_body(types, core, agg, dz, near_one, near_two, keep, send, h_one, h_two):
    h_one[...] = near_one[...]
    h_two[...] = near_two[...]
    write_grad(types, core, agg, dz, keep, send, ((0,), (0,)))


def back_body(types, core, parts, local, grad, slope, agg, keep, send, dz):
    rows = range(types.shape[0])
    totals = []
    for j in rows:
        total = parts[0, block(j), :].astype(F32)
        for q in range(1, parts.shape[0]):
            total = total + parts[q, block(j), :].astype(F32)
        totals.append(total.astype(BF))
    terms = [dot(local[block(j), :], totals[j], ((0,), (0,))) for j in rows]
    for j in rows:
        dh = grad[block(j), :].astype(F32) + terms[j]
        dz[block(j), :] = (dh * slope[block(j), :]).astype(BF)
    write_grad(types, core, agg, dz, keep, send, ((0,), (0,)))


def add_up(parts):
    total = parts[0].astype(F32)
    for i in range(1, parts.shape[0]):
        total = total + parts[i].astype(F32)
    return total


def first_body(parts, copies):
    total = add_up(parts).astype(BF)
    for i in range(copies.shape[0]):
        copies[i] = total


def second_body(parts, copies, table):
    rows, experts, cols = table.shape
    total = add_up(parts)
    for e in range(experts):
        table[:, e, :] = total[:, e * cols : (e + 1) * cols]
    laid = table[...].reshape(rows * experts, cols).astype(BF)
    for i in range(copies.shape[0]):
        copies[i] = laid


def widen_body(core, half, *refs):
    one, two = refs[-2:]
    step = pl.program_id(0)
    length = half.shape[1] // 2
    count = one.shape[0] // length
    for i in range(count):
        rows = half[step * count + i].astype(F32)
        one[i * length : (i + 1) * length, :] = rows[:length]
        two[i * length : (i + 1) * length, :] = rows[length:]


def widen(core, half, before=()):
    chunks, length, cols = half.shape
    steps = 2
    own = not before
    height = chunks // steps * (length // 2)
    target = pl.BlockSpec(
        (height, cols), lambda i, c: ((c[0] if own else 1 - c[0]) * steps + i, 0)
    )
    shape = jax.ShapeDtypeStruct((chunks * length, cols), F32)
    return pl.pallas_call(
        widen_body,
        grid_spec=pltpu.PrefetchScalarGridSpec(
            num_scalar_prefetch=1,
            grid=(steps,),
            in_specs=[VMEM] + [ANY] * len(before),
            out_specs=(target, target),
        ),
        out_shape=(shape, shape),
        input_output_aliases={} if own else {2: 0, 3: 1},
        compiler_params=PARAMS,
        name="widen_own" if own else "widen_other",
    )(core, half, *before)


def rings():
    def device(core, line, cross):
        y, z = (line, cross) if core == 0 else (cross, line)
        return (y * 8 + z) * 2 + core

    first = [
        [device(core, line, pair * PAIR + i) for i in range(PAIR) for line in range(8)]
        for core in range(2)
        for pair in range(8 // PAIR)
    ]
    second = [
        [device(core, line, pair * PAIR + i) for pair in range(8 // PAIR)]
        for core in range(2)
        for line in range(8)
        for i in range(PAIR)
    ]
    return first, second


def exchange(blocks, groups):
    return lax.all_to_all(
        blocks, "dom", split_axis=0, concat_axis=0, axis_index_groups=groups, tiled=True
    )


def across(blocks):
    return lax.all_to_all(blocks, "rep", split_axis=0, concat_axis=0, tiled=True)


def swap(rows):
    return lax.ppermute(rows, "dom", [(p, p ^ 1) for p in range(128)])


def shards(
    feats, hist_one, local_val, halo_val, halo_send, halo_tile, tile_type, w_one, w_two, grad_out
):
    nodes, cols = feats.shape
    rows = nodes // TILE
    width, experts, _ = w_one.shape
    parts, cap = halo_send.shape[1], halo_send.shape[2]
    pick, types = halo_tile[0], tile_type[0]
    core = lax.rem(lax.axis_index("dom"), 2).astype(jnp.int32).reshape(1)
    first, second = rings()
    flat = (nodes, cols)
    copied = (REPS, nodes, cols)

    (rows_out,) = call(
        pick_body,
        "pick",
        [FAR] * 3,
        [((parts, 2 * cap, cols), BF)],
        [
            pltpu.VMEM((parts, 2 * cap, cols), F32),
            pltpu.VMEM((cap, parts), jnp.int32),
            pltpu.VMEM((nodes, 2 * cols), BF),
            pltpu.SemaphoreType.DMA((3,)),
        ],
        FULL,
    )(jnp.swapaxes(halo_send[0], 0, 1), feats, hist_one)
    landed = lax.all_to_all(rows_out, "dom", split_axis=0, concat_axis=0, tiled=True)
    landed = landed.reshape(rows, 2 * TILE, cols)

    chosen = (rows, width, cols)
    pick_one, pick_two = call(
        choose_body,
        "choose",
        [SMEM] + [FAR] * 2,
        [(chosen, BF)] * 2,
        [pltpu.VMEM(w_one.shape, BF)] * 2 + [pltpu.SemaphoreType.DMA((2,))],
        FULL,
    )(types, w_one, w_two)
    base, wide = call(
        ready_body,
        "ready",
        [SMEM] + [VMEM] * 3,
        [(flat, F32), ((rows, 2 * TILE, 2 * TILE), BF)],
    )(pick, local_val, halo_val, feats)

    base, wide, pick_one, pick_two = lax.optimization_barrier((base, wide, pick_one, pick_two))
    copies, part = call(gather_body, "gather", [SMEM] + [VMEM] * 3, [(copied, BF), (flat, F32)])(
        pick, landed, wide, base
    )
    agg_one = across(copies)
    near_one, slope, copies = call(
        one_body, "one", [VMEM] * 5, [(flat, BF), (flat, F32), (copied, BF)]
    )(agg_one, pick_one, feats, local_val, part)
    agg_two = across(copies)
    near_two, dz_two, back = call(
        two_body, "two", [VMEM] * 4, [(flat, BF), (flat, BF), (copied, BF)]
    )(agg_two, pick_two, near_one, grad_out)
    back = across(back)

    half = (width // 2, experts * cols)
    keep_two, send_two, h_one, h_two = call(
        two_grad_body,
        "grad_two",
        [SMEM] * 2 + [VMEM] * 4,
        [(half, F32), (half, BF), (flat, BF), (flat, BF)],
    )(types, core, agg_two, dz_two, near_one, near_two)
    keep_one, send_one = call(
        back_body,
        "back",
        [SMEM] * 2 + [VMEM] * 5,
        [(half, F32), (half, BF)],
        [pltpu.VMEM(flat, BF)],
    )(types, core, back, local_val, grad_out, slope, agg_one)
    pair_one = (keep_one + swap(send_one).astype(F32)).astype(BF)
    pair_two = (keep_two + swap(send_two).astype(F32)).astype(BF)

    split = (RING, width // 2 // RING, experts * cols)
    both = jnp.concatenate([pair_one.reshape(split), pair_two.reshape(split)], axis=1)
    both = exchange(both, first)
    few = both.shape[1]
    (both,) = call(first_body, "first_sum", [VMEM], [((CROSS,) + both.shape[1:], BF)])(both)
    both = exchange(both, second)
    (both,) = call(
        second_body,
        "second_sum",
        [VMEM],
        [((RING, few * experts, cols), BF)],
        [pltpu.VMEM((few, experts, cols), F32)],
    )(both)
    same = exchange(both, first)
    grad_one, grad_two = widen(core, swap(same), widen(core, same))
    return h_two, h_one, grad_one.reshape(w_one.shape), grad_two.reshape(w_two.shape)


def solution(mesh):
    in_specs = (
        P("dom", "rep"),
        P("dom", "rep"),
        P("dom", None),
        P("dom", None),
        P("dom", None, None),
        P("dom", None),
        P("dom", None),
        P(None, None, "rep"),
        P(None, None, "rep"),
        P("dom", "rep"),
    )
    out_specs = (P("dom", "rep"), P("dom", "rep"), P(None, None, "rep"), P(None, None, "rep"))
    return jax.shard_map(shards, mesh=mesh, in_specs=in_specs, out_specs=out_specs, check_vma=False)
```
